32 devices in a mesh: dp: 16 (over z, y, x), tensor: 2 (over core).
Axes of the slice: x: 2, y: 2, z: 4, core: 2. Of those that a mesh axis runs over, the one named last changes fastest.
Arguments:
- tokens: bfloat16 [24576, 768], P(('dp', 'tensor')), may hold values from -6 to 6
- kept_patches: int32 [24576], P(('dp', 'tensor')), may hold values from 0 to 1567, as said below
- clip_lengths: int32 [128], replicated, may hold values from 39 to 314, as said below
- clip_device: int32 [128], replicated, may hold values from 0 to 31, as said below
- cot_output: bfloat16 [24576, 768], P(('dp', 'tensor')), may hold values from -6 to 6
- cot_aligned: bfloat16 [24576, 1024], P(('dp', 'tensor')), may hold values from -6 to 6
- entry_weight: float32 [1769472], P(('dp', 'tensor')), may hold values from -0.21875 to 0.21875
- entry_first: float32 [1769472], P(('dp', 'tensor')), may hold values from -112 to 112
- entry_second: float32 [1769472], P(('dp', 'tensor')), may hold values from 245.76 to 4096.8193
- exit_weight: float32 [589824], P(('dp', 'tensor')), may hold values from -1.75 to 1.75
- exit_first: float32 [589824], P(('dp', 'tensor')), may hold values from -24 to 24
- exit_second: float32 [589824], P(('dp', 'tensor')), may hold values from 12.288 to 204.71808
- align_weight: float32 [786432], P(('dp', 'tensor')), may hold values from -0.21875 to 0.21875
- align_first: float32 [786432], P(('dp', 'tensor')), may hold values from -128 to 128
- align_second: float32 [786432], P(('dp', 'tensor')), may hold values from 447.2832 to 8183.808
- expand_weight: float32 [3072, 768], P(('dp', 'tensor')), may hold values from -0.21875 to 0.21875
- expand_first: float32 [3072, 768], P(('dp', 'tensor')), may hold values from -32 to 32
- expand_second: float32 [3072, 768], P(('dp', 'tensor')), may hold values from 24.576 to 409.68192
- reduce_weight: float32 [3072, 768], P(('dp', 'tensor')), may hold values from -0.109375 to 0.109375
- reduce_first: float32 [3072, 768], P(('dp', 'tensor')), may hold values from -80 to 80
- reduce_second: float32 [3072, 768], P(('dp', 'tensor')), may hold values from 144.50688 to 2457.6
- position_table: float32 [1204224], P(('dp', 'tensor')), may hold values from -3 to 3
- position_first: float32 [1204224], P(('dp', 'tensor')), may hold values from -5 to 5
- position_second: float32 [1204224], P(('dp', 'tensor')), may hold values from 0.5219265 to 7.836735
- norm_params: float32 [3072], P(('dp', 'tensor')), may hold values from -1.5 to 1.5, as said below
- norm_first: float32 [3072], P(('dp', 'tensor')), may hold values from -128 to 128
- norm_second: float32 [3072], P(('dp', 'tensor')), may hold values from 447.2832 to 8183.808
Outputs:
- block_out: bfloat16 [24576, 768], P(('dp', 'tensor'))
- aligned: bfloat16 [24576, 1024], P(('dp', 'tensor'))
- token_grad: float32 [24576, 768], P(('dp', 'tensor'))
- new_entry_first: float32 [1769472], P(('dp', 'tensor'))
- new_entry_second: float32 [1769472], P(('dp', 'tensor'))
- new_entry_weight: float32 [1769472], P(('dp', 'tensor'))
- new_exit_first: float32 [589824], P(('dp', 'tensor'))
- new_exit_second: float32 [589824], P(('dp', 'tensor'))
- new_exit_weight: float32 [589824], P(('dp', 'tensor'))
- new_align_first: float32 [786432], P(('dp', 'tensor'))
- new_align_second: float32 [786432], P(('dp', 'tensor'))
- new_align_weight: float32 [786432], P(('dp', 'tensor'))
- new_expand_first: float32 [3072, 768], P(('dp', 'tensor'))
- new_expand_second: float32 [3072, 768], P(('dp', 'tensor'))
- new_expand_weight: float32 [3072, 768], P(('dp', 'tensor'))
- new_reduce_first: float32 [3072, 768], P(('dp', 'tensor'))
- new_reduce_second: float32 [3072, 768], P(('dp', 'tensor'))
- new_reduce_weight: float32 [3072, 768], P(('dp', 'tensor'))
- new_position_first: float32 [1204224], P(('dp', 'tensor'))
- new_position_second: float32 [1204224], P(('dp', 'tensor'))
- new_position_table: float32 [1204224], P(('dp', 'tensor'))
- new_norm_first: float32 [3072], P(('dp', 'tensor'))
- new_norm_second: float32 [3072], P(('dp', 'tensor'))
- new_norm_params: float32 [3072], P(('dp', 'tensor'))
- lamb_stats: float32 [3, 7], replicated
The draws below stay inside these ranges and needn't reach their ends.
Inputs may be any that keep to these rules, and one draw needn't show every extreme that they name: `clip_lengths`: every clip has 314 rows (a video clip) or 39 rows (an image). `clip_device`: each device index d = i * 2 + j holds exactly 4 clips, at most 2 of them video clips, and some device holds 2. `kept_patches`: within a video clip the rows hold distinct positions below 1568 in rising order, within an image distinct positions below 196 in rising order; padding rows hold 0. `norm_params`: gains lie in 0.5 to 1.5; shifts are normal of deviation 0.5, held within -1.5 to 1.5.
All inputs are finite; a program needn't handle non-finite values.
Results may differ from the reference program's by a relative error of at most 0.0085.
The reference program's roundings to bfloat16 on the way count: a program that leaves them out, or rounds other values in their place, can miss the bound.
Values may be sent and summed in bfloat16 or wider, within the bound.
A program may use at most 192 MiB of HBM per device.

```python
import math
import jax
import jax.numpy as jnp
from jax import lax

D = 768
H = 12
HD = 64
FF = 3072
AL = 1024
GRID = 196
VID_LEN = 314
IMG_LEN = 39
CLIP_DEV = 4
MAX_VID = 2
TOK_DEV = 768
POS = 1568
TOKENS = 24576
CLIPS = 128
N_DP = 16
N_TENSOR = 2


def clip_layout(key):
    base_key = jax.random.fold_in(key, 101)
    count_key, pick_key, order_key, patch_key = jax.random.split(base_key, 4)
    devices = CLIPS // CLIP_DEV
    videos = jax.random.randint(count_key, (devices,), 0, MAX_VID + 1)
    videos = videos.at[jax.random.randint(pick_key, (), 0, devices)].set(MAX_VID)
    slot_index = jnp.arange(CLIPS, dtype=jnp.int32)
    slot_device = slot_index // CLIP_DEV
    slot_length = jnp.where(slot_index % CLIP_DEV < videos[slot_device], VID_LEN, IMG_LEN).astype(jnp.int32)
    clip_order = jax.random.permutation(order_key, CLIPS).astype(jnp.int32)
    lengths = jnp.zeros((CLIPS,), jnp.int32).at[clip_order].set(slot_length)
    owner_device = jnp.zeros((CLIPS,), jnp.int32).at[clip_order].set(slot_device)
    return (lengths, owner_device, clip_order, slot_length, patch_key)


def draw_clip_lengths(key, part):
    return clip_layout(key)[0]


def draw_clip_device(key, part):
    return clip_layout(key)[1]


def draw_kept_patches(key, part):
    lengths, owner_device, clip_order, slot_length, patch_key = clip_layout(key)
    devices = CLIPS // CLIP_DEV
    clip_number = clip_order.reshape(devices, CLIP_DEV)
    clip_size = slot_length.reshape(devices, CLIP_DEV)
    clip_rank = jnp.sum((clip_number[:, None, :] < clip_number[:, :, None]).astype(jnp.int32), axis=2)
    clip_start = jnp.sum(jnp.where(clip_rank[:, None, :] < clip_rank[:, :, None], clip_size[:, None, :], 0), axis=2)
    patch_keys = jax.random.split(patch_key, CLIPS)
    video_pick = jax.vmap(lambda one_key: jnp.sort(jax.random.permutation(one_key, POS)[:VID_LEN]))(patch_keys)
    image_pick = jax.vmap(lambda one_key: jnp.sort(jax.random.permutation(jax.random.fold_in(one_key, 5), GRID)[:IMG_LEN]))(patch_keys)
    image_full = jnp.pad(image_pick, ((0, 0), (0, VID_LEN - IMG_LEN)))
    chosen = jnp.where((slot_length == VID_LEN)[:, None], video_pick, image_full).astype(jnp.int32)
    positions = jnp.arange(TOK_DEV, dtype=jnp.int32)
    covered = (positions[None, :, None] >= clip_start[:, None, :]) & (positions[None, :, None] < (clip_start + clip_size)[:, None, :])
    slot_taken = jnp.sum(jnp.where(covered, jnp.arange(CLIP_DEV, dtype=jnp.int32)[None, None, :], 0), axis=2)
    occupied = jnp.any(covered, axis=2)
    row_start = jnp.take_along_axis(clip_start, slot_taken, axis=1)
    within = jnp.clip(positions[None, :] - row_start, 0, VID_LEN - 1)
    flat_index = (jnp.arange(devices, dtype=jnp.int32)[:, None] * CLIP_DEV + slot_taken) * VID_LEN + within
    patches = jnp.where(occupied, jnp.take(chosen.reshape(-1), flat_index), 0)
    return patches.reshape(-1).astype(jnp.int32)


def draw_norm_params(key, part):
    gain_key, shift_key = jax.random.split(jax.random.fold_in(key, 3))
    gains = jax.random.uniform(gain_key, (2, D), jnp.float32, 0.5, 1.5)
    shifts = jnp.clip(0.5 * jax.random.normal(shift_key, (2, D), jnp.float32), -1.5, 1.5)
    return jnp.stack((gains[0], shifts[0], gains[1], shifts[1])).reshape(-1)


def levels(rng, extent, cuts, low, largest):
    factor_of, own = 1.0, jax.random.fold_in(rng, 6)
    for axis_at, shards_of in cuts:
        draws = jnp.exp(jax.random.uniform(jax.random.fold_in(own, axis_at), (shards_of,), jnp.float32, low / len(cuts), largest / len(cuts)))
        factor_of = factor_of * jnp.repeat(draws, extent[axis_at] // shards_of).reshape([-1 if axis == axis_at else 1 for axis in range(len(extent))])
    return factor_of


def normal_values(rng, dims, deviation, most, shards=(), held_as=jnp.bfloat16):
    result = jax.random.normal(rng, dims, jnp.float32) * deviation
    if len(shards) > 0:
        result = levels(rng, dims, shards, -0.22, 0.18) * result
    return jnp.clip(result, min=-most, max=most).astype(held_as)


def setup_inputs(seed: int = 0) -> dict:
    seeds = jax.random.split(jax.random.key(seed), 28)
    return {
        "tokens": normal_values(seeds[0], (TOKENS, D), 1.0, 6.0, ((0, 32),)),
        "kept_patches": draw_kept_patches(jax.random.fold_in(seeds[27], 71), 0),
        "clip_lengths": draw_clip_lengths(jax.random.fold_in(seeds[27], 71), 0),
        "clip_device": draw_clip_device(jax.random.fold_in(seeds[27], 71), 0),
        "cot_output": normal_values(seeds[4], (TOKENS, D), 1.0, 6.0, ((0, 32),)),
        "cot_aligned": normal_values(seeds[5], (TOKENS, AL), 1.0, 6.0, ((0, 32),)),
        "entry_weight": normal_values(seeds[6], (3 * D * D,), D ** -0.5, 0.21875, ((0, 32),), jnp.float32),
        "entry_first": normal_values(seeds[7], (3 * D * D,), (0.11 * TOKENS ** 0.5), 112.0, ((0, 32),), jnp.float32),
        "entry_second": jnp.clip(jnp.exp(math.log(4096.8193) - 2.8136108 * jax.random.uniform(seeds[8], (3 * D * D,), jnp.float32) ** levels(seeds[8], (3 * D * D,), ((0, 32),), -0.2, 0.2)), 245.76, 4096.8193),
        "exit_weight": normal_values(seeds[9], (D * D,), (D // 64) ** -0.5, 1.75, ((0, 32),), jnp.float32),
        "exit_first": normal_values(seeds[10], (D * D,), (0.025 * TOKENS ** 0.5), 24.0, ((0, 32),), jnp.float32),
        "exit_second": jnp.clip(jnp.exp(math.log(204.71808) - 2.8130106 * jax.random.uniform(seeds[11], (D * D,), jnp.float32) ** levels(seeds[11], (D * D,), ((0, 32),), -0.2, 0.2)), 12.288, 204.71808),
        "align_weight": normal_values(seeds[12], (D * AL,), D ** -0.5, 0.21875, ((0, 32),), jnp.float32),
        "align_first": normal_values(seeds[13], (D * AL,), (0.15 * TOKENS ** 0.5), 128.0, ((0, 32),), jnp.float32),
        "align_second": jnp.clip(jnp.exp(math.log(8183.808) - 2.9067209 * jax.random.uniform(seeds[14], (D * AL,), jnp.float32) ** levels(seeds[14], (D * AL,), ((0, 32),), -0.2, 0.2)), 447.2832, 8183.808),
        "expand_weight": normal_values(seeds[15], (FF, D), D ** -0.5, 0.21875, ((0, 32),), jnp.float32),
        "expand_first": normal_values(seeds[16], (FF, D), (0.035 * TOKENS ** 0.5), 32.0, ((0, 32),), jnp.float32),
        "expand_second": jnp.clip(jnp.exp(math.log(409.68192) - 2.8136107 * jax.random.uniform(seeds[17], (FF, D), jnp.float32) ** levels(seeds[17], (FF, D), ((0, 32),), -0.2, 0.2)), 24.576, 409.68192),
        "reduce_weight": normal_values(seeds[18], (FF, D), FF ** -0.5, 0.109375, ((0, 32),), jnp.float32),
        "reduce_first": normal_values(seeds[19], (FF, D), (0.085 * TOKENS ** 0.5), 80.0, ((0, 32),), jnp.float32),
        "reduce_second": jnp.clip(jnp.exp(math.log(2457.6) - 2.8336135 * jax.random.uniform(seeds[20], (FF, D), jnp.float32) ** levels(seeds[20], (FF, D), ((0, 32),), -0.2, 0.2)), 144.50688, 2457.6),
        "position_table": normal_values(seeds[21], (POS * D,), 0.5, 3.0, ((0, 32),), jnp.float32),
        "position_first": normal_values(seeds[22], (POS * D,), (0.2 * (TOKENS * POS ** -1) ** 0.5), 5.0, ((0, 32),), jnp.float32),
        "position_second": jnp.clip(jnp.exp(math.log(7.836735) - 2.7090507 * jax.random.uniform(seeds[23], (POS * D,), jnp.float32) ** levels(seeds[23], (POS * D,), ((0, 32),), -0.2, 0.2)), 0.5219265, 7.836735),
        "norm_params": draw_norm_params(jax.random.fold_in(seeds[27], 71), 0),
        "norm_first": normal_values(seeds[25], (4 * D,), (0.15 * TOKENS ** 0.5), 128.0, ((0, 32),), jnp.float32),
        "norm_second": jnp.clip(jnp.exp(math.log(8183.808) - 2.9067209 * jax.random.uniform(seeds[26], (4 * D,), jnp.float32) ** levels(seeds[26], (4 * D,), ((0, 32),), -0.2, 0.2)), 447.2832, 8183.808),
    }


@jax.custom_vjp
def low(v):
    return lax.optimization_barrier(v.astype(jnp.bfloat16)).astype(jnp.float32)

@jax.custom_vjp
def low_back(v):
    return v

def low_keep(v):
    return (low(v), None)

def low_pass(kept, grad):
    return (grad,)

def back_keep(v):
    return (v, None)

def back_low(kept, grad):
    return (low(grad),)
low.defvjp(low_keep, low_pass)
low_back.defvjp(back_keep, back_low)
LN_EPS = 1e-06
MASKED = -1e+30
RATE = 0.5
BETA_ONE = 0.9
BETA_TWO = 0.98
ADAM_EPS = 1e-06
DECAY = 0.05
TINY = 1e-06

def matmul_high(left, right):
    return jnp.dot(left, right, precision=lax.Precision.HIGHEST)

def layer_norm(values, gain, shift):
    center = values - lax.optimization_barrier(jnp.mean(values, axis=-1, keepdims=True))
    spread = lax.optimization_barrier(jnp.mean(center * center, axis=-1, keepdims=True))
    return center * lax.rsqrt(spread + LN_EPS) * gain + shift

def row_layout(clip_lengths, clip_device, device, row_count):
    mine = clip_device == device
    own_length = jnp.where(mine, clip_lengths, 0).astype(jnp.int32)
    starts = jnp.cumsum(own_length).astype(jnp.int32) - own_length
    filled = jnp.sum(own_length)
    positions = jnp.arange(row_count, dtype=jnp.int32)
    begun = mine[None, :] & (starts[None, :] <= positions[:, None])
    segment = lax.optimization_barrier(jnp.sum(begun.astype(jnp.int32), axis=1))
    valid_rows = positions < filled
    return (jnp.where(valid_rows, segment, 0).astype(jnp.int32), valid_rows)

def lamb_update(weight, gradient, first, second, decay):
    new_first = BETA_ONE * first + (1.0 - BETA_ONE) * gradient
    new_second = BETA_TWO * second + (1.0 - BETA_TWO) * gradient * gradient
    update = new_first / (jnp.sqrt(new_second) + ADAM_EPS) + decay * weight
    weight_square = jnp.sum(weight * weight)
    update_square = jnp.sum(update * update)
    trust = jnp.sqrt(weight_square) / jnp.sqrt(update_square + TINY)
    stats = jnp.stack((trust, jnp.sqrt(weight_square), jnp.sqrt(update_square)))
    return (new_first, new_second, weight - RATE * trust * update, stats)

def reference(tokens, kept_patches, clip_lengths, clip_device, cot_output, cot_aligned, entry_weight, entry_first, entry_second, exit_weight, exit_first, exit_second, align_weight, align_first, align_second, expand_weight, expand_first, expand_second, reduce_weight, reduce_first, reduce_second, position_table, position_first, position_second, norm_params, norm_first, norm_second):
    devices = N_DP * N_TENSOR
    device_ids = jnp.arange(devices, dtype=jnp.int32)
    segment, valid_rows = lax.map(lambda device: row_layout(clip_lengths, clip_device, device, TOK_DEV), device_ids)
    kept_rows = kept_patches.reshape(devices, TOK_DEV)
    score_scale = HD ** (-0.5)

    def forward(token_float, entry_master, exit_master, align_master, expand_master, reduce_master, table_master, norm_master):
        entry_low = low(entry_master.reshape(D, 3 * D))
        exit_low = low(exit_master.reshape(D, D))
        align_low = low(align_master.reshape(D, AL))
        expand_low = low(expand_master)
        reduce_low = low(reduce_master)
        table_low = low(table_master.reshape(POS, D))
        norm_low = low(norm_master).reshape(4, D)

        def one_device(entries):
            token_rows, kept_one, segment_one, valid_one = entries
            residual = token_rows + table_low[kept_one]
            normed_one = low(layer_norm(residual, norm_low[0], norm_low[1]))
            joint = low_back(low(matmul_high(normed_one, entry_low)))
            queries = joint[:, :D].reshape(TOK_DEV, H, HD)
            key_rows = joint[:, D:2 * D].reshape(TOK_DEV, H, HD)
            value_rows = joint[:, 2 * D:].reshape(TOK_DEV, H, HD)
            scores = jnp.einsum('qhd,khd->hqk', queries, key_rows, precision=lax.Precision.HIGHEST) * score_scale
            scores = low_back(scores)
            same_clip = segment_one[:, None] == segment_one[None, :]
            scores = jnp.where(same_clip[None, :, :], scores, MASKED)
            attention = jax.nn.softmax(scores, axis=-1)
            attended = jnp.einsum('hqk,khd->qhd', low(attention), value_rows, precision=lax.Precision.HIGHEST)
            attended = low_back(low(attended.reshape(TOK_DEV, D)))
            middle = residual + low_back(matmul_high(attended, exit_low))
            normed_two = low(layer_norm(middle, norm_low[2], norm_low[3]))
            hidden_pre = low_back(matmul_high(normed_two, expand_low.T))
            hidden_act = low(jax.nn.gelu(hidden_pre, approximate=False))
            block_rows = low(middle + low_back(matmul_high(hidden_act, reduce_low)))
            aligned_rows = low(matmul_high(block_rows, align_low))
            keep = valid_one[:, None].astype(jnp.float32)
            return (block_rows * keep, aligned_rows * keep)
        block_all, aligned_all = lax.map(jax.checkpoint(one_device), (token_float.reshape(devices, TOK_DEV, D), kept_rows, segment, valid_rows))
        return (block_all.reshape(-1, D), aligned_all.reshape(-1, AL))
    outputs, pullback = jax.vjp(forward, tokens.astype(jnp.float32), entry_weight, exit_weight, align_weight, expand_weight, reduce_weight, position_table, norm_params)
    grads = pullback((cot_output.astype(jnp.float32), cot_aligned.astype(jnp.float32)))
    entry_new = lamb_update(entry_weight, grads[1], entry_first, entry_second, DECAY)
    exit_new = lamb_update(exit_weight, grads[2], exit_first, exit_second, DECAY)
    align_new = lamb_update(align_weight, grads[3], align_first, align_second, DECAY)
    expand_new = lamb_update(expand_weight, grads[4], expand_first, expand_second, DECAY)
    reduce_new = lamb_update(reduce_weight, grads[5], reduce_first, reduce_second, DECAY)
    position_new = lamb_update(position_table, grads[6], position_first, position_second, DECAY)
    norm_new = lamb_update(norm_params, grads[7], norm_first, norm_second, 0.0)
    lamb_stats = jnp.stack((entry_new[3], exit_new[3], align_new[3], expand_new[3], reduce_new[3], position_new[3], norm_new[3]), axis=1)
    return (outputs[0].astype(jnp.bfloat16), outputs[1].astype(jnp.bfloat16), grads[0], entry_new[0], entry_new[1], entry_new[2], exit_new[0], exit_new[1], exit_new[2], align_new[0], align_new[1], align_new[2], expand_new[0], expand_new[1], expand_new[2], reduce_new[0], reduce_new[1], reduce_new[2], position_new[0], position_new[1], position_new[2], norm_new[0], norm_new[1], norm_new[2], lamb_stats)
```

```python
import functools

import jax
import jax.numpy as jnp
from jax import lax
from jax.experimental import pallas as pl
from jax.experimental.pallas import tpu as pltpu
from jax.sharding import PartitionSpec as P

H = 12
HD = 64
LN_EPS = 1e-06
RATE = 0.5
BETA_ONE = 0.9
BETA_TWO = 0.98
ADAM_EPS = 1e-06
DECAY = 0.05
TINY = 1e-06
BF = jnp.bfloat16
F32 = jnp.float32
MESH = pl.DeviceIdType.MESH
ANY = pl.BlockSpec(memory_space=pl.ANY)
VMEM = pl.BlockSpec(memory_space=pltpu.VMEM)
MIB = 1 << 20

TABLE, ENTRY, EXIT, EXPAND, REDUCE, ALIGN = range(6)
TABLE_ROWS = 49
TABLE_SLAB = 56
NORM_LANES = 96
ROUTED_DP = 16


def contract(left, right, left_dim, right_dim):
    return lax.dot_general(
        left, right, (((left_dim,), (right_dim,)), ((), ())), preferred_element_type=F32
    )


def layer_norm(values, gain, shift):
    center = values - jnp.mean(values, axis=-1, keepdims=True)
    spread = jnp.mean(center * center, axis=-1, keepdims=True)
    return center * lax.rsqrt(spread + LN_EPS) * gain + shift


def gelu_exact(values):
    return jax.nn.gelu(values, approximate=False)


def row_layout(clip_lengths, clip_device, device, row_count):
    mine = clip_device == device
    own_length = jnp.where(mine, clip_lengths, 0)
    starts = jnp.cumsum(own_length) - own_length
    filled = jnp.sum(own_length)
    positions = jnp.arange(row_count, dtype=jnp.int32)
    begun = mine[None, :] & (starts[None, :] <= positions[:, None])
    segment = jnp.sum(begun.astype(jnp.int32), axis=1)
    valid_rows = positions < filled
    return (jnp.where(valid_rows, segment, 0), valid_rows)


class Route:
    def __init__(self):
        dp = lax.axis_index("dp")
        core = lax.axis_index("tensor")
        z, y, x = dp // 4, (dp // 2) % 2, dp % 2
        across_y = dp + 2 - 4 * y
        across_x = dp + 1 - 2 * x
        self.dp, self.core, self.me = dp, core, dp * 2 + core
        self.near = across_y * (1 - core) + across_x * core
        self.far = across_x * (1 - core) + across_y * core
        self.both = self.near + self.far - dp
        levels = [z + 1 - 2 * (z % 2), 3 - z, (z + 2) % 4]
        self.peers = [level * 4 + y * 2 + x for level in levels]
        self.levels = [dp] + self.peers
        self.partners = [(peer, core) for peer in self.peers] + [
            (self.near, core),
            (self.far, core),
            (dp, 1 - core),
        ]

    def at_level(self, base, step):
        return (self.levels[step] // 4) * 4 + base % 4


def greet(partners):
    barrier = pltpu.get_barrier_semaphore()
    for partner in partners:
        pl.semaphore_signal(barrier, inc=1, device_id=partner, device_id_type=MESH)
    return lambda: pl.semaphore_wait(barrier, len(partners))


def fold_rows(source, rows, columns):
    blocks = columns // 128
    for block in range(blocks):
        yield block, source[pl.ds(block, rows, stride=blocks), :]


def gather_kernel(shapes, groups, *refs):
    count = len(shapes)
    shards, norm = refs[:count], refs[count]
    outs = refs[count + 1 : 2 * count + 1]
    slabs = refs[2 * count + 1 : 3 * count + 1]
    pad, send_sem, recv_sem, own_sem = refs[3 * count + 1 :]
    route = Route()
    arrive = greet(route.partners)
    for piece, (rows, columns) in enumerate(shapes):
        if piece == TABLE:
            blocks = columns // 128
            pad[...] = jnp.zeros_like(pad)
            pad[0:1, 0:NORM_LANES] = norm[...]
            norm_row = pad[0:1, :]
            row_id = lax.broadcasted_iota(jnp.int32, (8, 128), 0)
            for block in range(blocks):
                lanes = slice(block * 128, block * 128 + 128)
                whole = TABLE_ROWS - 1
                slabs[piece][0:whole, lanes] = shards[piece][
                    pl.ds(block, whole, stride=blocks), :
                ].astype(BF)
                last = shards[piece][pl.ds(whole * blocks + block, 1), :]
                tail = jnp.where(row_id == 0, last, 0.0)
                if block == 0:
                    tail = jnp.where(row_id == 1, norm_row, tail)
                slabs[piece][whole : whole + 8, lanes] = tail.astype(BF)
        elif shards[piece].shape == (rows, columns):
            slabs[piece][...] = shards[piece][...].astype(BF)
        else:
            for block, part in fold_rows(shards[piece], rows, columns):
                slabs[piece][:, block * 128 : block * 128 + 128] = part.astype(BF)
    arrive()
    pending = []

    def send(source, piece, origin, partner):
        copy = pltpu.make_async_remote_copy(
            src_ref=source,
            dst_ref=outs[piece].at[origin],
            send_sem=send_sem.at[len(pending)],
            recv_sem=recv_sem.at[piece, origin],
            device_id=partner,
            device_id_type=MESH,
        )
        copy.start()
        pending.append(copy)

    def wait(piece, origin):
        block = outs[piece].at[origin]
        pltpu.make_async_copy(block, block, recv_sem.at[piece, origin]).wait()

    core = route.core
    near, far, pair = (route.near, core), (route.far, core), (route.dp, 1 - core)
    own = []

    def pass_on(group, origin, partners):
        for piece in group:
            wait(piece, origin)
        for partner in partners:
            for piece in group:
                send(outs[piece].at[origin], piece, origin, partner)

    for group in groups:
        for piece in group:
            for partner in [near, far] + [(peer, core) for peer in route.peers] + [pair]:
                send(slabs[piece], piece, route.me, partner)
            copy = pltpu.make_async_copy(
                slabs[piece], outs[piece].at[route.me], own_sem.at[piece]
            )
            copy.start()
            own.append(copy)
        for step in range(4):
            if step > 0:
                pass_on(group, route.levels[step] * 2 + core, (near, far, pair))
            pass_on(group, route.at_level(route.near, step) * 2 + core, (far, pair))
        for step in range(4):
            for base in (route.far, route.both):
                pass_on(group, route.at_level(base, step) * 2 + core, (pair,))
    for group in groups:
        for piece in group:
            for dp in range(ROUTED_DP):
                wait(piece, dp * 2 + 1 - core)
    for copy in pending:
        copy.wait_send()
    for copy in own:
        copy.wait()


def gather_weights(shards, norm, shapes, devices):
    count = len(shapes)
    groups = ((TABLE, ENTRY), (EXIT, EXPAND, REDUCE, ALIGN))
    return pl.pallas_call(
        functools.partial(gather_kernel, shapes, groups),
        out_shape=[jax.ShapeDtypeStruct((devices,) + shape, BF) for shape in shapes],
        in_specs=[VMEM] * (count + 1),
        out_specs=[ANY] * count,
        scratch_shapes=[pltpu.VMEM(shape, BF) for shape in shapes]
        + [
            pltpu.VMEM((8, 128), F32),
            pltpu.SemaphoreType.DMA((31 * count,)),
            pltpu.SemaphoreType.DMA((count, devices)),
            pltpu.SemaphoreType.DMA((count,)),
        ],
        compiler_params=pltpu.CompilerParams(
            collective_id=0, has_side_effects=True, vmem_limit_bytes=40 * MIB
        ),
        name="gather_weights",
    )(*shards, norm)


def scatter_kernel(shapes, order, *refs):
    count = len(shapes)
    grads, outs = refs[:count], refs[count : 2 * count]
    own = refs[2 * count : 3 * count]
    from_pair = refs[3 * count : 4 * count]
    from_far = refs[4 * count : 5 * count]
    from_near = refs[5 * count : 6 * count]
    from_peer = refs[6 * count : 7 * count]
    send_sem, pair_sem, far_sem, near_sem, peer_sem, own_sem = refs[7 * count :]
    route = Route()
    arrive = greet(route.partners)
    core = route.core
    near, far, pair = (route.near, core), (route.far, core), (route.dp, 1 - core)
    pending, local = [], {}

    def send(source, target, semaphore, partner):
        copy = pltpu.make_async_remote_copy(
            src_ref=source,
            dst_ref=target,
            send_sem=send_sem.at[len(pending)],
            recv_sem=semaphore,
            device_id=partner,
            device_id_type=MESH,
        )
        copy.start()
        pending.append(copy)

    def landed(block, semaphore):
        pltpu.make_async_copy(block, block, semaphore).wait()

    far_list = [route.at_level(base, step) for step in range(4) for base in (route.far, route.both)]
    near_list = [route.at_level(route.near, step) for step in range(4)]
    own_list = route.levels
    for piece in order:
        for index, dp in enumerate(far_list + near_list + own_list):
            copy = pltpu.make_async_copy(
                grads[piece].at[dp * 2 + core], own[piece].at[index], own_sem.at[piece, index]
            )
            copy.start()
            local[piece, index] = copy
    arrive()
    for piece in order:
        for dp in range(ROUTED_DP):
            send(
                grads[piece].at[dp * 2 + 1 - core],
                from_pair[piece].at[dp],
                pair_sem.at[piece, dp],
                pair,
            )

    def total(piece, index, dp, sources):
        local[piece, index].wait()
        landed(from_pair[piece].at[dp], pair_sem.at[piece, dp])
        found = own[piece][index].astype(F32) + from_pair[piece][dp].astype(F32)
        for block, semaphore, slot in sources:
            landed(block.at[slot], semaphore.at[piece, slot])
            found = found + block[slot].astype(F32)
        return found

    def stage_far(piece):
        for index, dp in enumerate(far_list):
            own[piece][index] = total(piece, index, dp, ()).astype(BF)
            send(own[piece].at[index], from_far[piece].at[index], far_sem.at[piece, index], far)

    def stage_near(piece):
        for step, dp in enumerate(near_list):
            index = 8 + step
            found = total(piece, index, dp, ((from_far[piece], far_sem, step * 2 + 1),))
            own[piece][index] = found.astype(BF)
            send(own[piece].at[index], from_near[piece].at[step], near_sem.at[piece, step], near)

    def stage_peer(piece):
        for step in (1, 2, 3):
            index = 12 + step
            dp = own_list[step]
            found = total(
                piece,
                index,
                dp,
                ((from_far[piece], far_sem, step * 2), (from_near[piece], near_sem, step)),
            )
            own[piece][index] = found.astype(BF)
            send(
                own[piece].at[index],
                from_peer[piece].at[step - 1],
                peer_sem.at[piece, step - 1],
                (route.peers[step - 1], core),
            )

    def stage_own(piece):
        found = total(
            piece,
            12,
            own_list[0],
            ((from_far[piece], far_sem, 0), (from_near[piece], near_sem, 0))
            + tuple((from_peer[piece], peer_sem, slot) for slot in range(3)),
        )
        outs[piece][...] = found

    stages = (stage_far, stage_near, stage_peer, stage_own)
    for turn in range(len(order) + 3):
        for late, stage in enumerate(stages):
            if 0 <= turn - late < len(order):
                stage(order[turn - late])
    for copy in pending:
        copy.wait_send()


def scatter_gradients(grads, shapes, devices):
    count = len(shapes)
    order = (EXPAND, REDUCE, ALIGN, ENTRY, TABLE, EXIT)
    rows = devices // 2

    def buffers(slots):
        return [pltpu.VMEM((slots,) + shape, BF) for shape in shapes]

    return pl.pallas_call(
        functools.partial(scatter_kernel, shapes, order),
        out_shape=[jax.ShapeDtypeStruct(shape, F32) for shape in shapes],
        in_specs=[ANY] * count,
        out_specs=[VMEM] * count,
        scratch_shapes=buffers(rows)
        + buffers(rows)
        + buffers(8)
        + buffers(4)
        + buffers(3)
        + [
            pltpu.SemaphoreType.DMA((31 * count,)),
            pltpu.SemaphoreType.DMA((count, rows)),
            pltpu.SemaphoreType.DMA((count, 8)),
            pltpu.SemaphoreType.DMA((count, 4)),
            pltpu.SemaphoreType.DMA((count, 3)),
            pltpu.SemaphoreType.DMA((count, rows)),
        ],
        compiler_params=pltpu.CompilerParams(
            collective_id=1, has_side_effects=True, vmem_limit_bytes=60 * MIB
        ),
        name="scatter_gradients",
    )(*grads)


def exchange_kernel(devices, part, out, held, send_sem, recv_sem):
    dp = lax.axis_index("dp")
    core = lax.axis_index("tensor")
    me = dp * 2 + core
    barrier = pltpu.get_barrier_semaphore()

    def partner(step):
        other = lax.rem(me + step, devices)
        return other, (other // 2, lax.rem(other, 2))

    def hail(step, carry):
        pl.semaphore_signal(
            barrier, inc=1, device_id=partner(step)[1], device_id_type=MESH
        )
        return carry

    lax.fori_loop(1, devices, hail, 0)
    held[me] = part[...]
    pl.semaphore_wait(barrier, devices - 1)

    def copy_to(step):
        return pltpu.make_async_remote_copy(
            src_ref=held.at[me],
            dst_ref=held.at[me],
            send_sem=send_sem.at[step],
            recv_sem=recv_sem.at[me],
            device_id=partner(step)[1],
            device_id_type=MESH,
        )

    def start(step, carry):
        copy_to(step).start()
        return carry

    def take(step, carry):
        other = partner(step)[0]
        block = held.at[other]
        pltpu.make_async_copy(block, block, recv_sem.at[other]).wait()
        return carry

    def sent(step, carry):
        copy_to(step).wait_send()
        return carry

    lax.fori_loop(1, devices, start, 0)
    lax.fori_loop(1, devices, take, 0)
    out[...] = jnp.sum(held[...], axis=0)
    lax.fori_loop(1, devices, sent, 0)


def exchange_sums(part, devices):
    return pl.pallas_call(
        functools.partial(exchange_kernel, devices),
        out_shape=jax.ShapeDtypeStruct(part.shape, F32),
        in_specs=[VMEM],
        out_specs=VMEM,
        scratch_shapes=[
            pltpu.VMEM((devices,) + part.shape, F32),
            pltpu.SemaphoreType.DMA((devices,)),
            pltpu.SemaphoreType.DMA((devices,)),
        ],
        compiler_params=pltpu.CompilerParams(collective_id=2, has_side_effects=True),
        name="exchange_sums",
    )(part)


def lane_marks(head, segment_column):
    lane = lax.broadcasted_iota(jnp.int32, (segment_column.shape[0], 128), 1)
    mine = (lane // HD) == head
    same = (lane % HD) == segment_column
    return mine, same


def attend_kernel(segment, query, key, value, out):
    rows = query.shape[0]
    chunk = 256
    for head in (0, 1):
        mine, same = lane_marks(head, segment[...])
        keys = jnp.where(mine, key[...], jnp.where(same, 0.0, -1e30).astype(BF))
        queries = jnp.where(mine, query[...] * BF(HD**-0.5), same.astype(BF))
        values = value[...]
        for start in range(0, rows, chunk):
            scores = contract(queries[start : start + chunk], keys, 1, 1)
            peak = jnp.max(scores, axis=1, keepdims=True)
            raised = jnp.exp(scores - peak)
            scale = 1.0 / jnp.sum(raised, axis=1, keepdims=True)
            attention = (raised * scale).astype(BF)
            result = contract(attention, values, 1, 0).astype(BF)
            span = slice(start, start + chunk)
            if head == 0:
                out[span, :] = result
            else:
                out[span, :] = jnp.where(mine[span], result, out[span, :])


def attend(segment, joint):
    rows, width = joint.shape[0], joint.shape[1] // 3
    pairs = width // 128
    return pl.pallas_call(
        attend_kernel,
        grid=(pairs,),
        out_shape=jax.ShapeDtypeStruct((rows, width), BF),
        in_specs=[
            pl.BlockSpec((rows, 1), lambda pair: (0, 0)),
            pl.BlockSpec((rows, 128), lambda pair: (0, pair)),
            pl.BlockSpec((rows, 128), lambda pair: (0, pairs + pair)),
            pl.BlockSpec((rows, 128), lambda pair: (0, 2 * pairs + pair)),
        ],
        out_specs=pl.BlockSpec((rows, 128), lambda pair: (0, pair)),
        compiler_params=pltpu.CompilerParams(vmem_limit_bytes=40 * MIB),
        name="attend",
    )(segment, joint, joint, joint)


def attend_back_kernel(segment, query, key, value, grad, out, key_sum, value_sum):
    rows = query.shape[0]
    chunk = 256
    scale = HD**-0.5
    for head in (0, 1):
        mine, same = lane_marks(head, segment[...])
        keys = jnp.where(mine, key[...], jnp.where(same, 0.0, -1e30).astype(BF))
        scaled = query[...] * BF(scale)
        queries = jnp.where(mine, scaled, same.astype(BF))
        zero = jnp.zeros_like(scaled)
        pure_queries = jnp.where(mine, scaled, zero)
        pure_keys = jnp.where(mine, key[...], zero)
        grads = jnp.where(mine, grad[...], zero)
        values = value[...]
        for start in range(0, rows, chunk):
            span = slice(start, start + chunk)
            scores = contract(keys, queries[span], 1, 1)
            peak = jnp.max(scores, axis=0, keepdims=True)
            raised = jnp.exp(scores - peak)
            attention = raised * (1.0 / jnp.sum(raised, axis=0, keepdims=True))
            grad_values = contract(attention.astype(BF), grads[span], 1, 0)
            grad_attention = contract(values, grads[span], 1, 1)
            inner = jnp.sum(attention * grad_attention, axis=0, keepdims=True)
            grad_score = (attention * (grad_attention - inner)).astype(BF)
            grad_keys = contract(grad_score, pure_queries[span], 1, 0)
            grad_queries = contract(grad_score, pure_keys, 0, 0) * scale
            if head == 0:
                out[0, span, :] = grad_queries.astype(BF)
            else:
                out[0, span, :] = jnp.where(mine[span], grad_queries.astype(BF), out[0, span, :])
            if head == 0 and start == 0:
                key_sum[...] = grad_keys
                value_sum[...] = grad_values
            else:
                key_sum[...] += grad_keys
                value_sum[...] += grad_values
    out[1] = key_sum[...].astype(BF)
    out[2] = value_sum[...].astype(BF)


def attend_back(segment, joint, grad_attended):
    rows, width = grad_attended.shape
    pairs = width // 128
    return pl.pallas_call(
        attend_back_kernel,
        grid=(pairs,),
        out_shape=jax.ShapeDtypeStruct((3, rows, width), BF),
        in_specs=[
            pl.BlockSpec((rows, 1), lambda pair: (0, 0)),
            pl.BlockSpec((rows, 128), lambda pair: (0, pair)),
            pl.BlockSpec((rows, 128), lambda pair: (0, pairs + pair)),
            pl.BlockSpec((rows, 128), lambda pair: (0, 2 * pairs + pair)),
            pl.BlockSpec((rows, 128), lambda pair: (0, pair)),
        ],
        out_specs=pl.BlockSpec((3, rows, 128), lambda pair: (0, 0, pair)),
        scratch_shapes=[pltpu.VMEM((rows, 128), F32), pltpu.VMEM((rows, 128), F32)],
        compiler_params=pltpu.CompilerParams(vmem_limit_bytes=40 * MIB),
        name="attend_back",
    )(segment, joint, joint, joint, grad_attended)


def moments_kernel(decays, *refs):
    count = len(decays)
    sums = refs[7 * count]
    row = lax.broadcasted_iota(jnp.int32, (16, 128), 0)
    found = jnp.zeros((16, 128), F32)
    for member, decay in enumerate(decays):
        weight, gradient, first, second = refs[4 * member : 4 * member + 4]
        new_first_ref, new_second_ref, update_ref = refs[
            4 * count + 3 * member : 4 * count + 3 * member + 3
        ]
        slope = gradient[...]
        new_first = BETA_ONE * first[...] + (1.0 - BETA_ONE) * slope
        new_second = BETA_TWO * second[...] + (1.0 - BETA_TWO) * slope * slope
        update = new_first / (jnp.sqrt(new_second) + ADAM_EPS) + decay * weight[...]
        new_first_ref[...] = new_first
        new_second_ref[...] = new_second
        update_ref[...] = update
        found = jnp.where(row == member, jnp.sum(weight[...] * weight[...]), found)
        found = jnp.where(row == 8 + member, jnp.sum(update * update), found)
    sums[...] = found


def moments(members, decays):
    shapes = [jax.ShapeDtypeStruct(member[0].shape, F32) for member in members]
    outs = [shape for shape in shapes for _ in range(3)]
    flat = [array for member in members for array in member]
    return pl.pallas_call(
        functools.partial(moments_kernel, decays),
        out_shape=outs + [jax.ShapeDtypeStruct((16, 128), F32)],
        in_specs=[VMEM] * len(flat),
        out_specs=[VMEM] * (len(outs) + 1),
        compiler_params=pltpu.CompilerParams(vmem_limit_bytes=40 * MIB),
        name="moments",
    )(*flat)


def step_kernel(count, *refs):
    sums = refs[0]
    for member in range(count):
        weight, update = refs[1 + 2 * member : 3 + 2 * member]
        weight_square = sums[member : member + 1, :]
        update_square = sums[8 + member : 9 + member, :]
        trust = jnp.sqrt(weight_square) / jnp.sqrt(update_square + TINY)
        if weight.shape[1] % 128 == 0:
            trust = jnp.concatenate([trust] * (weight.shape[1] // 128), axis=1)
        else:
            trust = trust[:, : weight.shape[1]]
        refs[1 + 2 * count + member][...] = weight[...] - RATE * trust * update[...]


def take_step(sums, pairs):
    count = len(pairs)
    return pl.pallas_call(
        functools.partial(step_kernel, count),
        out_shape=[jax.ShapeDtypeStruct(weight.shape, F32) for weight, _ in pairs],
        in_specs=[VMEM] * (1 + 2 * count),
        out_specs=[VMEM] * count,
        compiler_params=pltpu.CompilerParams(vmem_limit_bytes=40 * MIB),
        name="take_step",
    )(sums, *[array for pair in pairs for array in pair])


def as_rows(flat):
    if flat.ndim == 2:
        return flat
    lanes = max(size for size in range(1, 129) if flat.shape[0] % size == 0)
    return flat.reshape(-1, lanes)


def local(
    tokens,
    kept_patches,
    clip_lengths,
    clip_device,
    cot_output,
    cot_aligned,
    entry_weight,
    entry_first,
    entry_second,
    exit_weight,
    exit_first,
    exit_second,
    align_weight,
    align_first,
    align_second,
    expand_weight,
    expand_first,
    expand_second,
    reduce_weight,
    reduce_first,
    reduce_second,
    position_table,
    position_first,
    position_second,
    norm_params,
    norm_first,
    norm_second,
):
    rows, width = tokens.shape
    align_width = cot_aligned.shape[1]
    axes = ("dp", "tensor")
    pair = lax.axis_size("tensor")
    devices = lax.axis_size("dp") * pair
    hidden = expand_weight.shape[0] * devices
    positions = position_table.shape[0] * devices // width
    routed = devices == 2 * ROUTED_DP and pair == 2
    device = lax.axis_index("dp") * pair + lax.axis_index("tensor")
    segment, valid_rows = row_layout(clip_lengths, clip_device, device, rows)
    segment_column = segment[:, None]
    valid_column = valid_rows[:, None]
    shapes = (
        (TABLE_SLAB, width),
        (width // devices, 3 * width),
        (width // devices, width),
        (hidden // devices, width),
        (hidden // devices, width),
        (width // devices, align_width),
    )
    wholes = (
        (positions, width),
        (width, 3 * width),
        (width, width),
        (hidden, width),
        (hidden, width),
        (width, align_width),
    )
    masters = (position_table, entry_weight, exit_weight, expand_weight, reduce_weight, align_weight)
    if routed:
        blocks = gather_weights(
            [as_rows(master) for master in masters], norm_params.reshape(1, -1), shapes, devices
        )
        lows = [block.reshape(-1, block.shape[2]) for block in blocks]
        norm_low = blocks[TABLE][:, TABLE_ROWS, :NORM_LANES].reshape(4, width)
        patch = kept_patches + (kept_patches // TABLE_ROWS) * (TABLE_SLAB - TABLE_ROWS)
    else:
        lows = [
            lax.all_gather(master.astype(BF).reshape(-1), axes, axis=0, tiled=True).reshape(whole)
            for master, whole in zip(masters, wholes)
        ]
        norm_low = lax.all_gather(norm_params.astype(BF), axes, axis=0, tiled=True).reshape(4, width)
        patch = kept_patches
    table_low, entry_low, exit_low, expand_low, reduce_low, align_low = lows
    norm_low = norm_low.astype(F32)

    residual = tokens.astype(F32) + jnp.take(table_low, patch, axis=0).astype(F32)
    normed_one = layer_norm(residual, norm_low[0], norm_low[1]).astype(BF)
    joint_low = contract(normed_one, entry_low, 1, 0).astype(BF)
    attended = attend(segment_column, joint_low)
    middle = residual + contract(attended, exit_low, 1, 0)
    normed_two = layer_norm(middle, norm_low[2], norm_low[3]).astype(BF)
    hidden_pre = contract(normed_two, expand_low, 1, 1)
    hidden_act = gelu_exact(hidden_pre).astype(BF)
    out_low = (middle + contract(hidden_act, reduce_low, 1, 0)).astype(BF)
    block_out = jnp.where(valid_column, out_low, jnp.zeros_like(out_low))
    align_rows = contract(out_low, align_low, 1, 0).astype(BF)
    aligned = jnp.where(valid_column, align_rows, jnp.zeros_like(align_rows))
    cot_align_valid = jnp.where(valid_column, cot_aligned, jnp.zeros_like(cot_aligned))
    grad_align = contract(out_low, cot_align_valid, 0, 0).astype(BF)
    grad_out = jnp.where(valid_column, cot_output.astype(F32), 0.0) + contract(
        cot_align_valid, align_low, 1, 1
    )
    grad_feed = grad_out.astype(BF)
    grad_act = contract(grad_feed, reduce_low, 1, 1)
    gelu_value, gelu_back = jax.vjp(gelu_exact, hidden_pre)
    grad_pre = gelu_back(grad_act)[0].astype(BF)
    grad_reduce = contract(hidden_act, grad_feed, 0, 0).astype(BF)
    grad_expand = contract(grad_pre, normed_two, 0, 0).astype(BF)
    grad_two = contract(grad_pre, expand_low, 1, 0)
    norm_value, norm_back_two = jax.vjp(layer_norm, middle, norm_low[2], norm_low[3])
    grad_from_two, grad_gain_two, grad_shift_two = norm_back_two(grad_two)
    grad_middle = grad_out + grad_from_two
    grad_branch = grad_middle.astype(BF)
    grad_exit = contract(attended, grad_branch, 0, 0).astype(BF)
    grad_attended = contract(grad_branch, exit_low, 1, 1).astype(BF)
    grad_parts = attend_back(segment_column, joint_low, grad_attended)
    grad_joint = jnp.concatenate([grad_parts[0], grad_parts[1], grad_parts[2]], axis=1)
    grad_entry = contract(normed_one, grad_joint, 0, 0).astype(BF)
    grad_one = contract(grad_joint, entry_low, 1, 1)
    norm_value_one, norm_back_one = jax.vjp(layer_norm, residual, norm_low[0], norm_low[1])
    grad_from_one, grad_gain_one, grad_shift_one = norm_back_one(grad_one)
    token_grad = grad_middle + grad_from_one
    picks = (patch[:, None] == jnp.arange(table_low.shape[0], dtype=jnp.int32)[None, :]).astype(BF)
    grad_table = contract(picks, token_grad.astype(BF), 0, 0)
    grad_norms = jnp.concatenate((grad_gain_one, grad_shift_one, grad_gain_two, grad_shift_two))
    if routed:
        table_part = grad_table.astype(BF).reshape(devices, TABLE_SLAB, width)
        norm_part = grad_norms.reshape(devices, NORM_LANES)
        norm_high = norm_part.astype(BF)
        norm_rest = (norm_part - norm_high.astype(F32)).astype(BF)
        extra = jnp.stack((norm_high, norm_rest), axis=1)
        table_part = table_part.at[:, TABLE_ROWS : TABLE_ROWS + 2, :NORM_LANES].set(extra)
        grads = (table_part, grad_entry, grad_exit, grad_expand, grad_reduce, grad_align)
        summed = scatter_gradients(
            [grad.reshape((devices,) + shape) for grad, shape in zip(grads, shapes)], shapes, devices
        )
        table_sum = summed[TABLE]
        norm_sum = (table_sum[TABLE_ROWS] + table_sum[TABLE_ROWS + 1])[:NORM_LANES]
        summed = [table_sum[:TABLE_ROWS]] + list(summed[1:])
    else:
        grads = (grad_table, grad_entry, grad_exit, grad_expand, grad_reduce, grad_align)
        summed = [
            lax.psum_scatter(grad.reshape(-1).astype(F32), axes, scatter_dimension=0, tiled=True)
            for grad in grads
        ]
        norm_sum = lax.psum_scatter(grad_norms, axes, scatter_dimension=0, tiled=True)

    def summed_like(master, index):
        return summed[index].reshape(master.shape)

    members = (
        (entry_weight, summed_like(entry_weight, ENTRY), entry_first, entry_second),
        (exit_weight, summed_like(exit_weight, EXIT), exit_first, exit_second),
        (align_weight, summed_like(align_weight, ALIGN), align_first, align_second),
        (expand_weight, summed_like(expand_weight, EXPAND), expand_first, expand_second),
        (reduce_weight, summed_like(reduce_weight, REDUCE), reduce_first, reduce_second),
        (position_table, summed_like(position_table, TABLE), position_first, position_second),
        (norm_params, norm_sum, norm_first, norm_second),
    )
    decays = (DECAY, DECAY, DECAY, DECAY, DECAY, DECAY, 0.0)
    members = [tuple(as_rows(array) for array in member) for member in members]
    found = moments(members, decays)
    sums = found[-1]
    sums = exchange_sums(sums, devices) if routed else lax.psum(sums, axes)
    stepped = take_step(
        sums, [(members[member][0], found[3 * member + 2]) for member in range(len(members))]
    )
    weight_squares, update_squares = sums[0:7, 0], sums[8:15, 0]
    trust = jnp.sqrt(weight_squares) / jnp.sqrt(update_squares + TINY)
    outputs = [block_out, aligned, token_grad]
    originals = (
        entry_weight,
        exit_weight,
        align_weight,
        expand_weight,
        reduce_weight,
        position_table,
        norm_params,
    )
    for member, original in enumerate(originals):
        for array in (found[3 * member], found[3 * member + 1], stepped[member]):
            outputs.append(array.reshape(original.shape))
    outputs.append(jnp.stack((trust, jnp.sqrt(weight_squares), jnp.sqrt(update_squares))))
    return tuple(outputs)


def solution(mesh):
    both = ("dp", "tensor")
    rows, flat, whole = P(both, None), P(both), P()
    weight_specs = (flat,) * 9 + (rows,) * 6 + (flat,) * 6
    placed = (rows, flat, whole, whole, rows, rows) + weight_specs
    return jax.shard_map(
        local,
        mesh=mesh,
        in_specs=placed,
        out_specs=(rows, rows, rows) + weight_specs + (whole,),
        check_vma=False,
    )
```

```python
import functools
import math

import jax
import jax.numpy as jnp
from jax import lax
from jax.experimental import pallas as pl
from jax.experimental.pallas import tpu as pltpu
from jax.sharding import PartitionSpec as P

H = 12
HD = 64
LN_EPS = 1e-06
RATE = 0.5
BETA_ONE = 0.9
BETA_TWO = 0.98
ADAM_EPS = 1e-06
DECAY = 0.05
TINY = 1e-06
BF = jnp.bfloat16
F32 = jnp.float32
MESH = pl.DeviceIdType.MESH
ANY = pl.BlockSpec(memory_space=pl.ANY)
VMEM = pl.BlockSpec(memory_space=pltpu.VMEM)
MIB = 1 << 20

TABLE, ENTRY, EXIT, EXPAND, REDUCE, ALIGN = range(6)
TABLE_ROWS = 49
TABLE_SLAB = 56
NORM_LANES = 96
ROUTED_DP = 16


def contract(left, right, left_dim, right_dim):
    return lax.dot_general(
        left, right, (((left_dim,), (right_dim,)), ((), ())), preferred_element_type=F32
    )


def layer_norm(values, gain, shift):
    center = values - jnp.mean(values, axis=-1, keepdims=True)
    spread = jnp.mean(center * center, axis=-1, keepdims=True)
    return center * lax.rsqrt(spread + LN_EPS) * gain + shift


def row_layout(clip_lengths, clip_device, device, row_count):
    mine = clip_device == device
    own_length = jnp.where(mine, clip_lengths, 0)
    starts = jnp.cumsum(own_length) - own_length
    filled = jnp.sum(own_length)
    positions = jnp.arange(row_count, dtype=jnp.int32)
    begun = mine[None, :] & (starts[None, :] <= positions[:, None])
    segment = jnp.sum(begun.astype(jnp.int32), axis=1)
    valid_rows = positions < filled
    return (jnp.where(valid_rows, segment, 0), valid_rows)


class Route:
    def __init__(self):
        dp = lax.axis_index("dp")
        core = lax.axis_index("tensor")
        z, y, x = dp // 4, (dp // 2) % 2, dp % 2
        across_y = dp + 2 - 4 * y
        across_x = dp + 1 - 2 * x
        self.dp, self.core, self.me = dp, core, dp * 2 + core
        self.z, self.column = z, y * 2 + x
        self.near = across_y * (1 - core) + across_x * core
        self.far = across_x * (1 - core) + across_y * core
        self.both = self.near + self.far - dp
        levels = [z + 1 - 2 * (z % 2), 3 - z, (z + 2) % 4]
        self.peers = [level * 4 + y * 2 + x for level in levels]
        self.partners = [(peer, core) for peer in self.peers] + [
            (self.near, core),
            (self.far, core),
            (dp, 1 - core),
        ]

    def level(self, step):
        high = lax.rem(self.z // 2 + step // 2, 2)
        low = lax.rem(self.z % 2 + step // 2 + step % 2, 2)
        return (high * 2 + low) * 4 + self.column

    def at(self, base, step):
        return (self.level(step) // 4) * 4 + base % 4


def greet(partners):
    barrier = pltpu.get_barrier_semaphore()
    for partner in partners:
        pl.semaphore_signal(barrier, inc=1, device_id=partner, device_id_type=MESH)
    return lambda: pl.semaphore_wait(barrier, len(partners))


def fold_rows(source, rows, columns):
    blocks = columns // 128
    for block in range(blocks):
        yield block, source[pl.ds(block, rows, stride=blocks), :]


def exchange_kernel(devices, part, out, held, send_sem, recv_sem):
    dp = lax.axis_index("dp")
    core = lax.axis_index("tensor")
    me = dp * 2 + core
    barrier = pltpu.get_barrier_semaphore()

    def partner(step):
        other = lax.rem(me + step, devices)
        return other, (other // 2, lax.rem(other, 2))

    def hail(step, carry):
        pl.semaphore_signal(
            barrier, inc=1, device_id=partner(step)[1], device_id_type=MESH
        )
        return carry

    lax.fori_loop(1, devices, hail, 0)
    held[me] = part[...]
    pl.semaphore_wait(barrier, devices - 1)

    def copy_to(step):
        return pltpu.make_async_remote_copy(
            src_ref=held.at[me],
            dst_ref=held.at[me],
            send_sem=send_sem.at[step],
            recv_sem=recv_sem.at[me],
            device_id=partner(step)[1],
            device_id_type=MESH,
        )

    def start(step, carry):
        copy_to(step).start()
        return carry

    def take(step, carry):
        other = partner(step)[0]
        block = held.at[other]
        pltpu.make_async_copy(block, block, recv_sem.at[other]).wait()
        return carry

    def sent(step, carry):
        copy_to(step).wait_send()
        return carry

    lax.fori_loop(1, devices, start, 0)
    lax.fori_loop(1, devices, take, 0)
    out[...] = jnp.sum(held[...], axis=0)
    lax.fori_loop(1, devices, sent, 0)


def exchange_sums(part, devices):
    return pl.pallas_call(
        functools.partial(exchange_kernel, devices),
        out_shape=jax.ShapeDtypeStruct(part.shape, F32),
        in_specs=[VMEM],
        out_specs=VMEM,
        scratch_shapes=[
            pltpu.VMEM((devices,) + part.shape, F32),
            pltpu.SemaphoreType.DMA((devices,)),
            pltpu.SemaphoreType.DMA((devices,)),
        ],
        compiler_params=pltpu.CompilerParams(collective_id=2, has_side_effects=True),
        name="exchange_sums",
    )(part)


def lane_marks(head, segment_column):
    lane = lax.broadcasted_iota(jnp.int32, (segment_column.shape[0], 128), 1)
    mine = (lane // HD) == head
    same = (lane % HD) == segment_column
    return mine, same


def attend_kernel(segment, query, key, value, out):
    rows = query.shape[0]
    chunk = 256
    for head in (0, 1):
        mine, same = lane_marks(head, segment[...])
        keys = jnp.where(mine, key[...], jnp.where(same, 0.0, -1e30).astype(BF))
        queries = jnp.where(mine, query[...] * BF(HD**-0.5), same.astype(BF))
        values = value[...]
        for start in range(0, rows, chunk):
            scores = contract(queries[start : start + chunk], keys, 1, 1)
            peak = jnp.max(scores, axis=1, keepdims=True)
            raised = jnp.exp(scores - peak)
            scale = 1.0 / jnp.sum(raised, axis=1, keepdims=True)
            attention = (raised * scale).astype(BF)
            result = contract(attention, values, 1, 0).astype(BF)
            span = slice(start, start + chunk)
            if head == 0:
                out[span, :] = result
            else:
                out[span, :] = jnp.where(mine[span], result, out[span, :])


def attend(segment, joint):
    rows, width = joint.shape[0], joint.shape[1] // 3
    pairs = width // 128
    return pl.pallas_call(
        attend_kernel,
        grid=(pairs,),
        out_shape=jax.ShapeDtypeStruct((rows, width), BF),
        in_specs=[
            pl.BlockSpec((rows, 1), lambda pair: (0, 0)),
            pl.BlockSpec((rows, 128), lambda pair: (0, pair)),
            pl.BlockSpec((rows, 128), lambda pair: (0, pairs + pair)),
            pl.BlockSpec((rows, 128), lambda pair: (0, 2 * pairs + pair)),
        ],
        out_specs=pl.BlockSpec((rows, 128), lambda pair: (0, pair)),
        compiler_params=pltpu.CompilerParams(vmem_limit_bytes=40 * MIB),
        name="attend",
    )(segment, joint, joint, joint)


def attend_back_kernel(segment, query, key, value, grad, out, key_sum, value_sum):
    rows = query.shape[0]
    chunk = 256
    scale = HD**-0.5
    for head in (0, 1):
        mine, same = lane_marks(head, segment[...])
        keys = jnp.where(mine, key[...], jnp.where(same, 0.0, -1e30).astype(BF))
        scaled = query[...] * BF(scale)
        queries = jnp.where(mine, scaled, same.astype(BF))
        zero = jnp.zeros_like(scaled)
        pure_queries = jnp.where(mine, scaled, zero)
        pure_keys = jnp.where(mine, key[...], zero)
        grads = jnp.where(mine, grad[...], zero)
        values = value[...]
        for start in range(0, rows, chunk):
            span = slice(start, start + chunk)
            scores = contract(keys, queries[span], 1, 1)
            peak = jnp.max(scores, axis=0, keepdims=True)
            raised = jnp.exp(scores - peak)
            attention = raised * (1.0 / jnp.sum(raised, axis=0, keepdims=True))
            grad_values = contract(attention.astype(BF), grads[span], 1, 0)
            grad_attention = contract(values, grads[span], 1, 1)
            inner = jnp.sum(attention * grad_attention, axis=0, keepdims=True)
            grad_score = (attention * (grad_attention - inner)).astype(BF)
            grad_keys = contract(grad_score, pure_queries[span], 1, 0)
            grad_queries = contract(grad_score, pure_keys, 0, 0) * scale
            if head == 0:
                out[0, span, :] = grad_queries.astype(BF)
            else:
                out[0, span, :] = jnp.where(mine[span], grad_queries.astype(BF), out[0, span, :])
            if head == 0 and start == 0:
                key_sum[...] = grad_keys
                value_sum[...] = grad_values
            else:
                key_sum[...] += grad_keys
                value_sum[...] += grad_values
    out[1] = key_sum[...].astype(BF)
    out[2] = value_sum[...].astype(BF)


def attend_back(segment, joint, grad_attended):
    rows, width = grad_attended.shape
    pairs = width // 128
    return pl.pallas_call(
        attend_back_kernel,
        grid=(pairs,),
        out_shape=jax.ShapeDtypeStruct((3, rows, width), BF),
        in_specs=[
            pl.BlockSpec((rows, 1), lambda pair: (0, 0)),
            pl.BlockSpec((rows, 128), lambda pair: (0, pair)),
            pl.BlockSpec((rows, 128), lambda pair: (0, pairs + pair)),
            pl.BlockSpec((rows, 128), lambda pair: (0, 2 * pairs + pair)),
            pl.BlockSpec((rows, 128), lambda pair: (0, pair)),
        ],
        out_specs=pl.BlockSpec((3, rows, 128), lambda pair: (0, 0, pair)),
        scratch_shapes=[pltpu.VMEM((rows, 128), F32), pltpu.VMEM((rows, 128), F32)],
        compiler_params=pltpu.CompilerParams(vmem_limit_bytes=40 * MIB),
        name="attend_back",
    )(segment, joint, joint, joint, grad_attended)


def forward_kernel(shapes, *refs):
    (
        tokens_hbm,
        patch,
        segment,
        table_f,
        entry_f,
        exit_f,
        expand_f,
        reduce_f,
        align_f,
        norm,
        entry_out,
        exit_out,
        expand_out,
        reduce_out,
        align_out,
        norms_out,
        residual_out,
        normed_one_out,
        joint_out,
        attended_out,
        middle_out,
        normed_two_out,
        act_out,
        slope_out,
        low_out,
        table_slab,
        entry_slab,
        exit_slab,
        expand_slab,
        reduce_slab,
        align_slab,
        table,
        entry,
        exit_low,
        wide,
        narrow,
        tokens,
        norms,
        residual,
        normed_one,
        joint,
        attended,
        feed,
        normed_two,
        act,
        slope,
        low,
        send_sem,
        recv_sem,
        own_sem,
        load_sem,
        save_sem,
        act_sem,
    ) = refs
    width = residual.shape[1]
    rows = residual.shape[0]
    slabs = (table_slab, entry_slab, exit_slab, expand_slab, reduce_slab, align_slab)
    targets = (table, entry, exit_low, wide, narrow, align_out)
    route = Route()
    core = route.core
    arrive = greet(route.partners)
    tokens_copy = pltpu.make_async_copy(tokens_hbm, tokens, load_sem.at[0])
    tokens_copy.start()
    near, far, pair = (route.near, core), (route.far, core), (route.dp, 1 - core)
    peers = [(peer, core) for peer in route.peers]

    def copy_to(source, piece, origin, partner, slot):
        return pltpu.make_async_remote_copy(
            src_ref=source,
            dst_ref=targets[piece].at[origin],
            send_sem=send_sem.at[piece, slot],
            recv_sem=recv_sem.at[piece, origin],
            device_id=partner,
            device_id_type=MESH,
        )

    def wait(piece, origin):
        block = targets[piece].at[origin]
        pltpu.make_async_copy(block, block, recv_sem.at[piece, origin]).wait()

    def pass_on(group, origin, partners, slot):
        for piece in group:
            wait(piece, origin)
            for index, partner in enumerate(partners):
                copy_to(targets[piece].at[origin], piece, origin, partner, slot + index).start()

    def launch(group, wide_part, plane_part):
        for index, partner in enumerate([near, far] + peers + [pair]):
            if plane_part if index < 2 else wide_part:
                for piece in group:
                    copy_to(slabs[piece], piece, route.me, partner, index).start()
        if wide_part:
            for piece in group:
                pltpu.make_async_copy(
                    slabs[piece], targets[piece].at[route.me], own_sem.at[piece]
                ).start()

    def peer_turn(group, step):
        pass_on(group, route.level(step) * 2 + core, (near, far, pair), 6 + (step - 1) * 3)

    def near_turn(group, step):
        pass_on(group, route.at(route.near, step) * 2 + core, (far, pair), 15 + step * 2)

    def far_turn(group, step):
        pass_on(group, route.at(route.far, step) * 2 + core, (pair,), 23 + step * 2)
        pass_on(group, route.at(route.both, step) * 2 + core, (pair,), 24 + step * 2)

    def pair_turn(group, step):
        for base in (route.dp, route.near, route.far, route.both):
            for piece in group:
                wait(piece, route.at(base, step) * 2 + 1 - core)

    def settle(group):
        for piece in group:
            pltpu.make_async_copy(
                slabs[piece], targets[piece].at[route.me], own_sem.at[piece]
            ).wait()

    blocks = width // 128
    whole = TABLE_ROWS - 1
    row_id = lax.broadcasted_iota(jnp.int32, (8, width), 0)
    lane_id = lax.broadcasted_iota(jnp.int32, (NORM_LANES, width), 1)
    from_id = lax.broadcasted_iota(jnp.int32, (NORM_LANES, width), 0)
    parts = width // NORM_LANES
    offset = lax.rem(route.me, parts) * NORM_LANES
    place = (lane_id == from_id + offset).astype(BF)
    spread = contract(norm[...].astype(BF), place, 1, 0)
    tail = jnp.where(row_id == 1, spread, 0.0)
    for block in range(blocks):
        lanes = slice(block * 128, block * 128 + 128)
        table_slab[0:whole, lanes] = table_f[pl.ds(block, whole, stride=blocks), :].astype(BF)
        last = table_f[pl.ds(whole * blocks + block, 1), :]
        mixed = jnp.where(row_id[:, lanes] == 0, last, tail[:, lanes])
        table_slab[whole : whole + 8, lanes] = mixed.astype(BF)
    for block, part in fold_rows(entry_f, *shapes[ENTRY]):
        entry_slab[:, block * 128 : block * 128 + 128] = part.astype(BF)
    for block, part in fold_rows(exit_f, *shapes[EXIT]):
        exit_slab[:, block * 128 : block * 128 + 128] = part.astype(BF)
    arrive()
    early = (TABLE, ENTRY, EXIT)
    last = (ALIGN,)
    launch(early, True, True)
    expand_slab[...] = expand_f[...].astype(BF)
    reduce_slab[...] = reduce_f[...].astype(BF)
    for block, part in fold_rows(align_f, *shapes[ALIGN]):
        align_slab[:, block * 128 : block * 128 + 128] = part.astype(BF)
    late = (EXPAND, REDUCE)

    def turn_of(group, turn):
        if 1 <= turn <= 3:
            peer_turn(group, turn)
        if 1 <= turn <= 4:
            near_turn(group, turn - 1)
        if 2 <= turn <= 5:
            far_turn(group, turn - 2)

    launch(late, True, False)
    for turn in range(1, 6):
        turn_of(early, turn)
    launch(late, False, True)
    for step in range(4):
        pair_turn((TABLE,), step)
    settle((TABLE,))
    tokens_copy.wait()

    for member in range(4):
        total = jnp.zeros((8, width), F32)
        for part in range(parts):
            total = total + table[member * parts + part, whole : whole + 8, :].astype(F32)
        norms[member : member + 1, :] = total[1:2, :]

    def embed(index, carry):
        span = pl.ds(pl.multiple_of(index * 256, 256), 256)
        entries = table.shape[0] * table.shape[1]
        picks = lax.broadcasted_iota(jnp.int32, (256, entries), 1) == patch[span, :]
        found = contract(picks.astype(BF), table[...].reshape(entries, width), 1, 0)
        values = tokens[span, :].astype(F32) + found
        residual[span, :] = values
        normed_one[span, :] = layer_norm(values, norms[0:1, :], norms[1:2, :]).astype(BF)
        return carry

    lax.fori_loop(0, rows // 256, embed, 0)
    for step in range(4):
        pair_turn((ENTRY, EXIT), step)
    settle((ENTRY, EXIT))

    saves = []

    def save(source, target):
        copy = pltpu.make_async_copy(source, target, save_sem.at[len(saves)])
        copy.start()
        saves.append(copy)

    save(entry, entry_out)
    save(exit_low, exit_out)
    save(norms, norms_out)
    save(residual, residual_out)
    save(normed_one, normed_one_out)

    def project(index, carry):
        span = pl.ds(pl.multiple_of(index * 256, 256), 256)
        weight = entry[:, :, span].reshape(width, 256)
        joint[:, span] = contract(normed_one[...], weight, 1, 0).astype(BF)
        return carry

    lax.fori_loop(0, 3 * width // 256, project, 0)
    save(joint, joint_out)

    def service(group, turn):
        @pl.when(turn <= 3)
        def _():
            peer_turn(group, turn)

        @pl.when(turn <= 4)
        def _():
            near_turn(group, turn - 1)

        @pl.when(jnp.logical_and(turn >= 2, turn <= 5))
        def _():
            far_turn(group, turn - 2)

    def attend_pair(index, carry):
        start = pl.multiple_of(index * 128, 128)
        here = pl.ds(start, 128)
        for head in (0, 1):
            mine, same = lane_marks(head, segment[...])
            marks = jnp.where(same, 0.0, -1e30).astype(BF)
            keys = jnp.where(mine, joint[:, pl.ds(start + width, 128)], marks)
            values = joint[:, pl.ds(start + 2 * width, 128)]

            def chunk(step, inner):
                span = pl.ds(pl.multiple_of(step * 256, 256), 256)
                mine, same = lane_marks(head, segment[span, :])
                queries = jnp.where(mine, joint[span, here] * BF(HD**-0.5), same.astype(BF))
                scores = contract(queries, keys, 1, 1)
                peak = jnp.max(scores, axis=1, keepdims=True)
                raised = jnp.exp(scores - peak)
                scale = 1.0 / jnp.sum(raised, axis=1, keepdims=True)
                attention = (raised * scale).astype(BF)
                result = contract(attention, values, 1, 0).astype(BF)
                if head == 0:
                    attended[span, here] = result
                else:
                    attended[span, here] = jnp.where(mine, result, attended[span, here])
                return inner

            lax.fori_loop(0, rows // 256, chunk, 0)

        @pl.when(lax.rem(index, 2) == 0)
        def _():
            service(late, index // 2 + 1)

        return carry

    lax.fori_loop(0, width // 128, attend_pair, 0)
    save(attended, attended_out)
    launch(last, True, True)
    service(late, 4)

    def leave(index, carry):
        span = pl.ds(pl.multiple_of(index * 256, 256), 256)
        weight = exit_low[...].reshape(width, width)
        values = residual[span, :] + contract(attended[span, :], weight, 1, 0)
        feed[span, :] = values
        normed_two[span, :] = layer_norm(values, norms[2:3, :], norms[3:4, :]).astype(BF)
        return carry

    saves[3].wait()
    lax.fori_loop(0, rows // 256, leave, 0)
    def keep(index, carry):
        span = pl.ds(pl.multiple_of(index * 256, 256), 256)
        residual[span, :] = feed[span, :]
        return carry

    lax.fori_loop(0, rows // 256, keep, 0)
    save(residual, middle_out)
    save(normed_two, normed_two_out)

    plane = width // expand_slab.shape[0]

    def feed_level(step, carry):
        level = route.level(step) // 4
        pair_turn(late, step)

        @pl.when(step == 0)
        def _():
            settle(late)

        slot = lax.rem(step, 2)

        @pl.when(step >= 2)
        def _():
            for copy in outgoing(slot, 0):
                copy.wait()

        slabs_here = pl.ds(level * plane, plane)

        def rows_block(index, inner):
            span = pl.ds(pl.multiple_of(index * 256, 256), 256)
            up = wide[slabs_here].reshape(width, width)
            values = contract(normed_two[span, :], up, 1, 1)
            share = 0.5 + 0.5 * lax.erf(values * (0.5**0.5))
            lifted = (values * share).astype(BF)
            act[slot, span, :] = lifted
            bell = jnp.exp(values * values * -0.5) * (0.5 / math.pi) ** 0.5
            slope[slot, span, :] = share + values * bell
            down = narrow[slabs_here].reshape(width, width)
            feed[span, :] += contract(lifted, down, 1, 0)
            return inner

        lax.fori_loop(0, rows // 256, rows_block, 0)
        for copy in outgoing(slot, level):
            copy.start()

        @pl.when(step == 0)
        def _():
            service(late, 5)

        @pl.when(step >= 1)
        def _():
            service(last, step)

        return carry

    def outgoing(number, level):
        hidden = pl.ds(pl.multiple_of(level * width, width), width)
        return (
            pltpu.make_async_copy(act.at[number], act_out.at[:, hidden], act_sem.at[0, number]),
            pltpu.make_async_copy(slope.at[number], slope_out.at[:, hidden], act_sem.at[1, number]),
        )

    lax.fori_loop(0, 4, feed_level, 0)
    save(wide, expand_out)
    save(narrow, reduce_out)
    service(last, 4)
    service(last, 5)

    def close(index, carry):
        span = pl.ds(pl.multiple_of(index * 256, 256), 256)
        low[span, :] = feed[span, :].astype(BF)
        return carry

    lax.fori_loop(0, rows // 256, close, 0)
    save(low, low_out)
    for step in range(4):
        pair_turn(last, step)
    settle(last)
    for number in (0, 1):
        for copy in outgoing(number, 0):
            copy.wait()
    for copy in saves[:3] + saves[4:]:
        copy.wait()

    def sent(slot, carry):
        for piece in range(len(shapes)):
            copy_to(slabs[piece], piece, route.me, near, slot).wait_send()
        return carry

    lax.fori_loop(0, 31, sent, 0)


def gather_forward(shards, norm, tokens, patch, segment, shapes, devices):
    rows, width = tokens.shape
    hidden = shapes[EXPAND][0] * devices

    def shape(dims, kind=BF):
        return jax.ShapeDtypeStruct(dims, kind)

    pieces = (ENTRY, EXIT, EXPAND, REDUCE, ALIGN)
    flat = (rows, width)
    outs = [shape((devices,) + shapes[piece]) for piece in pieces] + [
        shape((8, width), F32),
        shape(flat, F32),
        shape(flat),
        shape((rows, 3 * width)),
        shape(flat),
        shape(flat, F32),
        shape(flat),
        shape((rows, hidden)),
        shape((rows, hidden), F32),
        shape(flat),
    ]
    scratch = (
        [pltpu.VMEM(dims, BF) for dims in shapes]
        + [pltpu.VMEM((devices,) + shapes[piece], BF) for piece in (TABLE, ENTRY, EXIT)]
        + [
            pltpu.VMEM((devices,) + shapes[EXPAND], BF),
            pltpu.VMEM((devices,) + shapes[REDUCE], BF),
            pltpu.VMEM(flat, BF),
            pltpu.VMEM((8, width), F32),
            pltpu.VMEM(flat, F32),
            pltpu.VMEM(flat, BF),
            pltpu.VMEM((rows, 3 * width), BF),
            pltpu.VMEM(flat, BF),
            pltpu.VMEM(flat, F32),
            pltpu.VMEM(flat, BF),
            pltpu.VMEM((2,) + flat, BF),
            pltpu.VMEM((2,) + flat, F32),
            pltpu.VMEM(flat, BF),
            pltpu.SemaphoreType.DMA((6, 31)),
            pltpu.SemaphoreType.DMA((6, devices)),
            pltpu.SemaphoreType.DMA((6,)),
            pltpu.SemaphoreType.DMA((16,)),
            pltpu.SemaphoreType.DMA((12,)),
            pltpu.SemaphoreType.DMA((2, 2)),
        ]
    )
    return pl.pallas_call(
        functools.partial(forward_kernel, shapes),
        out_shape=outs,
        in_specs=[ANY, VMEM, VMEM] + [VMEM] * 7,
        out_specs=[ANY] * len(outs),
        scratch_shapes=scratch,
        compiler_params=pltpu.CompilerParams(
            collective_id=0, has_side_effects=True, vmem_limit_bytes=58 * MIB
        ),
        name="gather_forward",
    )(tokens, patch, segment, *shards, norm)


def norm_back(values, slope, gain):
    center = values - jnp.mean(values, axis=-1, keepdims=True)
    spread = jnp.mean(center * center, axis=-1, keepdims=True)
    scale = lax.rsqrt(spread + LN_EPS)
    unit = center * scale
    scaled = slope * gain
    level = jnp.mean(scaled, axis=-1, keepdims=True)
    tilt = jnp.mean(scaled * unit, axis=-1, keepdims=True)
    return scale * (scaled - level - unit * tilt), slope * unit


def backward_kernel(shapes, *refs):
    count = len(shapes)
    (
        patch_row,
        segment,
        norms,
        cot_out_hbm,
        cot_align_hbm,
        entry_hbm,
        exit_hbm,
        expand_hbm,
        reduce_hbm,
        align_hbm,
        residual_hbm,
        normed_one_hbm,
        joint_hbm,
        attended_hbm,
        middle_hbm,
        normed_two_hbm,
        act_hbm,
        slope_hbm,
        low_hbm,
    ) = refs[:19]
    outs = refs[19 : 19 + count]
    aligned_out, token_out = refs[19 + count : 21 + count]
    refs = refs[21 + count :]
    grads, refs = refs[:count], refs[count:]
    from_pair, refs = refs[:count], refs[count:]
    from_far, refs = refs[:count], refs[count:]
    from_near, refs = refs[:count], refs[count:]
    from_peer, refs = refs[:count], refs[count:]
    (
        wide_a,
        wide_b,
        spare,
        act,
        expand,
        reduce,
        normed_two,
        grad_feed,
        grad_out,
        grad_two,
        slope,
        key_sum,
        value_sum,
        norm_sums,
        send_sem,
        pair_sem,
        far_sem,
        near_sem,
        peer_sem,
        load_sem,
        save_sem,
    ) = refs
    rows, width = grad_out.shape
    align_width = cot_align_hbm.shape[1]
    route = Route()
    core = route.core
    near, far, pair = (route.near, core), (route.far, core), (route.dp, 1 - core)

    def load(source, target, number):
        copy = pltpu.make_async_copy(source, target, load_sem.at[number])
        copy.start()
        return copy

    align_low = wide_a.at[:, pl.ds(0, align_width)]
    cot_align = wide_a.at[:, pl.ds(align_width, align_width)]
    cot_align_copy = load(cot_align_hbm, cot_align, 0)
    align_copy = load(align_hbm, align_low, 1)
    low_copy = load(low_hbm, act, 2)
    cot_out_copy = load(cot_out_hbm, spare, 3)
    normed_two_copy = load(normed_two_hbm, normed_two, 4)
    joint_copy = load(joint_hbm, wide_b, 5)
    arrive = greet(route.partners)

    def level_rows(step):
        return pl.ds(pl.multiple_of((route.level(step) // 4) * width, width), width)

    def chunk_loads(step):
        here = level_rows(step)
        return (
            pltpu.make_async_copy(reduce_hbm.at[here, :], reduce, load_sem.at[6]),
            pltpu.make_async_copy(expand_hbm.at[here, :], expand, load_sem.at[7]),
            pltpu.make_async_copy(slope_hbm.at[:, here], slope, load_sem.at[8]),
        )

    def act_load(step):
        return pltpu.make_async_copy(act_hbm.at[:, level_rows(step)], act, load_sem.at[9])


    def copy_to(source, target, slot, piece, semaphore, partner):
        return pltpu.make_async_remote_copy(
            src_ref=source,
            dst_ref=target,
            send_sem=send_sem.at[piece, slot],
            recv_sem=semaphore,
            device_id=partner,
            device_id_type=MESH,
        )

    def landed(block, semaphore):
        pltpu.make_async_copy(block, block, semaphore).wait()

    def total(piece, dp, sources):
        landed(from_pair[piece].at[dp], pair_sem.at[piece, dp])
        found = grads[piece][dp * 2 + core].astype(F32) + from_pair[piece][dp].astype(F32)
        for block, semaphore, slot in sources:
            landed(block.at[slot], semaphore.at[piece, slot])
            found = found + block[slot].astype(F32)
        return found

    def stage_pair(piece, step):
        for base in (route.far, route.both, route.near, route.dp):
            dp = route.at(base, step)
            copy_to(
                grads[piece].at[dp * 2 + 1 - core],
                from_pair[piece].at[dp],
                dp,
                piece,
                pair_sem.at[piece, dp],
                pair,
            ).start()

    def forward_sum(piece, dp, sources, target, slot, semaphore, partner):
        grads[piece][dp * 2 + core] = total(piece, dp, sources).astype(BF)
        copy_to(
            grads[piece].at[dp * 2 + core], target, slot, piece, semaphore, partner
        ).start()

    def stage_far(piece, step):
        for side, base in enumerate((route.far, route.both)):
            slot = step * 2 + side
            forward_sum(
                piece,
                route.at(base, step),
                (),
                from_far[piece].at[slot],
                16 + slot,
                far_sem.at[piece, slot],
                far,
            )

    def stage_near(piece, step):
        forward_sum(
            piece,
            route.at(route.near, step),
            ((from_far[piece], far_sem, step * 2 + 1),),
            from_near[piece].at[step],
            24 + step,
            near_sem.at[piece, step],
            near,
        )

    def stage_peer(piece, step):
        forward_sum(
            piece,
            route.level(step),
            ((from_far[piece], far_sem, step * 2), (from_near[piece], near_sem, step)),
            from_peer[piece].at[step - 1],
            27 + step,
            peer_sem.at[piece, step - 1],
            (route.level(step), core),
        )

    def stage_own(piece):
        outs[piece][...] = total(
            piece,
            route.dp,
            ((from_far[piece], far_sem, 0), (from_near[piece], near_sem, 0))
            + tuple((from_peer[piece], peer_sem, slot) for slot in range(3)),
        )

    def each(stage, pieces, first=0):
        def body(turn, carry):
            for piece in pieces:
                stage(piece, turn)
            return carry

        lax.fori_loop(first, 4, body, 0)


    norm_sums[...] = jnp.zeros_like(norm_sums)
    cot_align_copy.wait()
    align_copy.wait()
    low_copy.wait()
    cot_out_copy.wait()
    for copy in chunk_loads(3):
        copy.start()

    def head_rows(index, carry):
        span = pl.ds(pl.multiple_of(index * 256, 256), 256)
        keep = segment[span, :] > 0
        slopes = jnp.where(keep, cot_align[span, :], jnp.zeros((256, align_width), BF))
        cot_align[span, :] = slopes
        found = contract(slopes, align_low[...], 1, 1)
        found = found + jnp.where(keep, spare[span, :].astype(F32), 0.0)
        grad_out[span, :] = found
        grad_feed[span, :] = found.astype(BF)
        return carry

    lax.fori_loop(0, rows // 256, head_rows, 0)

    def head_grads(index, carry):
        span = pl.ds(pl.multiple_of(index * 384, 384), 384)
        found = contract(act[:, span], cot_align[...], 0, 0).astype(BF)
        slabs = 384 // shapes[ALIGN][0]
        grads[ALIGN][pl.ds(index * slabs, slabs)] = found.reshape((slabs,) + shapes[ALIGN])
        return carry

    lax.fori_loop(0, width // 384, head_grads, 0)
    arrive()
    each(stage_pair, (ALIGN,))

    def head_out(index, carry):
        span = pl.ds(pl.multiple_of(index * 256, 256), 256)
        result = contract(act[span, :], align_low[...], 1, 0).astype(BF)
        cot_align[span, :] = result
        return carry

    lax.fori_loop(0, rows // 256, head_out, 0)
    aligned_copy = pltpu.make_async_copy(cot_align, aligned_out, save_sem.at[0])
    aligned_copy.start()
    act_load(3).start()
    normed_two_copy.wait()


    def feed_back(turn, carry):
        step = 3 - turn
        for copy in chunk_loads(step):
            copy.wait()

        def rows_block(index, inner):
            span = pl.ds(pl.multiple_of(index * 256, 256), 256)
            found = contract(grad_feed[span, :], reduce[...], 1, 1)
            before = (found * slope[span, :]).astype(BF)
            spare[span, :] = before
            part = contract(before, expand[...], 1, 0)

            @pl.when(turn == 0)
            def _():
                grad_two[span, :] = part

            @pl.when(turn > 0)
            def _():
                grad_two[span, :] += part

            return inner

        lax.fori_loop(0, rows // 256, rows_block, 0)

        @pl.when(turn < 3)
        def _():
            for copy in chunk_loads(step - 1):
                copy.start()

        @pl.when(turn == 3)
        def _():
            pltpu.make_async_copy(middle_hbm, slope, load_sem.at[8]).start()
            pltpu.make_async_copy(exit_hbm, expand, load_sem.at[7]).start()

        act_load(step).wait()
        per = 384 // shapes[EXPAND][0]
        plane = (route.level(step) // 4) * (width // shapes[EXPAND][0])

        def slabs_block(index, inner):
            span = pl.ds(pl.multiple_of(index * 384, 384), 384)
            here = pl.ds(plane + index * per, per)
            found = contract(act[:, span], grad_feed[...], 0, 0).astype(BF)
            grads[REDUCE][here] = found.reshape((per,) + shapes[REDUCE])
            found = contract(spare[:, span], normed_two[...], 0, 0).astype(BF)
            grads[EXPAND][here] = found.reshape((per,) + shapes[EXPAND])
            return inner

        lax.fori_loop(0, width // 384, slabs_block, 0)

        @pl.when(turn < 3)
        def _():
            act_load(step - 1).start()

        for piece in (REDUCE, EXPAND):
            stage_pair(piece, step)

        @pl.when(turn == 0)
        def _():
            each(stage_far, (ALIGN,))

        @pl.when(turn == 1)
        def _():
            each(stage_near, (ALIGN,))

        @pl.when(turn == 2)
        def _():
            each(stage_peer, (ALIGN,), 1)

        feed_turn(turn - 1)
        return carry

    def feed_turn(turn):
        for late, stage in enumerate((stage_far, stage_near, stage_peer)):
            step = 3 - (turn - late)
            lowest = 1 if stage is stage_peer else 0

            @pl.when(jnp.logical_and(step >= lowest, step <= 3))
            def _():
                for piece in (REDUCE, EXPAND):
                    stage(piece, step)

    lax.fori_loop(0, 4, feed_back, 0)
    aligned_copy.wait()
    attended_copy = load(attended_hbm, normed_two, 2)
    entry_copy = load(entry_hbm, wide_a, 1)
    normed_one_copy = load(normed_one_hbm, act, 9)
    pltpu.make_async_copy(middle_hbm, slope, load_sem.at[8]).wait()
    pltpu.make_async_copy(exit_hbm, expand, load_sem.at[7]).wait()


    def leave_back(index, carry):
        span = pl.ds(pl.multiple_of(index * 256, 256), 256)
        slopes = grad_two[span, :]
        through, gains = norm_back(slope[span, :], slopes, norms[2:3, :])
        norm_sums[2:3, :] += jnp.sum(gains, axis=0, keepdims=True)
        norm_sums[3:4, :] += jnp.sum(slopes, axis=0, keepdims=True)
        found = grad_out[span, :] + through
        grad_out[span, :] = found
        branch = found.astype(BF)
        grad_feed[span, :] = branch
        reduce[span, :] = contract(branch, expand[...], 1, 1).astype(BF)
        return carry

    lax.fori_loop(0, rows // 256, leave_back, 0)
    residual_copy = load(residual_hbm, grad_two, 0)
    attended_copy.wait()

    def exit_grads(index, carry):
        span = pl.ds(pl.multiple_of(index * 384, 384), 384)
        found = contract(normed_two[:, span], grad_feed[...], 0, 0).astype(BF)
        slabs = 384 // shapes[EXIT][0]
        grads[EXIT][pl.ds(index * slabs, slabs)] = found.reshape((slabs,) + shapes[EXIT])
        return carry

    lax.fori_loop(0, width // 384, exit_grads, 0)
    each(stage_pair, (EXIT,))
    feed_turn(3)
    joint_copy.wait()


    scale = HD**-0.5
    query_sum = slope.at[pl.ds(0, 128), :]

    def attend_pair(index, carry):
        start = pl.multiple_of(index * 128, 128)
        at_query = pl.ds(start, 128)
        at_key = pl.ds(start + width, 128)
        at_value = pl.ds(start + 2 * width, 128)
        key_sum[...] = jnp.zeros_like(key_sum)
        value_sum[...] = jnp.zeros_like(value_sum)
        query_sum[...] = jnp.zeros_like(query_sum)
        for head in (0, 1):
            mine, same = lane_marks(head, segment[...])
            marks = jnp.where(same, 0.0, -1e30).astype(BF)
            whole_keys = wide_b[:, at_key]
            keys = jnp.where(mine, whole_keys, marks)
            values = wide_b[:, at_value]
            pure = jnp.where(mine, whole_keys, jnp.zeros_like(whole_keys))
            turned = pure.astype(F32).T.astype(BF)

            def chunk(step, inner):
                span = pl.ds(pl.multiple_of(step * 256, 256), 256)
                mine, same = lane_marks(head, segment[span, :])
                scaled = wide_b[span, at_query] * BF(scale)
                queries = jnp.where(mine, scaled, same.astype(BF))
                pure_queries = jnp.where(mine, scaled, jnp.zeros_like(scaled))
                slopes = reduce[span, at_query]
                slopes = jnp.where(mine, slopes, jnp.zeros_like(slopes))
                scores = contract(keys, queries, 1, 1)
                peak = jnp.max(scores, axis=0, keepdims=True)
                raised = jnp.exp(scores - peak)
                attention = raised * (1.0 / jnp.sum(raised, axis=0, keepdims=True))
                value_sum[...] += contract(attention.astype(BF), slopes, 1, 0)
                slope_attention = contract(values, slopes, 1, 1)
                inner_sum = jnp.sum(attention * slope_attention, axis=0, keepdims=True)
                slope_score = (attention * (slope_attention - inner_sum)).astype(BF)
                key_sum[...] += contract(slope_score, pure_queries, 1, 0)
                query_sum[:, span] += contract(turned, slope_score, 1, 0)
                return inner

            lax.fori_loop(0, rows // 256, chunk, 0)
        wide_b[:, at_query] = (query_sum[...].T * scale).astype(BF)
        wide_b[:, at_key] = key_sum[...].astype(BF)
        wide_b[:, at_value] = value_sum[...].astype(BF)

        @pl.when(index == 0)
        def _():
            each(stage_far, (EXIT,))

        @pl.when(index == 1)
        def _():
            feed_turn(4)

        @pl.when(index == 2)
        def _():
            each(stage_near, (EXIT,))

        @pl.when(index == 3)
        def _():
            feed_turn(5)

        @pl.when(index == 4)
        def _():
            each(stage_peer, (EXIT,), 1)

        return carry

    lax.fori_loop(0, width // 128, attend_pair, 0)


    normed_one_copy.wait()
    for block in range(width // 128):
        lanes = slice(block * 128, block * 128 + 128)
        spare[lanes, :] = act[:, lanes].astype(F32).T.astype(BF)

    def entry_block(index, carry):
        half = index // 3
        column = pl.ds(pl.multiple_of(lax.rem(index, 3) * width, width), width)
        line = pl.ds(pl.multiple_of(half * 384, 384), 384)
        found = contract(spare[line, :], wide_b[:, column], 1, 0).astype(BF)
        slabs = 384 // shapes[ENTRY][0]
        grads[ENTRY][pl.ds(half * slabs, slabs), :, column] = found.reshape(
            (slabs, shapes[ENTRY][0], width)
        )
        return carry

    lax.fori_loop(0, 6, entry_block, 0)
    each(stage_pair, (ENTRY,))
    entry_copy.wait()
    residual_copy.wait()

    def enter_back(index, carry):
        span = pl.ds(pl.multiple_of(index * 256, 256), 256)
        slopes = contract(wide_b[span, :], wide_a[...], 1, 1)
        through, gains = norm_back(grad_two[span, :], slopes, norms[0:1, :])
        norm_sums[0:1, :] += jnp.sum(gains, axis=0, keepdims=True)
        norm_sums[1:2, :] += jnp.sum(slopes, axis=0, keepdims=True)
        found = grad_out[span, :] + through
        grad_out[span, :] = found
        grad_feed[span, :] = found.astype(BF)
        return carry

    lax.fori_loop(0, rows // 256, enter_back, 0)
    token_copy = pltpu.make_async_copy(grad_out, token_out, save_sem.at[1])
    token_copy.start()
    each(stage_far, (ENTRY,))

    slabs = 4
    block_rows = slabs * TABLE_SLAB

    def table_block(index, carry):
        entries = lax.broadcasted_iota(jnp.int32, (block_rows, rows), 0) + index * block_rows
        picks = (entries == patch_row[...]).astype(BF)
        found = contract(picks, grad_feed[...], 1, 0).astype(BF)
        grads[TABLE][pl.ds(index * slabs, slabs)] = found.reshape((slabs, TABLE_SLAB, width))
        return carry

    devices = grads[TABLE].shape[0]
    lax.fori_loop(0, devices // slabs, table_block, 0)
    whole = TABLE_ROWS - 1
    row_id = lax.broadcasted_iota(jnp.int32, (8, width), 0)
    for member in range(4):
        line = norm_sums[member : member + 1, :]
        high = line.astype(BF).astype(F32)
        tail = jnp.where(row_id == 1, high, jnp.where(row_id == 2, line - high, 0.0))

        def tuck(index, carry):
            slab = member * (devices // 4) + index
            kept = grads[TABLE][slab, whole : whole + 8, :].astype(F32)
            grads[TABLE][slab, whole : whole + 8, :] = jnp.where(row_id == 0, kept, tail).astype(BF)
            return carry

        lax.fori_loop(0, devices // 4, tuck, 0)
    each(stage_pair, (TABLE,))
    each(stage_near, (ENTRY,))
    each(stage_far, (TABLE,))
    each(stage_peer, (ENTRY,), 1)
    each(stage_near, (TABLE,))
    for piece in (ALIGN, REDUCE, EXPAND, EXIT):
        stage_own(piece)
    each(stage_peer, (TABLE,), 1)
    stage_own(ENTRY)
    stage_own(TABLE)

    def sent(slot, carry):
        for piece in range(count):
            copy_to(
                grads[piece].at[0], from_pair[piece].at[0], slot, piece, pair_sem.at[piece, 0], pair
            ).wait_send()
        return carry

    lax.fori_loop(0, 31, sent, 0)
    token_copy.wait()


def scatter_backward(patch_row, segment, norms, arrays, shapes, devices):
    rows, width = arrays[0].shape
    align_width = arrays[1].shape[1]
    dps = devices // 2
    flat = (rows, width)

    def buffers(slots):
        return [pltpu.VMEM((slots,) + dims, BF) for dims in shapes]

    count = len(shapes)
    scratch = (
        buffers(devices)
        + buffers(dps)
        + buffers(8)
        + buffers(4)
        + buffers(3)
        + [pltpu.VMEM((rows, 3 * width), BF)] * 2
        + [pltpu.VMEM(flat, BF)] * 6
        + [pltpu.VMEM(flat, F32)] * 3
        + [
            pltpu.VMEM((rows, 128), F32),
            pltpu.VMEM((rows, 128), F32),
            pltpu.VMEM((8, width), F32),
            pltpu.SemaphoreType.DMA((count, 31)),
            pltpu.SemaphoreType.DMA((count, dps)),
            pltpu.SemaphoreType.DMA((count, 8)),
            pltpu.SemaphoreType.DMA((count, 4)),
            pltpu.SemaphoreType.DMA((count, 3)),
            pltpu.SemaphoreType.DMA((10,)),
            pltpu.SemaphoreType.DMA((2,)),
        ]
    )
    outs = [jax.ShapeDtypeStruct(dims, F32) for dims in shapes] + [
        jax.ShapeDtypeStruct((rows, align_width), BF),
        jax.ShapeDtypeStruct(flat, F32),
    ]
    return pl.pallas_call(
        functools.partial(backward_kernel, shapes),
        out_shape=outs,
        in_specs=[VMEM] * 3 + [ANY] * len(arrays),
        out_specs=[VMEM] * count + [ANY] * 2,
        scratch_shapes=scratch,
        compiler_params=pltpu.CompilerParams(
            collective_id=1, has_side_effects=True, vmem_limit_bytes=60 * MIB
        ),
        name="scatter_backward",
    )(patch_row, segment, norms, *arrays)


def moments_kernel(decays, *refs):
    count = len(decays)
    sums = refs[7 * count]
    row = lax.broadcasted_iota(jnp.int32, (16, 128), 0)
    found = jnp.zeros((16, 128), F32)
    for member, decay in enumerate(decays):
        weight, gradient, first, second = refs[4 * member : 4 * member + 4]
        new_first_ref, new_second_ref, update_ref = refs[
            4 * count + 3 * member : 4 * count + 3 * member + 3
        ]
        slope = gradient[...]
        new_first = BETA_ONE * first[...] + (1.0 - BETA_ONE) * slope
        new_second = BETA_TWO * second[...] + (1.0 - BETA_TWO) * slope * slope
        update = new_first / (jnp.sqrt(new_second) + ADAM_EPS) + decay * weight[...]
        new_first_ref[...] = new_first
        new_second_ref[...] = new_second
        update_ref[...] = update
        found = jnp.where(row == member, jnp.sum(weight[...] * weight[...]), found)
        found = jnp.where(row == 8 + member, jnp.sum(update * update), found)
    sums[...] = found


def moments(members, decays):
    shapes = [jax.ShapeDtypeStruct(member[0].shape, F32) for member in members]
    outs = [shape for shape in shapes for _ in range(3)]
    flat = [array for member in members for array in member]
    return pl.pallas_call(
        functools.partial(moments_kernel, decays),
        out_shape=outs + [jax.ShapeDtypeStruct((16, 128), F32)],
        in_specs=[VMEM] * len(flat),
        out_specs=[VMEM] * (len(outs) + 1),
        compiler_params=pltpu.CompilerParams(vmem_limit_bytes=40 * MIB),
        name="moments",
    )(*flat)


def step_kernel(count, *refs):
    sums = refs[0]
    for member in range(count):
        weight, update = refs[1 + 2 * member : 3 + 2 * member]
        weight_square = sums[member : member + 1, :]
        update_square = sums[8 + member : 9 + member, :]
        trust = jnp.sqrt(weight_square) / jnp.sqrt(update_square + TINY)
        if weight.shape[1] % 128 == 0:
            trust = jnp.concatenate([trust] * (weight.shape[1] // 128), axis=1)
        else:
            trust = trust[:, : weight.shape[1]]
        refs[1 + 2 * count + member][...] = weight[...] - RATE * trust * update[...]


def take_step(sums, pairs):
    count = len(pairs)
    return pl.pallas_call(
        functools.partial(step_kernel, count),
        out_shape=[jax.ShapeDtypeStruct(weight.shape, F32) for weight, _ in pairs],
        in_specs=[VMEM] * (1 + 2 * count),
        out_specs=[VMEM] * count,
        compiler_params=pltpu.CompilerParams(vmem_limit_bytes=40 * MIB),
        name="take_step",
    )(sums, *[array for pair in pairs for array in pair])


def as_rows(flat):
    if flat.ndim == 2:
        return flat
    lanes = max(size for size in range(1, 129) if flat.shape[0] % size == 0)
    return flat.reshape(-1, lanes)


def local(
    tokens,
    kept_patches,
    clip_lengths,
    clip_device,
    cot_output,
    cot_aligned,
    entry_weight,
    entry_first,
    entry_second,
    exit_weight,
    exit_first,
    exit_second,
    align_weight,
    align_first,
    align_second,
    expand_weight,
    expand_first,
    expand_second,
    reduce_weight,
    reduce_first,
    reduce_second,
    position_table,
    position_first,
    position_second,
    norm_params,
    norm_first,
    norm_second,
):
    rows, width = tokens.shape
    align_width = cot_aligned.shape[1]
    axes = ("dp", "tensor")
    pair = lax.axis_size("tensor")
    devices = lax.axis_size("dp") * pair
    hidden = expand_weight.shape[0] * devices
    positions = position_table.shape[0] * devices // width
    routed = devices == 2 * ROUTED_DP and pair == 2
    device = lax.axis_index("dp") * pair + lax.axis_index("tensor")
    segment, valid_rows = row_layout(clip_lengths, clip_device, device, rows)
    segment_column = segment[:, None]
    valid_column = valid_rows[:, None]
    shapes = (
        (TABLE_SLAB, width),
        (width // devices, 3 * width),
        (width // devices, width),
        (hidden // devices, width),
        (hidden // devices, width),
        (width // devices, align_width),
    )
    wholes = (
        (positions, width),
        (width, 3 * width),
        (width, width),
        (hidden, width),
        (hidden, width),
        (width, align_width),
    )
    masters = (position_table, entry_weight, exit_weight, expand_weight, reduce_weight, align_weight)
    if routed:
        patch = kept_patches + (kept_patches // TABLE_ROWS) * (TABLE_SLAB - TABLE_ROWS)
        found = gather_forward(
            [as_rows(master) for master in masters],
            norm_params.reshape(1, -1),
            tokens,
            patch[:, None],
            segment_column,
            shapes,
            devices,
        )
        lows = [block.reshape(-1, block.shape[2]) for block in found[:5]]
        entry_low, exit_low, expand_low, reduce_low, align_low = lows
        norm_low = found[5]
        residual, normed_one, joint_low, attended, middle = found[6:11]
        normed_two, hidden_act, hidden_slope, out_low = found[11:]
    else:
        lows = [
            lax.all_gather(master.astype(BF).reshape(-1), axes, axis=0, tiled=True).reshape(whole)
            for master, whole in zip(masters, wholes)
        ]
        norm_low = lax.all_gather(norm_params.astype(BF), axes, axis=0, tiled=True).reshape(4, width)
        patch = kept_patches
        table_low, entry_low, exit_low, expand_low, reduce_low, align_low = lows
        norm_low = norm_low.astype(F32)
        residual = tokens.astype(F32) + jnp.take(table_low, patch, axis=0).astype(F32)
        normed_one = layer_norm(residual, norm_low[0], norm_low[1]).astype(BF)
        joint_low = contract(normed_one, entry_low, 1, 0).astype(BF)
        attended = attend(segment_column, joint_low)
        middle = residual + contract(attended, exit_low, 1, 0)
        normed_two = layer_norm(middle, norm_low[2], norm_low[3]).astype(BF)
        hidden_pre = contract(normed_two, expand_low, 1, 1)
        share = 0.5 + 0.5 * lax.erf(hidden_pre * 0.5**0.5)
        hidden_act = (hidden_pre * share).astype(BF)
        hidden_slope = share + hidden_pre * jnp.exp(-0.5 * hidden_pre * hidden_pre) * (0.5 / math.pi) ** 0.5
        out_low = (middle + contract(hidden_act, reduce_low, 1, 0)).astype(BF)
    if routed:
        arrays = (cot_output, cot_aligned) + tuple(lows) + tuple(found[6:])
        results = scatter_backward(
            patch[None, :],
            segment_column,
            norm_low,
            arrays,
            shapes,
            devices,
        )
        align_rows, token_grad = results[6:]
        table_sum = results[TABLE]
        norm_row = table_sum[TABLE_ROWS] + table_sum[TABLE_ROWS + 1]
        norm_sum = lax.dynamic_slice_in_dim(
            norm_row, (device % (width // NORM_LANES)) * NORM_LANES, NORM_LANES
        )
        summed = [table_sum[:TABLE_ROWS]] + list(results[1:6])
    else:
        align_rows = contract(out_low, align_low, 1, 0).astype(BF)
        cot_align_valid = jnp.where(valid_column, cot_aligned, jnp.zeros_like(cot_aligned))
        grad_align = contract(out_low, cot_align_valid, 0, 0)
        grad_out = jnp.where(valid_column, cot_output.astype(F32), 0.0) + contract(
            cot_align_valid, align_low, 1, 1
        )
        grad_feed = grad_out.astype(BF)
        grad_act = contract(grad_feed, reduce_low, 1, 1)
        grad_pre = (grad_act * hidden_slope).astype(BF)
        grad_reduce = contract(hidden_act, grad_feed, 0, 0)
        grad_expand = contract(grad_pre, normed_two, 0, 0)
        grad_two = contract(grad_pre, expand_low, 1, 0)
        through, gains = norm_back(middle, grad_two, norm_low[2])
        grad_middle = grad_out + through
        grad_branch = grad_middle.astype(BF)
        grad_exit = contract(attended, grad_branch, 0, 0)
        grad_attended = contract(grad_branch, exit_low, 1, 1).astype(BF)
        grad_parts = attend_back(segment_column, joint_low, grad_attended)
        grad_joint = jnp.concatenate([grad_parts[0], grad_parts[1], grad_parts[2]], axis=1)
        grad_entry = contract(normed_one, grad_joint, 0, 0)
        grad_one = contract(grad_joint, entry_low, 1, 1)
        through_one, gains_one = norm_back(residual, grad_one, norm_low[0])
        token_grad = grad_middle + through_one
        places = jnp.arange(positions, dtype=jnp.int32)
        picks = (patch[:, None] == places[None, :]).astype(BF)
        grad_table = contract(picks, token_grad.astype(BF), 0, 0)
        grad_norms = jnp.concatenate(
            [jnp.sum(part, axis=0) for part in (gains_one, grad_one, gains, grad_two)]
        )
        grads = (grad_table, grad_entry, grad_exit, grad_expand, grad_reduce, grad_align)
        summed = [
            lax.psum_scatter(grad.reshape(-1), axes, scatter_dimension=0, tiled=True)
            for grad in grads
        ]
        norm_sum = lax.psum_scatter(grad_norms, axes, scatter_dimension=0, tiled=True)
    block_out = jnp.where(valid_column, out_low, jnp.zeros_like(out_low))
    aligned = jnp.where(valid_column, align_rows, jnp.zeros_like(align_rows))

    def summed_like(master, index):
        return summed[index].reshape(master.shape)

    members = (
        (entry_weight, summed_like(entry_weight, ENTRY), entry_first, entry_second),
        (exit_weight, summed_like(exit_weight, EXIT), exit_first, exit_second),
        (align_weight, summed_like(align_weight, ALIGN), align_first, align_second),
        (expand_weight, summed_like(expand_weight, EXPAND), expand_first, expand_second),
        (reduce_weight, summed_like(reduce_weight, REDUCE), reduce_first, reduce_second),
        (position_table, summed_like(position_table, TABLE), position_first, position_second),
        (norm_params, norm_sum, norm_first, norm_second),
    )
    decays = (DECAY, DECAY, DECAY, DECAY, DECAY, DECAY, 0.0)
    members = [tuple(as_rows(array) for array in member) for member in members]
    found = moments(members, decays)
    sums = found[-1]
    sums = exchange_sums(sums, devices) if routed else lax.psum(sums, axes)
    stepped = take_step(
        sums, [(members[member][0], found[3 * member + 2]) for member in range(len(members))]
    )
    weight_squares, update_squares = sums[0:7, 0], sums[8:15, 0]
    trust = jnp.sqrt(weight_squares) / jnp.sqrt(update_squares + TINY)
    outputs = [block_out, aligned, token_grad]
    originals = (
        entry_weight,
        exit_weight,
        align_weight,
        expand_weight,
        reduce_weight,
        position_table,
        norm_params,
    )
    for member, original in enumerate(originals):
        for array in (found[3 * member], found[3 * member + 1], stepped[member]):
            outputs.append(array.reshape(original.shape))
    outputs.append(jnp.stack((trust, jnp.sqrt(weight_squares), jnp.sqrt(update_squares))))
    return tuple(outputs)


def solution(mesh):
    both = ("dp", "tensor")
    rows, flat, whole = P(both, None), P(both), P()
    weight_specs = (flat,) * 9 + (rows,) * 6 + (flat,) * 6
    placed = (rows, flat, whole, whole, rows, rows) + weight_specs
    return jax.shard_map(
        local,
        mesh=mesh,
        in_specs=placed,
        out_specs=(rows, rows, rows) + weight_specs + (whole,),
        check_vma=False,
    )
```

```python
import functools
import math

import jax
import jax.numpy as jnp
from jax import lax
from jax.experimental import pallas as pl
from jax.experimental.pallas import tpu as pltpu
from jax.sharding import PartitionSpec as P

H = 12
HD = 64
LN_EPS = 1e-06
RATE = 0.5
BETA_ONE = 0.9
BETA_TWO = 0.98
ADAM_EPS = 1e-06
DECAY = 0.05
TINY = 1e-06
BF = jnp.bfloat16
F32 = jnp.float32
MESH = pl.DeviceIdType.MESH
ANY = pl.BlockSpec(memory_space=pl.ANY)
VMEM = pl.BlockSpec(memory_space=pltpu.VMEM)
MIB = 1 << 20

TABLE, ENTRY, EXIT, EXPAND, REDUCE, ALIGN = range(6)
MEMBERS = (ENTRY, EXIT, ALIGN, EXPAND, REDUCE, TABLE)
TABLE_ROWS = 49
TABLE_SLAB = 56
NORM_LANES = 96
ROUTED_DP = 16


def contract(left, right, left_dim, right_dim):
    return lax.dot_general(
        left, right, (((left_dim,), (right_dim,)), ((), ())), preferred_element_type=F32
    )


def layer_norm(values, gain, shift):
    center = values - jnp.mean(values, axis=-1, keepdims=True)
    spread = jnp.mean(center * center, axis=-1, keepdims=True)
    return center * lax.rsqrt(spread + LN_EPS) * gain + shift


def row_layout(clip_lengths, clip_device, device, row_count):
    mine = clip_device == device
    own_length = jnp.where(mine, clip_lengths, 0)
    starts = jnp.cumsum(own_length) - own_length
    filled = jnp.sum(own_length)
    positions = jnp.arange(row_count, dtype=jnp.int32)
    begun = mine[None, :] & (starts[None, :] <= positions[:, None])
    segment = jnp.sum(begun.astype(jnp.int32), axis=1)
    valid_rows = positions < filled
    return (jnp.where(valid_rows, segment, 0), valid_rows)


class Route:
    def __init__(self):
        dp = lax.axis_index("dp")
        core = lax.axis_index("tensor")
        z, y, x = dp // 4, (dp // 2) % 2, dp % 2
        across_y = dp + 2 - 4 * y
        across_x = dp + 1 - 2 * x
        self.dp, self.core, self.me = dp, core, dp * 2 + core
        self.z, self.column = z, y * 2 + x
        self.near = across_y * (1 - core) + across_x * core
        self.far = across_x * (1 - core) + across_y * core
        self.both = self.near + self.far - dp
        levels = [z + 1 - 2 * (z % 2), 3 - z, (z + 2) % 4]
        self.peers = [level * 4 + y * 2 + x for level in levels]
        self.partners = [(peer, core) for peer in self.peers] + [
            (self.near, core),
            (self.far, core),
            (dp, 1 - core),
        ]
        self.corner = (self.both, core)

    def level(self, step):
        high = lax.rem(self.z // 2 + step // 2, 2)
        low = lax.rem(self.z % 2 + step // 2 + step % 2, 2)
        return (high * 2 + low) * 4 + self.column

    def at(self, base, step):
        return (self.level(step) // 4) * 4 + base % 4


def greet(partners):
    barrier = pltpu.get_barrier_semaphore()
    for partner in partners:
        pl.semaphore_signal(barrier, inc=1, device_id=partner, device_id_type=MESH)
    return lambda: pl.semaphore_wait(barrier, len(partners))


def fold_rows(source, rows, columns):
    blocks = columns // 128
    for block in range(blocks):
        yield block, source[pl.ds(block, rows, stride=blocks), :]


def lane_marks(head, segment_column):
    lane = lax.broadcasted_iota(jnp.int32, (segment_column.shape[0], 128), 1)
    mine = lax.shift_right_logical(lane, 6) == head
    same = jnp.bitwise_and(lane, HD - 1) == segment_column
    return mine, same


def attend_kernel(segment, query, key, value, out):
    rows = query.shape[0]
    chunk = 256
    for head in (0, 1):
        mine, same = lane_marks(head, segment[...])
        keys = jnp.where(mine, key[...], jnp.where(same, 0.0, -1e30).astype(BF))
        queries = jnp.where(mine, query[...] * BF(HD**-0.5), same.astype(BF))
        values = value[...]
        for start in range(0, rows, chunk):
            scores = contract(queries[start : start + chunk], keys, 1, 1)
            peak = jnp.max(scores, axis=1, keepdims=True)
            raised = jnp.exp(scores - peak)
            scale = 1.0 / jnp.sum(raised, axis=1, keepdims=True)
            attention = (raised * scale).astype(BF)
            result = contract(attention, values, 1, 0).astype(BF)
            span = slice(start, start + chunk)
            if head == 0:
                out[span, :] = result
            else:
                out[span, :] = jnp.where(mine[span], result, out[span, :])


def attend(segment, joint):
    rows, width = joint.shape[0], joint.shape[1] // 3
    pairs = width // 128
    return pl.pallas_call(
        attend_kernel,
        grid=(pairs,),
        out_shape=jax.ShapeDtypeStruct((rows, width), BF),
        in_specs=[
            pl.BlockSpec((rows, 1), lambda pair: (0, 0)),
            pl.BlockSpec((rows, 128), lambda pair: (0, pair)),
            pl.BlockSpec((rows, 128), lambda pair: (0, pairs + pair)),
            pl.BlockSpec((rows, 128), lambda pair: (0, 2 * pairs + pair)),
        ],
        out_specs=pl.BlockSpec((rows, 128), lambda pair: (0, pair)),
        compiler_params=pltpu.CompilerParams(vmem_limit_bytes=40 * MIB),
        name="attend",
    )(segment, joint, joint, joint)


def attend_back_kernel(segment, query, key, value, grad, out, key_sum, value_sum):
    rows = query.shape[0]
    chunk = 256
    scale = HD**-0.5
    for head in (0, 1):
        mine, same = lane_marks(head, segment[...])
        keys = jnp.where(mine, key[...], jnp.where(same, 0.0, -1e30).astype(BF))
        scaled = query[...] * BF(scale)
        queries = jnp.where(mine, scaled, same.astype(BF))
        zero = jnp.zeros_like(scaled)
        pure_queries = jnp.where(mine, scaled, zero)
        pure_keys = jnp.where(mine, key[...], zero)
        grads = jnp.where(mine, grad[...], zero)
        values = value[...]
        for start in range(0, rows, chunk):
            span = slice(start, start + chunk)
            scores = contract(keys, queries[span], 1, 1)
            peak = jnp.max(scores, axis=0, keepdims=True)
            raised = jnp.exp(scores - peak)
            attention = raised * (1.0 / jnp.sum(raised, axis=0, keepdims=True))
            grad_values = contract(attention.astype(BF), grads[span], 1, 0)
            grad_attention = contract(values, grads[span], 1, 1)
            inner = jnp.sum(attention * grad_attention, axis=0, keepdims=True)
            grad_score = (attention * (grad_attention - inner)).astype(BF)
            grad_keys = contract(grad_score, pure_queries[span], 1, 0)
            grad_queries = contract(grad_score, pure_keys, 0, 0) * scale
            if head == 0:
                out[0, span, :] = grad_queries.astype(BF)
            else:
                out[0, span, :] = jnp.where(mine[span], grad_queries.astype(BF), out[0, span, :])
            if head == 0 and start == 0:
                key_sum[...] = grad_keys
                value_sum[...] = grad_values
            else:
                key_sum[...] += grad_keys
                value_sum[...] += grad_values
    out[1] = key_sum[...].astype(BF)
    out[2] = value_sum[...].astype(BF)


def attend_back(segment, joint, grad_attended):
    rows, width = grad_attended.shape
    pairs = width // 128
    return pl.pallas_call(
        attend_back_kernel,
        grid=(pairs,),
        out_shape=jax.ShapeDtypeStruct((3, rows, width), BF),
        in_specs=[
            pl.BlockSpec((rows, 1), lambda pair: (0, 0)),
            pl.BlockSpec((rows, 128), lambda pair: (0, pair)),
            pl.BlockSpec((rows, 128), lambda pair: (0, pairs + pair)),
            pl.BlockSpec((rows, 128), lambda pair: (0, 2 * pairs + pair)),
            pl.BlockSpec((rows, 128), lambda pair: (0, pair)),
        ],
        out_specs=pl.BlockSpec((3, rows, 128), lambda pair: (0, 0, pair)),
        scratch_shapes=[pltpu.VMEM((rows, 128), F32), pltpu.VMEM((rows, 128), F32)],
        compiler_params=pltpu.CompilerParams(vmem_limit_bytes=40 * MIB),
        name="attend_back",
    )(segment, joint, joint, joint, grad_attended)


def segments(lengths, owners, device, rows):
    count = lengths.shape[1]
    mine = owners == device
    own = jnp.broadcast_to(jnp.where(mine, lengths, 0).astype(F32), (8, count))
    before = lax.broadcasted_iota(jnp.int32, (count, count), 0)
    after = lax.broadcasted_iota(jnp.int32, (count, count), 1)
    starts = lax.dot_general(
        own,
        (before < after).astype(F32),
        (((1,), (0,)), ((), ())),
        precision=lax.Precision.HIGHEST,
        preferred_element_type=F32,
    )[0:1, :]
    filled = jnp.sum(own[0:1, :], axis=1, keepdims=True)
    place = lax.broadcasted_iota(jnp.int32, (rows, count), 0).astype(F32)
    begun = jnp.where(jnp.logical_and(mine, starts <= place), 1.0, 0.0)
    number = jnp.sum(begun, axis=1, keepdims=True)
    return jnp.where(place[:, 0:1] < filled, number, 0.0).astype(jnp.int32)


def slab_places(patch):
    return patch + lax.shift_right_logical(patch * 1338, 16) * (TABLE_SLAB - TABLE_ROWS)


def forward_kernel(shapes, *refs):
    (
        tokens_hbm,
        kept,
        lengths,
        owners,
        table_f,
        entry_f,
        exit_f,
        expand_f,
        reduce_f,
        align_f,
        norm,
        entry_out,
        exit_out,
        expand_out,
        reduce_out,
        align_out,
        norms_out,
        residual_out,
        normed_one_out,
        joint_out,
        attended_out,
        middle_out,
        normed_two_out,
        act_out,
        slope_out,
        low_out,
        totals_out,
        segment_out,
        table_slab,
        entry_slab,
        exit_slab,
        expand_slab,
        reduce_slab,
        align_slab,
        table,
        entry,
        exit_low,
        wide,
        narrow,
        tokens,
        norms,
        residual,
        normed_one,
        joint,
        attended,
        feed,
        normed_two,
        act,
        slope,
        low,
        totals,
        patch,
        segment,
        send_sem,
        recv_sem,
        own_sem,
        load_sem,
        save_sem,
        act_sem,
    ) = refs
    width = residual.shape[1]
    rows = residual.shape[0]
    slabs = (table_slab, entry_slab, exit_slab, expand_slab, reduce_slab, align_slab)
    targets = (table, entry, exit_low, wide, narrow, align_out)
    route = Route()
    core = route.core
    arrive = greet(route.partners)
    tokens_copy = pltpu.make_async_copy(tokens_hbm, tokens, load_sem.at[0])
    tokens_copy.start()
    near, far, pair = (route.near, core), (route.far, core), (route.dp, 1 - core)
    peers = [(peer, core) for peer in route.peers]

    def copy_to(source, piece, origin, partner, slot):
        return pltpu.make_async_remote_copy(
            src_ref=source,
            dst_ref=targets[piece].at[origin],
            send_sem=send_sem.at[piece, slot],
            recv_sem=recv_sem.at[piece, origin],
            device_id=partner,
            device_id_type=MESH,
        )

    def wait(piece, origin):
        block = targets[piece].at[origin]
        pltpu.make_async_copy(block, block, recv_sem.at[piece, origin]).wait()

    def pass_on(group, origin, partners, slot):
        for piece in group:
            wait(piece, origin)
            for index, partner in enumerate(partners):
                copy_to(targets[piece].at[origin], piece, origin, partner, slot + index).start()

    def launch(group, wide_part, plane_part):
        for index, partner in enumerate([near, far] + peers + [pair]):
            if plane_part if index < 2 else wide_part:
                for piece in group:
                    copy_to(slabs[piece], piece, route.me, partner, index).start()
        if wide_part:
            for piece in group:
                pltpu.make_async_copy(
                    slabs[piece], targets[piece].at[route.me], own_sem.at[piece]
                ).start()

    def peer_turn(group, step):
        pass_on(group, route.level(step) * 2 + core, (near, far, pair), 6 + (step - 1) * 3)

    def near_turn(group, step):
        pass_on(group, route.at(route.near, step) * 2 + core, (far, pair), 15 + step * 2)

    def far_turn(group, step):
        pass_on(group, route.at(route.far, step) * 2 + core, (pair,), 23 + step * 2)
        pass_on(group, route.at(route.both, step) * 2 + core, (pair,), 24 + step * 2)

    def pair_turn(group, step):
        for base in (route.dp, route.near, route.far, route.both):
            for piece in group:
                wait(piece, route.at(base, step) * 2 + 1 - core)

    def settle(group):
        for piece in group:
            pltpu.make_async_copy(
                slabs[piece], targets[piece].at[route.me], own_sem.at[piece]
            ).wait()

    totals[...] = jnp.zeros_like(totals)
    segment[...] = segments(lengths[...], owners[...], route.me, rows)
    lifted = jnp.broadcast_to(slab_places(kept[...]).astype(F32), (8, rows))
    patch[...] = lifted.T[:, 0:1].astype(jnp.int32)
    blocks = width // 128
    whole = TABLE_ROWS - 1
    row_id = lax.broadcasted_iota(jnp.int32, (8, width), 0)
    lane_id = lax.broadcasted_iota(jnp.int32, (NORM_LANES, width), 1)
    from_id = lax.broadcasted_iota(jnp.int32, (NORM_LANES, width), 0)
    parts = width // NORM_LANES
    offset = lax.rem(route.me, parts) * NORM_LANES
    place = (lane_id == from_id + offset).astype(BF)
    spread = contract(norm[...].astype(BF), place, 1, 0)
    tail = jnp.where(row_id == 1, spread, 0.0)
    for block in range(blocks):
        lanes = slice(block * 128, block * 128 + 128)
        table_slab[0:whole, lanes] = table_f[pl.ds(block, whole, stride=blocks), :].astype(BF)
        last = table_f[pl.ds(whole * blocks + block, 1), :]
        mixed = jnp.where(row_id[:, lanes] == 0, last, tail[:, lanes])
        table_slab[whole : whole + 8, lanes] = mixed.astype(BF)
    for block, part in fold_rows(entry_f, *shapes[ENTRY]):
        entry_slab[:, block * 128 : block * 128 + 128] = part.astype(BF)
    for block, part in fold_rows(exit_f, *shapes[EXIT]):
        exit_slab[:, block * 128 : block * 128 + 128] = part.astype(BF)
    arrive()
    early = (TABLE, ENTRY, EXIT)
    last = (ALIGN,)
    launch(early, True, True)
    expand_slab[...] = expand_f[...].astype(BF)
    reduce_slab[...] = reduce_f[...].astype(BF)
    for block, part in fold_rows(align_f, *shapes[ALIGN]):
        align_slab[:, block * 128 : block * 128 + 128] = part.astype(BF)
    late = (EXPAND, REDUCE)

    def turn_of(group, turn):
        if 1 <= turn <= 3:
            peer_turn(group, turn)
        if 1 <= turn <= 4:
            near_turn(group, turn - 1)
        if 2 <= turn <= 5:
            far_turn(group, turn - 2)

    launch(late, True, False)
    for turn in range(1, 6):
        turn_of(early, turn)
    launch(late, False, True)
    for step in range(4):
        pair_turn((TABLE,), step)
    settle((TABLE,))
    tokens_copy.wait()

    for member in range(4):
        total = jnp.zeros((8, width), F32)
        for part in range(parts):
            total = total + table[member * parts + part, whole : whole + 8, :].astype(F32)
        norms[member : member + 1, :] = total[1:2, :]

    def embed(index, carry):
        span = pl.ds(pl.multiple_of(index * 256, 256), 256)
        entries = table.shape[0] * table.shape[1]
        picks = lax.broadcasted_iota(jnp.int32, (256, entries), 1) == patch[span, :]
        found = contract(picks.astype(BF), table[...].reshape(entries, width), 1, 0)
        values = tokens[span, :].astype(F32) + found
        residual[span, :] = values
        normed_one[span, :] = layer_norm(values, norms[0:1, :], norms[1:2, :]).astype(BF)
        return carry

    lax.fori_loop(0, rows // 256, embed, 0)
    for step in range(4):
        pair_turn((ENTRY, EXIT), step)
    settle((ENTRY, EXIT))

    saves = []

    def save(source, target):
        copy = pltpu.make_async_copy(source, target, save_sem.at[len(saves)])
        copy.start()
        saves.append(copy)

    save(entry, entry_out)
    save(exit_low, exit_out)
    save(norms, norms_out)
    save(segment, segment_out)
    save(residual, residual_out)
    save(normed_one, normed_one_out)

    def project(index, carry):
        span = pl.ds(pl.multiple_of(index * 256, 256), 256)
        weight = entry[:, :, span].reshape(width, 256)
        joint[:, span] = contract(normed_one[...], weight, 1, 0).astype(BF)
        return carry

    lax.fori_loop(0, 3 * width // 256, project, 0)
    save(joint, joint_out)

    def service(group, turn):
        @pl.when(turn <= 3)
        def _():
            peer_turn(group, turn)

        @pl.when(turn <= 4)
        def _():
            near_turn(group, turn - 1)

        @pl.when(jnp.logical_and(turn >= 2, turn <= 5))
        def _():
            far_turn(group, turn - 2)

    def attend_pair(index, carry):
        start = pl.multiple_of(index * 128, 128)
        here = pl.ds(start, 128)
        whole_keys = joint[:, pl.ds(start + width, 128)]
        values = joint[:, pl.ds(start + 2 * width, 128)]
        keys = []
        for head in (0, 1):
            mine, same = lane_marks(head, segment[...])
            keys.append(jnp.where(mine, whole_keys, jnp.where(same, 0.0, -1e30).astype(BF)))

        def chunk(step, inner):
            span = pl.ds(pl.multiple_of(step * 256, 256), 256)
            lane = lax.broadcasted_iota(jnp.int32, (256, 128), 1)
            scaled = joint[span, here] * BF(HD**-0.5)
            found = []
            logs = totals[span, :]
            for head in (0, 1):
                mine, same = lane_marks(head, segment[span, :])
                queries = jnp.where(mine, scaled, same.astype(BF))
                scores = contract(queries, keys[head], 1, 1)
                peak = jnp.max(scores, axis=1, keepdims=True)
                raised = jnp.exp(scores - peak)
                total = jnp.sum(raised, axis=1, keepdims=True)
                attention = (raised * (1.0 / total)).astype(BF)
                found.append(contract(attention, values, 1, 0))
                logs = jnp.where(lane == index * 2 + head, peak + jnp.log(total), logs)
            totals[span, :] = logs
            attended[span, here] = jnp.where(lane < HD, found[0], found[1]).astype(BF)
            return inner

        lax.fori_loop(0, rows // 256, chunk, 0)

        @pl.when(lax.rem(index, 2) == 0)
        def _():
            service(late, index // 2 + 1)

        return carry

    lax.fori_loop(0, width // 128, attend_pair, 0)
    save(attended, attended_out)
    save(totals, totals_out)
    launch(last, True, True)
    service(late, 4)

    def leave(index, carry):
        span = pl.ds(pl.multiple_of(index * 256, 256), 256)
        weight = exit_low[...].reshape(width, width)
        values = residual[span, :] + contract(attended[span, :], weight, 1, 0)
        feed[span, :] = values
        normed_two[span, :] = layer_norm(values, norms[2:3, :], norms[3:4, :]).astype(BF)
        return carry

    saves[4].wait()
    lax.fori_loop(0, rows // 256, leave, 0)
    def keep(index, carry):
        span = pl.ds(pl.multiple_of(index * 256, 256), 256)
        residual[span, :] = feed[span, :]
        return carry

    lax.fori_loop(0, rows // 256, keep, 0)
    save(residual, middle_out)
    save(normed_two, normed_two_out)

    plane = width // expand_slab.shape[0]

    def feed_level(step, carry):
        level = route.level(step) // 4
        pair_turn(late, step)

        @pl.when(step == 0)
        def _():
            settle(late)

        slot = lax.rem(step, 2)

        @pl.when(step >= 2)
        def _():
            for copy in outgoing(slot, 0):
                copy.wait()

        slabs_here = pl.ds(level * plane, plane)

        def rows_block(index, inner):
            span = pl.ds(pl.multiple_of(index * 256, 256), 256)
            up = wide[slabs_here].reshape(width, width)
            values = contract(normed_two[span, :], up, 1, 1)
            share = 0.5 + 0.5 * lax.erf(values * (0.5**0.5))
            lifted = (values * share).astype(BF)
            act[slot, span, :] = lifted
            bell = jnp.exp(values * values * -0.5) * (0.5 / math.pi) ** 0.5
            slope[slot, span, :] = share + values * bell
            down = narrow[slabs_here].reshape(width, width)
            feed[span, :] += contract(lifted, down, 1, 0)
            return inner

        lax.fori_loop(0, rows // 256, rows_block, 0)
        for copy in outgoing(slot, level):
            copy.start()

        @pl.when(step == 0)
        def _():
            service(late, 5)

        @pl.when(step >= 1)
        def _():
            service(last, step)

        return carry

    def outgoing(number, level):
        hidden = pl.ds(pl.multiple_of(level * width, width), width)
        return (
            pltpu.make_async_copy(act.at[number], act_out.at[:, hidden], act_sem.at[0, number]),
            pltpu.make_async_copy(slope.at[number], slope_out.at[:, hidden], act_sem.at[1, number]),
        )

    lax.fori_loop(0, 4, feed_level, 0)
    save(wide, expand_out)
    save(narrow, reduce_out)
    service(last, 4)
    service(last, 5)

    def close(index, carry):
        span = pl.ds(pl.multiple_of(index * 256, 256), 256)
        low[span, :] = feed[span, :].astype(BF)
        return carry

    lax.fori_loop(0, rows // 256, close, 0)
    save(low, low_out)
    for step in range(4):
        pair_turn(last, step)
    settle(last)
    for number in (0, 1):
        for copy in outgoing(number, 0):
            copy.wait()
    for copy in saves[:4] + saves[5:]:
        copy.wait()

    def sent(slot, carry):
        for piece in range(len(shapes)):
            copy_to(slabs[piece], piece, route.me, near, slot).wait_send()
        return carry

    lax.fori_loop(0, 31, sent, 0)


def gather_forward(shards, norm, tokens, kept, lengths, owners, shapes, devices):
    rows, width = tokens.shape
    hidden = shapes[EXPAND][0] * devices

    def shape(dims, kind=BF):
        return jax.ShapeDtypeStruct(dims, kind)

    pieces = (ENTRY, EXIT, EXPAND, REDUCE, ALIGN)
    flat = (rows, width)
    outs = [shape((devices,) + shapes[piece]) for piece in pieces] + [
        shape((8, width), F32),
        shape(flat, F32),
        shape(flat),
        shape((rows, 3 * width)),
        shape(flat),
        shape(flat, F32),
        shape(flat),
        shape((rows, hidden)),
        shape((rows, hidden), F32),
        shape(flat),
        shape((rows, 128), F32),
        shape((rows, 1), jnp.int32),
    ]
    scratch = (
        [pltpu.VMEM(dims, BF) for dims in shapes]
        + [pltpu.VMEM((devices,) + shapes[piece], BF) for piece in (TABLE, ENTRY, EXIT)]
        + [
            pltpu.VMEM((devices,) + shapes[EXPAND], BF),
            pltpu.VMEM((devices,) + shapes[REDUCE], BF),
            pltpu.VMEM(flat, BF),
            pltpu.VMEM((8, width), F32),
            pltpu.VMEM(flat, F32),
            pltpu.VMEM(flat, BF),
            pltpu.VMEM((rows, 3 * width), BF),
            pltpu.VMEM(flat, BF),
            pltpu.VMEM(flat, F32),
            pltpu.VMEM(flat, BF),
            pltpu.VMEM((2,) + flat, BF),
            pltpu.VMEM((2,) + flat, F32),
            pltpu.VMEM(flat, BF),
            pltpu.VMEM((rows, 128), F32),
            pltpu.VMEM((rows, 1), jnp.int32),
            pltpu.VMEM((rows, 1), jnp.int32),
            pltpu.SemaphoreType.DMA((6, 31)),
            pltpu.SemaphoreType.DMA((6, devices)),
            pltpu.SemaphoreType.DMA((6,)),
            pltpu.SemaphoreType.DMA((16,)),
            pltpu.SemaphoreType.DMA((16,)),
            pltpu.SemaphoreType.DMA((2, 2)),
        ]
    )
    return pl.pallas_call(
        functools.partial(forward_kernel, shapes),
        out_shape=outs,
        in_specs=[ANY] + [VMEM] * 10,
        out_specs=[ANY] * len(outs),
        scratch_shapes=scratch,
        compiler_params=pltpu.CompilerParams(
            collective_id=0, has_side_effects=True, vmem_limit_bytes=58 * MIB
        ),
        name="gather_forward",
    )(tokens, kept, lengths, owners, *shards, norm)


def norm_back(values, slope, gain):
    center = values - jnp.mean(values, axis=-1, keepdims=True)
    spread = jnp.mean(center * center, axis=-1, keepdims=True)
    scale = lax.rsqrt(spread + LN_EPS)
    unit = center * scale
    scaled = slope * gain
    level = jnp.mean(scaled, axis=-1, keepdims=True)
    tilt = jnp.mean(scaled * unit, axis=-1, keepdims=True)
    return scale * (scaled - level - unit * tilt), slope * unit


def backward_kernel(shapes, *refs):
    count = len(shapes)
    (
        kept,
        segment,
        norms,
        norm_weight,
        norm_first,
        norm_second,
        cot_out_hbm,
        cot_align_hbm,
        entry_hbm,
        exit_hbm,
        expand_hbm,
        reduce_hbm,
        align_hbm,
        residual_hbm,
        normed_one_hbm,
        joint_hbm,
        attended_hbm,
        middle_hbm,
        normed_two_hbm,
        act_hbm,
        slope_hbm,
        low_hbm,
        totals_hbm,
    ) = refs[:23]
    states = [refs[23 + 3 * piece : 26 + 3 * piece] for piece in range(count)]
    refs = refs[23 + 3 * count :]
    outs = refs[:count]
    norm_out, sums_out, aligned_out, token_out = refs[count : 4 + count]
    refs = refs[4 + count :]
    grads, refs = refs[:count], refs[count:]
    from_pair, refs = refs[:count], refs[count:]
    from_far, refs = refs[:count], refs[count:]
    from_near, refs = refs[:count], refs[count:]
    from_peer, refs = refs[:count], refs[count:]
    (
        wide_b,
        spare,
        act,
        expand,
        reduce,
        normed_two,
        grad_feed,
        grad_out,
        grad_two,
        slope,
        query_sum,
        norm_sums,
        held,
        table_first,
        table_second,
        table_third,
        send_sem,
        pair_sem,
        far_sem,
        near_sem,
        peer_sem,
        load_sem,
        save_sem,
        state_sem,
        held_sem,
        sums_sem,
    ) = refs
    rows, width = grad_out.shape
    align_width = cot_align_hbm.shape[1]
    route = Route()
    core = route.core
    near, far, pair = (route.near, core), (route.far, core), (route.dp, 1 - core)

    def load(source, target, number):
        copy = pltpu.make_async_copy(source, target, load_sem.at[number])
        copy.start()
        return copy

    align_low = wide_b.at[:, pl.ds(0, align_width)]
    cot_align = wide_b.at[:, pl.ds(align_width, align_width)]
    cot_align_copy = load(cot_align_hbm, cot_align, 0)
    align_copy = load(align_hbm, align_low, 1)
    low_copy = load(low_hbm, act, 2)
    cot_out_copy = load(cot_out_hbm, spare, 3)
    normed_two_copy = load(normed_two_hbm, normed_two, 4)
    arrive = greet(route.partners + [route.corner])

    def level_rows(step):
        return pl.ds(pl.multiple_of((route.level(step) // 4) * width, width), width)

    def chunk_loads(step):
        here = level_rows(step)
        return (
            pltpu.make_async_copy(reduce_hbm.at[here, :], reduce, load_sem.at[6]),
            pltpu.make_async_copy(expand_hbm.at[here, :], expand, load_sem.at[7]),
            pltpu.make_async_copy(slope_hbm.at[:, here], slope, load_sem.at[8]),
        )

    def act_load(step):
        return pltpu.make_async_copy(act_hbm.at[:, level_rows(step)], act, load_sem.at[9])


    def copy_to(source, target, slot, piece, semaphore, partner):
        return pltpu.make_async_remote_copy(
            src_ref=source,
            dst_ref=target,
            send_sem=send_sem.at[piece, slot],
            recv_sem=semaphore,
            device_id=partner,
            device_id_type=MESH,
        )

    def landed(block, semaphore):
        pltpu.make_async_copy(block, block, semaphore).wait()

    def total(piece, dp, sources):
        landed(from_pair[piece].at[dp], pair_sem.at[piece, dp])
        found = grads[piece][dp * 2 + core].astype(F32) + from_pair[piece][dp].astype(F32)
        for block, semaphore, slot in sources:
            landed(block.at[slot], semaphore.at[piece, slot])
            found = found + block[slot].astype(F32)
        return found

    def stage_pair(piece, step):
        for base in (route.far, route.both, route.near, route.dp):
            dp = route.at(base, step)
            copy_to(
                grads[piece].at[dp * 2 + 1 - core],
                from_pair[piece].at[dp],
                dp,
                piece,
                pair_sem.at[piece, dp],
                pair,
            ).start()

    def forward_sum(piece, dp, sources, target, slot, semaphore, partner):
        grads[piece][dp * 2 + core] = total(piece, dp, sources).astype(BF)
        copy_to(
            grads[piece].at[dp * 2 + core], target, slot, piece, semaphore, partner
        ).start()

    def stage_far(piece, step):
        for side, base in enumerate((route.far, route.both)):
            slot = step * 2 + side
            forward_sum(
                piece,
                route.at(base, step),
                (),
                from_far[piece].at[slot],
                16 + slot,
                far_sem.at[piece, slot],
                far,
            )

    def stage_near(piece, step):
        forward_sum(
            piece,
            route.at(route.near, step),
            ((from_far[piece], far_sem, step * 2 + 1),),
            from_near[piece].at[step],
            24 + step,
            near_sem.at[piece, step],
            near,
        )

    def stage_peer(piece, step):
        forward_sum(
            piece,
            route.level(step),
            ((from_far[piece], far_sem, step * 2), (from_near[piece], near_sem, step)),
            from_peer[piece].at[step - 1],
            27 + step,
            peer_sem.at[piece, step - 1],
            (route.level(step), core),
        )

    def stage_own(piece):
        found = total(
            piece,
            route.dp,
            ((from_far[piece], far_sem, 0), (from_near[piece], near_sem, 0))
            + tuple((from_peer[piece], peer_sem, slot) for slot in range(3)),
        )
        if outs[piece].shape == found.shape:
            outs[piece][...] = found
            return
        blocks = found.shape[1] // 128
        lines = TABLE_ROWS - 1 if piece == TABLE else found.shape[0]
        for block in range(blocks):
            part = found[:, block * 128 : block * 128 + 128]
            outs[piece][pl.ds(block, lines, stride=blocks), :] = part[:lines]
            if piece == TABLE:
                outs[piece][pl.ds(lines * blocks + block, 1), :] = part[lines : lines + 1]
        if piece == TABLE:
            norm_sums[4:5, :] = found[lines + 1 : lines + 2] + found[lines + 2 : lines + 3]

    def each(stage, pieces, first=0):
        def body(turn, carry):
            for piece in pieces:
                stage(piece, turn)
            return carry

        lax.fori_loop(first, 4, body, 0)

    def flow(piece, turn):
        for late, stage in enumerate((stage_far, stage_near, stage_peer)):
            step = 3 - (turn - late)
            lowest = 1 if stage is stage_peer else 0

            @pl.when(jnp.logical_and(step >= lowest, step <= 3))
            def _():
                stage(piece, step)


    norm_sums[...] = jnp.zeros_like(norm_sums)
    cot_align_copy.wait()
    align_copy.wait()
    low_copy.wait()
    cot_out_copy.wait()
    for copy in chunk_loads(3):
        copy.start()

    def head_rows(index, carry):
        span = pl.ds(pl.multiple_of(index * 256, 256), 256)
        keep = segment[span, :] > 0
        slopes = jnp.where(keep, cot_align[span, :], jnp.zeros((256, align_width), BF))
        cot_align[span, :] = slopes
        found = contract(slopes, align_low[...], 1, 1)
        found = found + jnp.where(keep, spare[span, :].astype(F32), 0.0)
        grad_out[span, :] = found
        grad_feed[span, :] = found.astype(BF)
        return carry

    lax.fori_loop(0, rows // 256, head_rows, 0)

    def head_grads(index, carry):
        span = pl.ds(pl.multiple_of(index * 384, 384), 384)
        found = contract(act[:, span], cot_align[...], 0, 0).astype(BF)
        slabs = 384 // shapes[ALIGN][0]
        grads[ALIGN][pl.ds(index * slabs, slabs)] = found.reshape((slabs,) + shapes[ALIGN])
        return carry

    lax.fori_loop(0, width // 384, head_grads, 0)
    arrive()
    each(stage_pair, (ALIGN,))

    def head_out(index, carry):
        span = pl.ds(pl.multiple_of(index * 256, 256), 256)
        result = contract(act[span, :], align_low[...], 1, 0).astype(BF)
        cot_align[span, :] = result
        return carry

    lax.fori_loop(0, rows // 256, head_out, 0)
    aligned_copy = pltpu.make_async_copy(cot_align, aligned_out, save_sem.at[0])
    aligned_copy.start()
    act_load(3).start()
    normed_two_copy.wait()


    def feed_back(turn, carry):
        step = 3 - turn
        for copy in chunk_loads(step):
            copy.wait()

        def rows_block(index, inner):
            span = pl.ds(pl.multiple_of(index * 256, 256), 256)
            found = contract(grad_feed[span, :], reduce[...], 1, 1)
            before = (found * slope[span, :]).astype(BF)
            spare[span, :] = before
            part = contract(before, expand[...], 1, 0)

            @pl.when(turn == 0)
            def _():
                grad_two[span, :] = part

            @pl.when(turn > 0)
            def _():
                grad_two[span, :] += part

            return inner

        lax.fori_loop(0, rows // 256, rows_block, 0)

        @pl.when(turn < 3)
        def _():
            for copy in chunk_loads(step - 1):
                copy.start()

        @pl.when(turn == 3)
        def _():
            pltpu.make_async_copy(middle_hbm, slope, load_sem.at[8]).start()
            pltpu.make_async_copy(exit_hbm, expand, load_sem.at[7]).start()

        @pl.when(turn == 0)
        def _():
            each(stage_far, (ALIGN,))

        @pl.when(turn > 0)
        def _():
            feed_stage(stage_far, step + 1)

        act_load(step).wait()
        per = 384 // shapes[EXPAND][0]
        plane = (route.level(step) // 4) * (width // shapes[EXPAND][0])

        def slabs_block(index, inner):
            span = pl.ds(pl.multiple_of(index * 384, 384), 384)
            here = pl.ds(plane + index * per, per)
            found = contract(act[:, span], grad_feed[...], 0, 0).astype(BF)
            grads[REDUCE][here] = found.reshape((per,) + shapes[REDUCE])
            found = contract(spare[:, span], normed_two[...], 0, 0).astype(BF)
            grads[EXPAND][here] = found.reshape((per,) + shapes[EXPAND])
            return inner

        lax.fori_loop(0, width // 384, slabs_block, 0)

        @pl.when(turn < 3)
        def _():
            act_load(step - 1).start()

        for piece in (REDUCE, EXPAND):
            stage_pair(piece, step)

        @pl.when(turn == 3)
        def _():
            feed_stage(stage_near, 3)

        return carry

    def feed_stage(stage, step):
        for piece in (REDUCE, EXPAND):
            stage(piece, step)

    lax.fori_loop(0, 4, feed_back, 0)
    aligned_copy.wait()
    joint_copy = load(joint_hbm, wide_b, 5)
    attended_copy = load(attended_hbm, normed_two, 2)
    normed_one_copy = load(normed_one_hbm, act, 9)
    pltpu.make_async_copy(middle_hbm, slope, load_sem.at[8]).wait()
    pltpu.make_async_copy(exit_hbm, expand, load_sem.at[7]).wait()


    def leave_back(index, carry):
        span = pl.ds(pl.multiple_of(index * 256, 256), 256)
        slopes = grad_two[span, :]
        through, gains = norm_back(slope[span, :], slopes, norms[2:3, :])
        norm_sums[2:3, :] += jnp.sum(gains, axis=0, keepdims=True)
        norm_sums[3:4, :] += jnp.sum(slopes, axis=0, keepdims=True)
        found = grad_out[span, :] + through
        grad_out[span, :] = found
        branch = found.astype(BF)
        grad_feed[span, :] = branch
        reduce[span, :] = contract(branch, expand[...], 1, 1).astype(BF)
        return carry

    lax.fori_loop(0, rows // 256, leave_back, 0)
    residual_copy = load(residual_hbm, grad_two, 0)

    def load_entry(part, target):
        return load(entry_hbm.at[:, pl.ds(part * width, width)], target, (1, 3, 6)[part])

    entry_copies = [load_entry(0, expand)]
    key_sum, value_sum, totals = (slope.at[:, pl.ds(number * 128, 128)] for number in range(3))
    totals_copy = load(totals_hbm, totals, 10)
    attended_copy.wait()

    def exit_grads(index, carry):
        span = pl.ds(pl.multiple_of(index * 384, 384), 384)
        found = contract(normed_two[:, span], grad_feed[...], 0, 0).astype(BF)
        slabs = 384 // shapes[EXIT][0]
        grads[EXIT][pl.ds(index * slabs, slabs)] = found.reshape((slabs,) + shapes[EXIT])
        return carry

    lax.fori_loop(0, width // 384, exit_grads, 0)
    each(stage_pair, (EXIT,))
    feed_stage(stage_far, 0)
    joint_copy.wait()


    scale = HD**-0.5
    totals_copy.wait()

    def split(values):
        high = values.astype(BF)
        rest = values - high.astype(F32)
        middle = rest.astype(BF)
        return high, middle, (rest - middle.astype(F32)).astype(BF)

    def with_parts(lane, values, others):
        parts = split(values)
        for number in range(3):
            others = jnp.where(lane == 8 + number, parts[number], others)
        return others

    def attend_pair(index, carry):
        start = pl.multiple_of(index * 128, 128)
        at_query = pl.ds(start, 128)
        at_key = pl.ds(start + width, 128)
        at_value = pl.ds(start + 2 * width, 128)
        key_sum[...] = jnp.zeros_like(key_sum)
        value_sum[...] = jnp.zeros_like(value_sum)
        whole_keys = wide_b[:, at_key]
        whole_values = wide_b[:, at_value]
        turned = whole_keys.astype(F32).T.astype(BF)
        lane = jnp.bitwise_and(lax.broadcasted_iota(jnp.int32, (rows, 128), 1), HD - 1)
        parted = jnp.logical_and(lane >= 8, lane < 11)
        ones = parted.astype(BF)
        keys = []
        for head in (0, 1):
            mine, same = lane_marks(head, segment[...])
            marks = jnp.where(same, 0.0, -1e30).astype(BF)
            keys.append(jnp.where(mine, whole_keys, jnp.where(parted, ones, marks)))

        def chunk(step, inner):
            span = pl.ds(pl.multiple_of(step * 256, 256), 256)
            whole_lane = lax.broadcasted_iota(jnp.int32, (256, 128), 1)
            lane = jnp.bitwise_and(whole_lane, HD - 1)
            scaled = wide_b[span, at_query] * BF(scale)
            both_slopes = reduce[span, at_query]
            zero = jnp.zeros_like(scaled)
            queries, pure_queries, slopes = [], [], []
            for head in (0, 1):
                mine, same = lane_marks(head, segment[span, :])
                log_total = jnp.sum(
                    jnp.where(whole_lane == index * 2 + head, totals[span, :], 0.0),
                    axis=1,
                    keepdims=True,
                )
                marks = with_parts(lane, -log_total, same.astype(BF))
                queries.append(jnp.where(mine, scaled, marks))
                pure_queries.append(jnp.where(mine, scaled, zero))
                slopes.append(jnp.where(mine, both_slopes, zero))
            pure_queries = jnp.concatenate(pure_queries, axis=0)
            slopes = jnp.concatenate(slopes, axis=0)
            scores = [contract(keys[head], queries[head], 1, 1) for head in (0, 1)]
            slope_attention = contract(whole_values, slopes, 1, 1)
            attentions, slope_scores = [], []
            for head in (0, 1):
                attention = jnp.exp(scores[head])
                mine = slope_attention[:, head * 256 : head * 256 + 256]
                inner_sum = jnp.sum(attention * mine, axis=0, keepdims=True)
                slope_scores.append((attention * (mine - inner_sum)).astype(BF))
                attentions.append(attention.astype(BF))
            value_sum[...] += contract(jnp.concatenate(attentions, axis=1), slopes, 1, 0)
            key_sum[...] += contract(jnp.concatenate(slope_scores, axis=1), pure_queries, 1, 0)
            for head in (0, 1):
                half = slice(head * HD, head * HD + HD)
                query_sum[half, span] = contract(turned[half, :], slope_scores[head], 1, 0)
            return inner

        lax.fori_loop(0, rows // 256, chunk, 0)
        wide_b[:, at_query] = (query_sum[...].T * scale).astype(BF)
        wide_b[:, at_key] = key_sum[...].astype(BF)
        wide_b[:, at_value] = value_sum[...].astype(BF)

        @pl.when(index == 0)
        def _():
            feed_stage(stage_near, 2)
            each(stage_far, (EXIT,))

        @pl.when(index == 1)
        def _():
            feed_stage(stage_near, 1)
            feed_stage(stage_peer, 3)
            each(stage_near, (ALIGN,))

        @pl.when(index == 2)
        def _():
            feed_stage(stage_near, 0)
            feed_stage(stage_peer, 2)
            each(stage_near, (EXIT,))

        @pl.when(index == 3)
        def _():
            feed_stage(stage_peer, 1)
            each(stage_peer, (ALIGN,), 1)

        @pl.when(index == 4)
        def _():
            each(stage_peer, (EXIT,), 1)

        return carry

    lax.fori_loop(0, width // 128, attend_pair, 0)

    table_states = (table_first, table_second, table_third)
    homes, line = {}, {}
    for number in range(3):
        for piece in (ENTRY, EXIT, ALIGN):
            start = line.get(number, 0)
            size = states[piece][number].shape[0]
            homes[piece, number] = slope.at[
                pl.ds(start, size), pl.ds(number * 128, 128)
            ]
            line[number] = start + size
        homes[TABLE, number] = table_states[number]
        for turn, piece in enumerate((EXPAND, REDUCE)):
            size = shapes[piece][0]
            homes[piece, number] = grad_two.at[pl.ds((turn * 3 + number) * size, size), :]

    def state_copy(piece, number):
        return pltpu.make_async_copy(
            states[piece][number], homes[piece, number], state_sem.at[piece, number]
        )

    def start_states(pieces):
        for piece in pieces:
            for number in range(3):
                state_copy(piece, number).start()

    entry_copies.append(load_entry(1, reduce))
    start_states((ENTRY, EXIT, ALIGN, TABLE))


    normed_one_copy.wait()
    for block in range(width // 128):
        lanes = slice(block * 128, block * 128 + 128)
        spare[lanes, :] = act[:, lanes].astype(F32).T.astype(BF)

    entry_copies.append(load_entry(2, act))

    def entry_block(index, carry):
        half = index // 3
        column = pl.ds(pl.multiple_of(lax.rem(index, 3) * width, width), width)
        line = pl.ds(pl.multiple_of(half * 384, 384), 384)
        found = contract(spare[line, :], wide_b[:, column], 1, 0).astype(BF)
        slabs = 384 // shapes[ENTRY][0]
        grads[ENTRY][pl.ds(half * slabs, slabs), :, column] = found.reshape(
            (slabs, shapes[ENTRY][0], width)
        )
        return carry

    lax.fori_loop(0, 6, entry_block, 0)
    each(stage_pair, (ENTRY,))
    for copy in entry_copies:
        copy.wait()
    residual_copy.wait()

    def enter_back(index, carry):
        span = pl.ds(pl.multiple_of(index * 256, 256), 256)
        slopes = contract(wide_b[span, 0:width], expand[...], 1, 1)
        slopes += contract(wide_b[span, width : 2 * width], reduce[...], 1, 1)
        slopes += contract(wide_b[span, 2 * width : 3 * width], act[...], 1, 1)
        through, gains = norm_back(grad_two[span, :], slopes, norms[0:1, :])
        norm_sums[0:1, :] += jnp.sum(gains, axis=0, keepdims=True)
        norm_sums[1:2, :] += jnp.sum(slopes, axis=0, keepdims=True)
        found = grad_out[span, :] + through
        grad_out[span, :] = found
        grad_feed[span, :] = found.astype(BF)
        flow(ENTRY, index)
        return carry

    lax.fori_loop(0, rows // 256, enter_back, 0)
    token_copy = pltpu.make_async_copy(grad_out, token_out, save_sem.at[1])
    token_copy.start()
    start_states((EXPAND, REDUCE))

    slabs = 4
    block_rows = slabs * TABLE_SLAB

    def table_block(index, carry):
        entries = lax.broadcasted_iota(jnp.int32, (block_rows, rows), 0) + index * block_rows
        picks = (entries == slab_places(kept[...])).astype(BF)
        found = contract(picks, grad_feed[...], 1, 0).astype(BF)
        grads[TABLE][pl.ds(index * slabs, slabs)] = found.reshape((slabs, TABLE_SLAB, width))

        @pl.when(lax.rem(index, 2) == 0)
        def _():
            flow(ENTRY, 3 + index // 2)

        return carry

    devices = grads[TABLE].shape[0]
    lax.fori_loop(0, devices // slabs, table_block, 0)
    whole = TABLE_ROWS - 1
    row_id = lax.broadcasted_iota(jnp.int32, (8, width), 0)
    for member in range(4):
        line = norm_sums[member : member + 1, :]
        high = line.astype(BF).astype(F32)
        tail = jnp.where(row_id == 1, high, jnp.where(row_id == 2, line - high, 0.0))

        def tuck(index, carry):
            slab = member * (devices // 4) + index
            kept = grads[TABLE][slab, whole : whole + 8, :].astype(F32)
            grads[TABLE][slab, whole : whole + 8, :] = jnp.where(row_id == 0, kept, tail).astype(BF)
            return carry

        lax.fori_loop(0, devices // 4, tuck, 0)
    each(stage_pair, (TABLE,))
    row_id16 = lax.broadcasted_iota(jnp.int32, (16, 128), 0)

    def squares(piece):
        for number in range(3):
            state_copy(piece, number).wait()
        weight, first, second = (homes[piece, number][...] for number in range(3))
        update = lamb_update(weight, outs[piece][...], first, second, DECAY)[2]
        note(MEMBERS.index(piece), total_square(weight), total_square(update))

    def note(member, weight_square, update_square):
        kept = held[0]
        kept = jnp.where(row_id16 == member, weight_square, kept)
        held[0] = jnp.where(row_id16 == 8 + member, update_square, kept)

    held[0] = jnp.zeros_like(held[0])
    for turn in range(3):
        flow(TABLE, turn)
    for piece in (ALIGN, REDUCE, EXPAND, EXIT):
        stage_own(piece)
        squares(piece)
    for turn in range(3, 6):
        flow(TABLE, turn)
    stage_own(ENTRY)
    squares(ENTRY)
    stage_own(TABLE)
    squares(TABLE)
    norm_row = norm_sums[4:5, :]
    share = lax.rem(route.me, width // NORM_LANES)
    norm_slope = jnp.zeros((1, NORM_LANES), F32)
    for number in range(width // NORM_LANES):
        part = norm_row[:, number * NORM_LANES : (number + 1) * NORM_LANES]
        norm_slope = jnp.where(share == number, part, norm_slope)
    norm_out[...] = norm_slope
    update = lamb_update(norm_weight[...], norm_slope, norm_first[...], norm_second[...], 0.0)[2]
    note(len(MEMBERS), total_square(norm_weight[...]), total_square(update))


    def sums_to(slot, target, partner, number):
        copy = pltpu.make_async_remote_copy(
            src_ref=held.at[slot],
            dst_ref=held.at[target],
            send_sem=sums_sem.at[number],
            recv_sem=held_sem.at[target],
            device_id=partner,
            device_id_type=MESH,
        )
        copy.start()
        return copy

    def sums_from(slot):
        pltpu.make_async_copy(held.at[slot], held.at[slot], held_sem.at[slot]).wait()

    sums_sent = [sums_to(0, 1, pair, 0)]
    sums_from(1)
    column = route.column
    held[2 + column] = held[0] + held[1]
    plane = [(route.near, core), (route.far, core), route.corner]
    for number, partner in enumerate(plane):
        sums_sent.append(sums_to(2 + column, 2 + column, partner, 1 + number))
    for partner, _ in plane:
        sums_from(2 + lax.rem(partner, 4))
    held[6 + route.z] = held[2] + held[3] + held[4] + held[5]
    for number, peer in enumerate(route.peers):
        sums_sent.append(sums_to(6 + route.z, 6 + route.z, (peer, core), 4 + number))
    for peer in route.peers:
        sums_from(6 + peer // 4)
    sums_out[...] = held[6] + held[7] + held[8] + held[9]
    for copy in sums_sent:
        copy.wait_send()

    def sent(slot, carry):
        for piece in range(count):
            copy_to(
                grads[piece].at[0], from_pair[piece].at[0], slot, piece, pair_sem.at[piece, 0], pair
            ).wait_send()
        return carry

    lax.fori_loop(0, 31, sent, 0)
    token_copy.wait()


def scatter_backward(kept, segment, norms, norm_states, arrays, states, shapes, devices):
    rows, width = arrays[0].shape
    align_width = arrays[1].shape[1]
    dps = devices // 2
    flat = (rows, width)

    def buffers(slots):
        return [pltpu.VMEM((slots,) + dims, BF) for dims in shapes]

    count = len(shapes)
    scratch = (
        buffers(devices)
        + buffers(dps)
        + buffers(8)
        + buffers(4)
        + buffers(3)
        + [pltpu.VMEM((rows, 3 * width), BF)]
        + [pltpu.VMEM(flat, BF)] * 6
        + [pltpu.VMEM(flat, F32)] * 3
        + [
            pltpu.VMEM((128, rows), F32),
            pltpu.VMEM((8, width), F32),
            pltpu.VMEM((10, 16, 128), F32),
        ]
        + [pltpu.VMEM(states[3 * TABLE].shape, F32)] * 3
        + [
            pltpu.SemaphoreType.DMA((count, 31)),
            pltpu.SemaphoreType.DMA((count, dps)),
            pltpu.SemaphoreType.DMA((count, 8)),
            pltpu.SemaphoreType.DMA((count, 4)),
            pltpu.SemaphoreType.DMA((count, 3)),
            pltpu.SemaphoreType.DMA((11,)),
            pltpu.SemaphoreType.DMA((2,)),
            pltpu.SemaphoreType.DMA((count, 3)),
            pltpu.SemaphoreType.DMA((10,)),
            pltpu.SemaphoreType.DMA((7,)),
        ]
    )
    outs = [jax.ShapeDtypeStruct(state.shape, F32) for state in states[::3]] + [
        jax.ShapeDtypeStruct((1, NORM_LANES), F32),
        jax.ShapeDtypeStruct((16, 128), F32),
        jax.ShapeDtypeStruct((rows, align_width), BF),
        jax.ShapeDtypeStruct(flat, F32),
    ]
    return pl.pallas_call(
        functools.partial(backward_kernel, shapes),
        out_shape=outs,
        in_specs=[VMEM] * 6 + [ANY] * (len(arrays) + len(states)),
        out_specs=[VMEM] * (count + 2) + [ANY] * 2,
        scratch_shapes=scratch,
        compiler_params=pltpu.CompilerParams(
            collective_id=1, has_side_effects=True, vmem_limit_bytes=60 * MIB
        ),
        name="scatter_backward",
    )(kept, segment, norms, *norm_states, *arrays, *states)


def lamb_update(weight, gradient, first, second, decay):
    new_first = BETA_ONE * first + (1.0 - BETA_ONE) * gradient
    new_second = BETA_TWO * second + (1.0 - BETA_TWO) * gradient * gradient
    update = new_first / (jnp.sqrt(new_second) + ADAM_EPS) + decay * weight
    return new_first, new_second, update


def total_square(values):
    return jnp.sum(jnp.sum(values * values, axis=1, keepdims=True), axis=0, keepdims=True)


def finish_kernel(count, *refs):
    segment, sums, norm_slope = refs[:3]
    norm_states = refs[3:6]
    slopes_hbm = refs[6 : 6 + count]
    refs = refs[6 + count :]
    states, refs = refs[: 3 * count], refs[3 * count :]
    low_hbm, aligned_hbm, token_hbm = refs[:3]
    outs, refs = refs[3 : 3 + 3 * count], refs[3 + 3 * count :]
    norm_outs = refs[:3]
    block_out, aligned_out, token_out, stats = refs[3:7]
    refs = refs[7:]
    held, refs = refs[: 3 * count], refs[3 * count :]
    made, refs = refs[: 3 * count], refs[3 * count :]
    slopes, refs = refs[:count], refs[count:]
    slope_sem, low, aligned, token, in_sem, out_sem, row_sem = refs
    slope_loads = [
        pltpu.make_async_copy(slopes_hbm[piece], slopes[piece], slope_sem.at[piece])
        for piece in range(count)
    ]
    for copy in slope_loads:
        copy.start()
    token_copy = pltpu.make_async_copy(token_hbm, token, row_sem.at[0])
    token_copy.start()
    low_copy = pltpu.make_async_copy(low_hbm, low, row_sem.at[1])
    low_copy.start()
    aligned_copy = pltpu.make_async_copy(aligned_hbm, aligned, row_sem.at[2])
    aligned_copy.start()
    loads = [
        pltpu.make_async_copy(states[number], held[number], in_sem.at[number])
        for number in range(3 * count)
    ]
    for copy in loads:
        copy.start()

    def trust_of(member):
        weight_square = sums[member : member + 1, :]
        update_square = sums[8 + member : 9 + member, :]
        return jnp.sqrt(weight_square) / jnp.sqrt(update_square + TINY)

    lane = lax.broadcasted_iota(jnp.int32, (1, 128), 1)
    lines = [jnp.zeros((1, 128), F32)] * 3
    for member in range(len(MEMBERS) + 1):
        found = (
            trust_of(member),
            jnp.sqrt(sums[member : member + 1, :]),
            jnp.sqrt(sums[8 + member : 9 + member, :]),
        )
        lines = [jnp.where(lane == member, new, line) for new, line in zip(found, lines)]
    for row, line in enumerate(lines):
        stats[row : row + 1, :] = line[:, : stats.shape[1]]
    weight, first, second = (state[...] for state in norm_states)
    made_norm = lamb_update(weight, norm_slope[...], first, second, 0.0)
    norm_outs[0][...] = made_norm[0]
    norm_outs[1][...] = made_norm[1]
    step = RATE * trust_of(len(MEMBERS))[:, :NORM_LANES] * made_norm[2]
    norm_outs[2][...] = weight - step
    token_copy.wait()
    token_copy = pltpu.make_async_copy(token, token_out, row_sem.at[0])
    token_copy.start()
    low_copy.wait()
    keep = segment[...] > 0
    low[...] = jnp.where(keep, low[...], jnp.zeros_like(low))
    low_copy = pltpu.make_async_copy(low, block_out, row_sem.at[1])
    low_copy.start()
    aligned_copy.wait()
    aligned[...] = jnp.where(keep, aligned[...], jnp.zeros_like(aligned))
    aligned_copy = pltpu.make_async_copy(aligned, aligned_out, row_sem.at[2])
    aligned_copy.start()
    saves = []
    for member, piece in enumerate(MEMBERS):
        trust = trust_of(member)
        for number in range(3):
            loads[3 * piece + number].wait()
        slope_loads[piece].wait()
        weight, first, second = (held[3 * piece + number][...] for number in range(3))
        new_first, new_second, update = lamb_update(
            weight, slopes[piece][...], first, second, DECAY
        )
        wide = trust if update.shape[1] == 128 else trust[:, 0:1]
        made[3 * piece][...] = new_first
        made[3 * piece + 1][...] = new_second
        made[3 * piece + 2][...] = weight - RATE * wide * update
        for number in range(3):
            copy = pltpu.make_async_copy(
                made[3 * piece + number], outs[3 * piece + number], out_sem.at[3 * piece + number]
            )
            copy.start()
            saves.append(copy)
    for copy in saves + [low_copy, aligned_copy, token_copy]:
        copy.wait()


def finish(segment, sums, norm_slope, norm_states, slopes, states, rows):
    count = len(slopes)
    low, aligned, token = rows

    def like(array):
        return jax.ShapeDtypeStruct(array.shape, array.dtype)

    outs = (
        [like(state) for state in states]
        + [like(state) for state in norm_states]
        + [like(low), like(aligned), like(token)]
        + [jax.ShapeDtypeStruct((3, len(MEMBERS) + 1), F32)]
    )
    return pl.pallas_call(
        functools.partial(finish_kernel, count),
        out_shape=outs,
        in_specs=[VMEM] * 6 + [ANY] * (4 * count + 3),
        out_specs=[ANY] * (3 * count) + [VMEM] * 3 + [ANY] * 3 + [VMEM],
        scratch_shapes=[pltpu.VMEM(state.shape, F32) for state in states] * 2
        + [pltpu.VMEM(slope.shape, F32) for slope in slopes]
        + [
            pltpu.SemaphoreType.DMA((count,)),
            pltpu.VMEM(low.shape, BF),
            pltpu.VMEM(aligned.shape, BF),
            pltpu.VMEM(token.shape, F32),
            pltpu.SemaphoreType.DMA((3 * count,)),
            pltpu.SemaphoreType.DMA((3 * count,)),
            pltpu.SemaphoreType.DMA((3,)),
        ],
        compiler_params=pltpu.CompilerParams(vmem_limit_bytes=60 * MIB),
        name="finish",
    )(segment, sums, norm_slope, *norm_states, *slopes, *states, low, aligned, token)


def moments_kernel(decays, *refs):
    count = len(decays)
    sums = refs[7 * count]
    row = lax.broadcasted_iota(jnp.int32, (16, 128), 0)
    found = jnp.zeros((16, 128), F32)
    for member, decay in enumerate(decays):
        weight, gradient, first, second = refs[4 * member : 4 * member + 4]
        new_first_ref, new_second_ref, update_ref = refs[
            4 * count + 3 * member : 4 * count + 3 * member + 3
        ]
        slope = gradient[...]
        new_first = BETA_ONE * first[...] + (1.0 - BETA_ONE) * slope
        new_second = BETA_TWO * second[...] + (1.0 - BETA_TWO) * slope * slope
        update = new_first / (jnp.sqrt(new_second) + ADAM_EPS) + decay * weight[...]
        new_first_ref[...] = new_first
        new_second_ref[...] = new_second
        update_ref[...] = update
        found = jnp.where(row == member, jnp.sum(weight[...] * weight[...]), found)
        found = jnp.where(row == 8 + member, jnp.sum(update * update), found)
    sums[...] = found


def moments(members, decays):
    shapes = [jax.ShapeDtypeStruct(member[0].shape, F32) for member in members]
    outs = [shape for shape in shapes for _ in range(3)]
    flat = [array for member in members for array in member]
    return pl.pallas_call(
        functools.partial(moments_kernel, decays),
        out_shape=outs + [jax.ShapeDtypeStruct((16, 128), F32)],
        in_specs=[VMEM] * len(flat),
        out_specs=[VMEM] * (len(outs) + 1),
        compiler_params=pltpu.CompilerParams(vmem_limit_bytes=40 * MIB),
        name="moments",
    )(*flat)


def step_kernel(count, *refs):
    sums = refs[0]
    for member in range(count):
        weight, update = refs[1 + 2 * member : 3 + 2 * member]
        weight_square = sums[member : member + 1, :]
        update_square = sums[8 + member : 9 + member, :]
        trust = jnp.sqrt(weight_square) / jnp.sqrt(update_square + TINY)
        if weight.shape[1] % 128 == 0:
            trust = jnp.concatenate([trust] * (weight.shape[1] // 128), axis=1)
        else:
            trust = trust[:, : weight.shape[1]]
        refs[1 + 2 * count + member][...] = weight[...] - RATE * trust * update[...]


def take_step(sums, pairs):
    count = len(pairs)
    return pl.pallas_call(
        functools.partial(step_kernel, count),
        out_shape=[jax.ShapeDtypeStruct(weight.shape, F32) for weight, _ in pairs],
        in_specs=[VMEM] * (1 + 2 * count),
        out_specs=[VMEM] * count,
        compiler_params=pltpu.CompilerParams(vmem_limit_bytes=40 * MIB),
        name="take_step",
    )(sums, *[array for pair in pairs for array in pair])


def as_rows(flat):
    if flat.ndim == 2:
        return flat
    lanes = max(size for size in range(1, 129) if flat.shape[0] % size == 0)
    return flat.reshape(-1, lanes)


def local(
    tokens,
    kept_patches,
    clip_lengths,
    clip_device,
    cot_output,
    cot_aligned,
    entry_weight,
    entry_first,
    entry_second,
    exit_weight,
    exit_first,
    exit_second,
    align_weight,
    align_first,
    align_second,
    expand_weight,
    expand_first,
    expand_second,
    reduce_weight,
    reduce_first,
    reduce_second,
    position_table,
    position_first,
    position_second,
    norm_params,
    norm_first,
    norm_second,
):
    rows, width = tokens.shape
    align_width = cot_aligned.shape[1]
    axes = ("dp", "tensor")
    pair = lax.axis_size("tensor")
    devices = lax.axis_size("dp") * pair
    hidden = expand_weight.shape[0] * devices
    positions = position_table.shape[0] * devices // width
    routed = devices == 2 * ROUTED_DP and pair == 2
    device = lax.axis_index("dp") * pair + lax.axis_index("tensor")
    shapes = (
        (TABLE_SLAB, width),
        (width // devices, 3 * width),
        (width // devices, width),
        (hidden // devices, width),
        (hidden // devices, width),
        (width // devices, align_width),
    )
    wholes = (
        (positions, width),
        (width, 3 * width),
        (width, width),
        (hidden, width),
        (hidden, width),
        (width, align_width),
    )
    masters = (position_table, entry_weight, exit_weight, expand_weight, reduce_weight, align_weight)
    triples = {
        TABLE: (position_table, position_first, position_second),
        ENTRY: (entry_weight, entry_first, entry_second),
        EXIT: (exit_weight, exit_first, exit_second),
        EXPAND: (expand_weight, expand_first, expand_second),
        REDUCE: (reduce_weight, reduce_first, reduce_second),
        ALIGN: (align_weight, align_first, align_second),
    }
    norms = (norm_params, norm_first, norm_second)
    if routed:
        states = [as_rows(array) for piece in range(6) for array in triples[piece]]
        norm_states = [array.reshape(1, -1) for array in norms]
        kept = kept_patches.reshape(1, -1)
        found = gather_forward(
            states[::3],
            norm_states[0],
            tokens,
            kept,
            clip_lengths.reshape(1, -1),
            clip_device.reshape(1, -1),
            shapes,
            devices,
        )
        lows = [block.reshape(-1, block.shape[2]) for block in found[:5]]
        out_low, segment = found[14], found[16]
        arrays = (cot_output, cot_aligned) + tuple(lows) + tuple(found[6:16])
        results = scatter_backward(
            kept, segment, found[5], norm_states, arrays, states, shapes, devices
        )
        norm_slope, sums, align_rows, token_grad = results[6:]
        done = finish(
            segment,
            sums,
            norm_slope,
            norm_states,
            results[:6],
            states,
            (out_low, align_rows, token_grad),
        )
        outputs = list(done[21:24])
        for piece in MEMBERS:
            for number in range(3):
                outputs.append(done[3 * piece + number].reshape(triples[piece][number].shape))
        outputs = outputs + [array.reshape(-1) for array in done[18:21]] + [done[24]]
        return tuple(outputs)

    segment, valid_rows = row_layout(clip_lengths, clip_device, device, rows)
    segment_column = segment[:, None]
    valid_column = valid_rows[:, None]
    lows = [
        lax.all_gather(master.astype(BF).reshape(-1), axes, axis=0, tiled=True).reshape(whole)
        for master, whole in zip(masters, wholes)
    ]
    norm_low = lax.all_gather(norm_params.astype(BF), axes, axis=0, tiled=True).reshape(4, width)
    patch = kept_patches
    table_low, entry_low, exit_low, expand_low, reduce_low, align_low = lows
    norm_low = norm_low.astype(F32)
    residual = tokens.astype(F32) + jnp.take(table_low, patch, axis=0).astype(F32)
    normed_one = layer_norm(residual, norm_low[0], norm_low[1]).astype(BF)
    joint_low = contract(normed_one, entry_low, 1, 0).astype(BF)
    attended = attend(segment_column, joint_low)
    middle = residual + contract(attended, exit_low, 1, 0)
    normed_two = layer_norm(middle, norm_low[2], norm_low[3]).astype(BF)
    hidden_pre = contract(normed_two, expand_low, 1, 1)
    share = 0.5 + 0.5 * lax.erf(hidden_pre * 0.5**0.5)
    hidden_act = (hidden_pre * share).astype(BF)
    hidden_slope = share + hidden_pre * jnp.exp(-0.5 * hidden_pre * hidden_pre) * (0.5 / math.pi) ** 0.5
    out_low = (middle + contract(hidden_act, reduce_low, 1, 0)).astype(BF)
    align_rows = contract(out_low, align_low, 1, 0).astype(BF)
    cot_align_valid = jnp.where(valid_column, cot_aligned, jnp.zeros_like(cot_aligned))
    grad_align = contract(out_low, cot_align_valid, 0, 0)
    grad_out = jnp.where(valid_column, cot_output.astype(F32), 0.0) + contract(
        cot_align_valid, align_low, 1, 1
    )
    grad_feed = grad_out.astype(BF)
    grad_act = contract(grad_feed, reduce_low, 1, 1)
    grad_pre = (grad_act * hidden_slope).astype(BF)
    grad_reduce = contract(hidden_act, grad_feed, 0, 0)
    grad_expand = contract(grad_pre, normed_two, 0, 0)
    grad_two = contract(grad_pre, expand_low, 1, 0)
    through, gains = norm_back(middle, grad_two, norm_low[2])
    grad_middle = grad_out + through
    grad_branch = grad_middle.astype(BF)
    grad_exit = contract(attended, grad_branch, 0, 0)
    grad_attended = contract(grad_branch, exit_low, 1, 1).astype(BF)
    grad_parts = attend_back(segment_column, joint_low, grad_attended)
    grad_joint = jnp.concatenate([grad_parts[0], grad_parts[1], grad_parts[2]], axis=1)
    grad_entry = contract(normed_one, grad_joint, 0, 0)
    grad_one = contract(grad_joint, entry_low, 1, 1)
    through_one, gains_one = norm_back(residual, grad_one, norm_low[0])
    token_grad = grad_middle + through_one
    places = jnp.arange(positions, dtype=jnp.int32)
    picks = (patch[:, None] == places[None, :]).astype(BF)
    grad_table = contract(picks, token_grad.astype(BF), 0, 0)
    grad_norms = jnp.concatenate(
        [jnp.sum(part, axis=0) for part in (gains_one, grad_one, gains, grad_two)]
    )
    grads = (grad_table, grad_entry, grad_exit, grad_expand, grad_reduce, grad_align)
    summed = [
        lax.psum_scatter(grad.reshape(-1), axes, scatter_dimension=0, tiled=True)
        for grad in grads
    ]
    norm_sum = lax.psum_scatter(grad_norms, axes, scatter_dimension=0, tiled=True)
    block_out = jnp.where(valid_column, out_low, jnp.zeros_like(out_low))
    aligned = jnp.where(valid_column, align_rows, jnp.zeros_like(align_rows))

    def summed_like(master, index):
        return summed[index].reshape(master.shape)

    members = (
        (entry_weight, summed_like(entry_weight, ENTRY), entry_first, entry_second),
        (exit_weight, summed_like(exit_weight, EXIT), exit_first, exit_second),
        (align_weight, summed_like(align_weight, ALIGN), align_first, align_second),
        (expand_weight, summed_like(expand_weight, EXPAND), expand_first, expand_second),
        (reduce_weight, summed_like(reduce_weight, REDUCE), reduce_first, reduce_second),
        (position_table, summed_like(position_table, TABLE), position_first, position_second),
        (norm_params, norm_sum, norm_first, norm_second),
    )
    decays = (DECAY, DECAY, DECAY, DECAY, DECAY, DECAY, 0.0)
    members = [tuple(as_rows(array) for array in member) for member in members]
    found = moments(members, decays)
    sums = found[-1]
    sums = lax.psum(sums, axes)
    stepped = take_step(
        sums, [(members[member][0], found[3 * member + 2]) for member in range(len(members))]
    )
    weight_squares, update_squares = sums[0:7, 0], sums[8:15, 0]
    trust = jnp.sqrt(weight_squares) / jnp.sqrt(update_squares + TINY)
    outputs = [block_out, aligned, token_grad]
    originals = (
        entry_weight,
        exit_weight,
        align_weight,
        expand_weight,
        reduce_weight,
        position_table,
        norm_params,
    )
    for member, original in enumerate(originals):
        for array in (found[3 * member], found[3 * member + 1], stepped[member]):
            outputs.append(array.reshape(original.shape))
    outputs.append(jnp.stack((trust, jnp.sqrt(weight_squares), jnp.sqrt(update_squares))))
    return tuple(outputs)


def solution(mesh):
    both = ("dp", "tensor")
    rows, flat, whole = P(both, None), P(both), P()
    weight_specs = (flat,) * 9 + (rows,) * 6 + (flat,) * 6
    placed = (rows, flat, whole, whole, rows, rows) + weight_specs
    return jax.shard_map(
        local,
        mesh=mesh,
        in_specs=placed,
        out_specs=(rows, rows, rows) + weight_specs + (whole,),
        check_vma=False,
    )
```

```python
import functools
import math

import jax
import jax.numpy as jnp
from jax import lax
from jax.experimental import pallas as pl
from jax.experimental.pallas import tpu as pltpu
from jax.sharding import PartitionSpec as P

H = 12
HD = 64
LN_EPS = 1e-06
RATE = 0.5
BETA_ONE = 0.9
BETA_TWO = 0.98
ADAM_EPS = 1e-06
DECAY = 0.05
TINY = 1e-06
BF = jnp.bfloat16
F32 = jnp.float32
MESH = pl.DeviceIdType.MESH
ANY = pl.BlockSpec(memory_space=pl.ANY)
VMEM = pl.BlockSpec(memory_space=pltpu.VMEM)
MIB = 1 << 20

TABLE, ENTRY, EXIT, EXPAND, REDUCE, ALIGN = range(6)
MEMBERS = (ENTRY, EXIT, ALIGN, EXPAND, REDUCE, TABLE)
TABLE_ROWS = 49
TABLE_SLAB = 56
NORM_LANES = 96
ROUTED_DP = 16


def contract(left, right, left_dim, right_dim):
    return lax.dot_general(
        left, right, (((left_dim,), (right_dim,)), ((), ())), preferred_element_type=F32
    )


def layer_norm(values, gain, shift):
    center = values - jnp.mean(values, axis=-1, keepdims=True)
    spread = jnp.mean(center * center, axis=-1, keepdims=True)
    return center * lax.rsqrt(spread + LN_EPS) * gain + shift


def row_layout(clip_lengths, clip_device, device, row_count):
    mine = clip_device == device
    own_length = jnp.where(mine, clip_lengths, 0)
    starts = jnp.cumsum(own_length) - own_length
    filled = jnp.sum(own_length)
    positions = jnp.arange(row_count, dtype=jnp.int32)
    begun = mine[None, :] & (starts[None, :] <= positions[:, None])
    segment = jnp.sum(begun.astype(jnp.int32), axis=1)
    valid_rows = positions < filled
    return (jnp.where(valid_rows, segment, 0), valid_rows)


class Route:
    def __init__(self):
        dp = lax.axis_index("dp")
        core = lax.axis_index("tensor")
        z, y, x = dp // 4, (dp // 2) % 2, dp % 2
        across_y = dp + 2 - 4 * y
        across_x = dp + 1 - 2 * x
        self.dp, self.core, self.me = dp, core, dp * 2 + core
        self.z, self.column = z, y * 2 + x
        self.near = across_y * (1 - core) + across_x * core
        self.far = across_x * (1 - core) + across_y * core
        self.both = self.near + self.far - dp
        levels = [z + 1 - 2 * (z % 2), 3 - z, (z + 2) % 4]
        self.peers = [level * 4 + y * 2 + x for level in levels]
        self.partners = [(peer, core) for peer in self.peers] + [
            (self.near, core),
            (self.far, core),
            (dp, 1 - core),
        ]
        self.corner = (self.both, core)

    def level(self, step):
        high = lax.rem(self.z // 2 + step // 2, 2)
        low = lax.rem(self.z % 2 + step // 2 + step % 2, 2)
        return (high * 2 + low) * 4 + self.column

    def at(self, base, step):
        return (self.level(step) // 4) * 4 + base % 4


def greet(partners):
    barrier = pltpu.get_barrier_semaphore()
    for partner in partners:
        pl.semaphore_signal(barrier, inc=1, device_id=partner, device_id_type=MESH)
    return lambda: pl.semaphore_wait(barrier, len(partners))


def fold_rows(source, rows, columns):
    blocks = columns // 128
    for block in range(blocks):
        yield block, source[pl.ds(block, rows, stride=blocks), :]


def lane_marks(head, segment_column):
    lane = lax.broadcasted_iota(jnp.int32, (segment_column.shape[0], 128), 1)
    mine = lax.shift_right_logical(lane, 6) == head
    same = jnp.bitwise_and(lane, HD - 1) == segment_column
    return mine, same


def attend_kernel(segment, query, key, value, out):
    rows = query.shape[0]
    chunk = 256
    for head in (0, 1):
        mine, same = lane_marks(head, segment[...])
        keys = jnp.where(mine, key[...], jnp.where(same, 0.0, -1e30).astype(BF))
        queries = jnp.where(mine, query[...] * BF(HD**-0.5), same.astype(BF))
        values = value[...]
        for start in range(0, rows, chunk):
            scores = contract(queries[start : start + chunk], keys, 1, 1)
            peak = jnp.max(scores, axis=1, keepdims=True)
            raised = jnp.exp(scores - peak)
            scale = 1.0 / jnp.sum(raised, axis=1, keepdims=True)
            attention = (raised * scale).astype(BF)
            result = contract(attention, values, 1, 0).astype(BF)
            span = slice(start, start + chunk)
            if head == 0:
                out[span, :] = result
            else:
                out[span, :] = jnp.where(mine[span], result, out[span, :])


def attend(segment, joint):
    rows, width = joint.shape[0], joint.shape[1] // 3
    pairs = width // 128
    return pl.pallas_call(
        attend_kernel,
        grid=(pairs,),
        out_shape=jax.ShapeDtypeStruct((rows, width), BF),
        in_specs=[
            pl.BlockSpec((rows, 1), lambda pair: (0, 0)),
            pl.BlockSpec((rows, 128), lambda pair: (0, pair)),
            pl.BlockSpec((rows, 128), lambda pair: (0, pairs + pair)),
            pl.BlockSpec((rows, 128), lambda pair: (0, 2 * pairs + pair)),
        ],
        out_specs=pl.BlockSpec((rows, 128), lambda pair: (0, pair)),
        compiler_params=pltpu.CompilerParams(vmem_limit_bytes=40 * MIB),
        name="attend",
    )(segment, joint, joint, joint)


def attend_back_kernel(segment, query, key, value, grad, out, key_sum, value_sum):
    rows = query.shape[0]
    chunk = 256
    scale = HD**-0.5
    for head in (0, 1):
        mine, same = lane_marks(head, segment[...])
        keys = jnp.where(mine, key[...], jnp.where(same, 0.0, -1e30).astype(BF))
        scaled = query[...] * BF(scale)
        queries = jnp.where(mine, scaled, same.astype(BF))
        zero = jnp.zeros_like(scaled)
        pure_queries = jnp.where(mine, scaled, zero)
        pure_keys = jnp.where(mine, key[...], zero)
        grads = jnp.where(mine, grad[...], zero)
        values = value[...]
        for start in range(0, rows, chunk):
            span = slice(start, start + chunk)
            scores = contract(keys, queries[span], 1, 1)
            peak = jnp.max(scores, axis=0, keepdims=True)
            raised = jnp.exp(scores - peak)
            attention = raised * (1.0 / jnp.sum(raised, axis=0, keepdims=True))
            grad_values = contract(attention.astype(BF), grads[span], 1, 0)
            grad_attention = contract(values, grads[span], 1, 1)
            inner = jnp.sum(attention * grad_attention, axis=0, keepdims=True)
            grad_score = (attention * (grad_attention - inner)).astype(BF)
            grad_keys = contract(grad_score, pure_queries[span], 1, 0)
            grad_queries = contract(grad_score, pure_keys, 0, 0) * scale
            if head == 0:
                out[0, span, :] = grad_queries.astype(BF)
            else:
                out[0, span, :] = jnp.where(mine[span], grad_queries.astype(BF), out[0, span, :])
            if head == 0 and start == 0:
                key_sum[...] = grad_keys
                value_sum[...] = grad_values
            else:
                key_sum[...] += grad_keys
                value_sum[...] += grad_values
    out[1] = key_sum[...].astype(BF)
    out[2] = value_sum[...].astype(BF)


def attend_back(segment, joint, grad_attended):
    rows, width = grad_attended.shape
    pairs = width // 128
    return pl.pallas_call(
        attend_back_kernel,
        grid=(pairs,),
        out_shape=jax.ShapeDtypeStruct((3, rows, width), BF),
        in_specs=[
            pl.BlockSpec((rows, 1), lambda pair: (0, 0)),
            pl.BlockSpec((rows, 128), lambda pair: (0, pair)),
            pl.BlockSpec((rows, 128), lambda pair: (0, pairs + pair)),
            pl.BlockSpec((rows, 128), lambda pair: (0, 2 * pairs + pair)),
            pl.BlockSpec((rows, 128), lambda pair: (0, pair)),
        ],
        out_specs=pl.BlockSpec((3, rows, 128), lambda pair: (0, 0, pair)),
        scratch_shapes=[pltpu.VMEM((rows, 128), F32), pltpu.VMEM((rows, 128), F32)],
        compiler_params=pltpu.CompilerParams(vmem_limit_bytes=40 * MIB),
        name="attend_back",
    )(segment, joint, joint, joint, grad_attended)


def segments(lengths, owners, device, rows):
    count = lengths.shape[1]
    mine = owners == device
    own = jnp.broadcast_to(jnp.where(mine, lengths, 0).astype(F32), (8, count))
    before = lax.broadcasted_iota(jnp.int32, (count, count), 0)
    after = lax.broadcasted_iota(jnp.int32, (count, count), 1)
    starts = lax.dot_general(
        own,
        (before < after).astype(F32),
        (((1,), (0,)), ((), ())),
        precision=lax.Precision.HIGHEST,
        preferred_element_type=F32,
    )[0:1, :]
    filled = jnp.sum(own[0:1, :], axis=1, keepdims=True)
    place = lax.broadcasted_iota(jnp.int32, (rows, count), 0).astype(F32)
    begun = jnp.where(jnp.logical_and(mine, starts <= place), 1.0, 0.0)
    number = jnp.sum(begun, axis=1, keepdims=True)
    return jnp.where(place[:, 0:1] < filled, number, 0.0).astype(jnp.int32)


def slab_places(patch):
    return patch + lax.shift_right_logical(patch * 1338, 16) * (TABLE_SLAB - TABLE_ROWS)


def forward_kernel(shapes, *refs):
    (
        tokens_hbm,
        kept,
        lengths,
        owners,
        table_f,
        entry_f,
        exit_f,
        expand_f,
        reduce_f,
        align_f,
        norm,
        entry_out,
        exit_out,
        expand_out,
        reduce_out,
        align_out,
        norms_out,
        residual_out,
        normed_one_out,
        joint_out,
        attended_out,
        middle_out,
        normed_two_out,
        act_out,
        slope_out,
        low_out,
        totals_out,
        segment_out,
        table_slab,
        entry_slab,
        exit_slab,
        expand_slab,
        reduce_slab,
        align_slab,
        table,
        entry,
        exit_low,
        wide,
        narrow,
        tokens,
        norms,
        residual,
        normed_one,
        joint,
        attended,
        feed,
        normed_two,
        act,
        slope,
        low,
        totals,
        patch,
        segment,
        send_sem,
        recv_sem,
        own_sem,
        load_sem,
        save_sem,
        act_sem,
    ) = refs
    width = residual.shape[1]
    rows = residual.shape[0]
    slabs = (table_slab, entry_slab, exit_slab, expand_slab, reduce_slab, align_slab)
    targets = (table, entry, exit_low, wide, narrow, align_out)
    route = Route()
    core = route.core
    arrive = greet(route.partners)
    tokens_copy = pltpu.make_async_copy(tokens_hbm, tokens, load_sem.at[0])
    tokens_copy.start()
    near, far, pair = (route.near, core), (route.far, core), (route.dp, 1 - core)
    peers = [(peer, core) for peer in route.peers]

    def copy_to(source, piece, origin, partner, slot):
        return pltpu.make_async_remote_copy(
            src_ref=source,
            dst_ref=targets[piece].at[origin],
            send_sem=send_sem.at[piece, slot],
            recv_sem=recv_sem.at[piece, origin],
            device_id=partner,
            device_id_type=MESH,
        )

    def wait(piece, origin):
        block = targets[piece].at[origin]
        pltpu.make_async_copy(block, block, recv_sem.at[piece, origin]).wait()

    def pass_on(group, origin, partners, slot):
        for piece in group:
            wait(piece, origin)
            for index, partner in enumerate(partners):
                copy_to(targets[piece].at[origin], piece, origin, partner, slot + index).start()

    def launch(group, wide_part, plane_part):
        for index, partner in enumerate([near, far] + peers + [pair]):
            if plane_part if index < 2 else wide_part:
                for piece in group:
                    copy_to(slabs[piece], piece, route.me, partner, index).start()
        if wide_part:
            for piece in group:
                pltpu.make_async_copy(
                    slabs[piece], targets[piece].at[route.me], own_sem.at[piece]
                ).start()

    def peer_turn(group, step):
        pass_on(group, route.level(step) * 2 + core, (near, far, pair), 6 + (step - 1) * 3)

    def near_turn(group, step):
        pass_on(group, route.at(route.near, step) * 2 + core, (far, pair), 15 + step * 2)

    def far_turn(group, step):
        pass_on(group, route.at(route.far, step) * 2 + core, (pair,), 23 + step * 2)
        pass_on(group, route.at(route.both, step) * 2 + core, (pair,), 24 + step * 2)

    def pair_turn(group, step):
        for base in (route.dp, route.near, route.far, route.both):
            for piece in group:
                wait(piece, route.at(base, step) * 2 + 1 - core)

    def settle(group):
        for piece in group:
            pltpu.make_async_copy(
                slabs[piece], targets[piece].at[route.me], own_sem.at[piece]
            ).wait()

    totals[...] = jnp.zeros_like(totals)
    segment[...] = segments(lengths[...], owners[...], route.me, rows)
    lifted = jnp.broadcast_to(slab_places(kept[...]).astype(F32), (8, rows))
    patch[...] = lifted.T[:, 0:1].astype(jnp.int32)
    blocks = width // 128
    whole = TABLE_ROWS - 1
    row_id = lax.broadcasted_iota(jnp.int32, (8, width), 0)
    lane_id = lax.broadcasted_iota(jnp.int32, (NORM_LANES, width), 1)
    from_id = lax.broadcasted_iota(jnp.int32, (NORM_LANES, width), 0)
    parts = width // NORM_LANES
    offset = lax.rem(route.me, parts) * NORM_LANES
    place = (lane_id == from_id + offset).astype(BF)
    spread = contract(norm[...].astype(BF), place, 1, 0)
    tail = jnp.where(row_id == 1, spread, 0.0)
    for block in range(blocks):
        lanes = slice(block * 128, block * 128 + 128)
        table_slab[0:whole, lanes] = table_f[pl.ds(block, whole, stride=blocks), :].astype(BF)
        last = table_f[pl.ds(whole * blocks + block, 1), :]
        mixed = jnp.where(row_id[:, lanes] == 0, last, tail[:, lanes])
        table_slab[whole : whole + 8, lanes] = mixed.astype(BF)
    for block, part in fold_rows(entry_f, *shapes[ENTRY]):
        entry_slab[:, block * 128 : block * 128 + 128] = part.astype(BF)
    for block, part in fold_rows(exit_f, *shapes[EXIT]):
        exit_slab[:, block * 128 : block * 128 + 128] = part.astype(BF)
    arrive()
    early = (TABLE, ENTRY, EXIT)
    last = (ALIGN,)
    launch(early, True, True)
    expand_slab[...] = expand_f[...].astype(BF)
    reduce_slab[...] = reduce_f[...].astype(BF)
    for block, part in fold_rows(align_f, *shapes[ALIGN]):
        align_slab[:, block * 128 : block * 128 + 128] = part.astype(BF)
    late = (EXPAND, REDUCE, ALIGN)

    def turn_of(group, turn):
        if 1 <= turn <= 3:
            peer_turn(group, turn)
        if 1 <= turn <= 4:
            near_turn(group, turn - 1)
        if 2 <= turn <= 5:
            far_turn(group, turn - 2)

    launch(late, True, False)
    for turn in range(1, 6):
        turn_of(early, turn)
    launch(late, False, True)
    for step in range(4):
        pair_turn((TABLE,), step)
    settle((TABLE,))
    tokens_copy.wait()

    for member in range(4):
        total = jnp.zeros((8, width), F32)
        for part in range(parts):
            total = total + table[member * parts + part, whole : whole + 8, :].astype(F32)
        norms[member : member + 1, :] = total[1:2, :]

    def embed(index, carry):
        span = pl.ds(pl.multiple_of(index * 256, 256), 256)
        entries = table.shape[0] * table.shape[1]
        picks = lax.broadcasted_iota(jnp.int32, (256, entries), 1) == patch[span, :]
        found = contract(picks.astype(BF), table[...].reshape(entries, width), 1, 0)
        values = tokens[span, :].astype(F32) + found
        residual[span, :] = values
        normed_one[span, :] = layer_norm(values, norms[0:1, :], norms[1:2, :]).astype(BF)
        return carry

    lax.fori_loop(0, rows // 256, embed, 0)
    for step in range(4):
        pair_turn((ENTRY, EXIT), step)
    settle((ENTRY, EXIT))

    saves = []

    def save(source, target):
        copy = pltpu.make_async_copy(source, target, save_sem.at[len(saves)])
        copy.start()
        saves.append(copy)

    save(entry, entry_out)
    save(exit_low, exit_out)
    save(norms, norms_out)
    save(segment, segment_out)
    save(residual, residual_out)
    save(normed_one, normed_one_out)

    def project(index, carry):
        span = pl.ds(pl.multiple_of(index * 256, 256), 256)
        weight = entry[:, :, span].reshape(width, 256)
        joint[:, span] = contract(normed_one[...], weight, 1, 0).astype(BF)
        return carry

    lax.fori_loop(0, 3 * width // 256, project, 0)
    save(joint, joint_out)

    def service(group, turn):
        @pl.when(turn <= 4)
        def _():
            near_turn(group, turn - 1)

        @pl.when(jnp.logical_and(turn >= 2, turn <= 5))
        def _():
            far_turn(group, turn - 2)

        @pl.when(turn <= 3)
        def _():
            peer_turn(group, turn)

    def attend_pair(index, carry):
        start = pl.multiple_of(index * 128, 128)
        here = pl.ds(start, 128)
        whole_keys = joint[:, pl.ds(start + width, 128)]
        values = joint[:, pl.ds(start + 2 * width, 128)]
        keys = []
        for head in (0, 1):
            mine, same = lane_marks(head, segment[...])
            keys.append(jnp.where(mine, whole_keys, jnp.where(same, 0.0, -1e30).astype(BF)))

        def chunk(step, inner):
            span = pl.ds(pl.multiple_of(step * 256, 256), 256)
            lane = lax.broadcasted_iota(jnp.int32, (256, 128), 1)
            scaled = joint[span, here] * BF(HD**-0.5)
            found = []
            logs = totals[span, :]
            for head in (0, 1):
                mine, same = lane_marks(head, segment[span, :])
                queries = jnp.where(mine, scaled, same.astype(BF))
                scores = contract(queries, keys[head], 1, 1)
                peak = jnp.max(scores, axis=1, keepdims=True)
                raised = jnp.exp(scores - peak)
                total = jnp.sum(raised, axis=1, keepdims=True)
                attention = (raised * (1.0 / total)).astype(BF)
                found.append(contract(attention, values, 1, 0))
                logs = jnp.where(lane == index * 2 + head, peak + jnp.log(total), logs)
            totals[span, :] = logs
            attended[span, here] = jnp.where(lane < HD, found[0], found[1]).astype(BF)
            return inner

        lax.fori_loop(0, rows // 256, chunk, 0)

        @pl.when(lax.rem(index, 2) == 0)
        def _():
            service(late, index // 2 + 1)

        return carry

    lax.fori_loop(0, width // 128, attend_pair, 0)
    save(attended, attended_out)
    save(totals, totals_out)

    def leave(index, carry):
        span = pl.ds(pl.multiple_of(index * 256, 256), 256)
        weight = exit_low[...].reshape(width, width)
        values = residual[span, :] + contract(attended[span, :], weight, 1, 0)
        feed[span, :] = values
        normed_two[span, :] = layer_norm(values, norms[2:3, :], norms[3:4, :]).astype(BF)
        return carry

    saves[4].wait()
    lax.fori_loop(0, rows // 256, leave, 0)
    def keep(index, carry):
        span = pl.ds(pl.multiple_of(index * 256, 256), 256)
        residual[span, :] = feed[span, :]
        return carry

    lax.fori_loop(0, rows // 256, keep, 0)
    save(residual, middle_out)
    save(normed_two, normed_two_out)

    plane = width // expand_slab.shape[0]

    def feed_level(step, carry):
        level = route.level(step) // 4
        pair_turn((EXPAND, REDUCE), step)

        @pl.when(step == 0)
        def _():
            settle((EXPAND, REDUCE))

        slot = lax.rem(step, 2)

        @pl.when(step >= 2)
        def _():
            for copy in outgoing(slot, 0):
                copy.wait()

        slabs_here = pl.ds(level * plane, plane)

        def rows_block(index, inner):
            span = pl.ds(pl.multiple_of(index * 256, 256), 256)
            up = wide[slabs_here].reshape(width, width)
            values = contract(normed_two[span, :], up, 1, 1)
            share = 0.5 + 0.5 * lax.erf(values * (0.5**0.5))
            lifted = (values * share).astype(BF)
            act[slot, span, :] = lifted
            bell = jnp.exp(values * values * -0.5) * (0.5 / math.pi) ** 0.5
            slope[slot, span, :] = share + values * bell
            down = narrow[slabs_here].reshape(width, width)
            feed[span, :] += contract(lifted, down, 1, 0)
            return inner

        lax.fori_loop(0, rows // 256, rows_block, 0)
        for copy in outgoing(slot, level):
            copy.start()

        @pl.when(step <= 1)
        def _():
            service(late, step + 4)

        return carry

    def outgoing(number, level):
        hidden = pl.ds(pl.multiple_of(level * width, width), width)
        return (
            pltpu.make_async_copy(act.at[number], act_out.at[:, hidden], act_sem.at[0, number]),
            pltpu.make_async_copy(slope.at[number], slope_out.at[:, hidden], act_sem.at[1, number]),
        )

    lax.fori_loop(0, 4, feed_level, 0)
    save(wide, expand_out)
    save(narrow, reduce_out)

    def close(index, carry):
        span = pl.ds(pl.multiple_of(index * 256, 256), 256)
        low[span, :] = feed[span, :].astype(BF)
        return carry

    lax.fori_loop(0, rows // 256, close, 0)
    save(low, low_out)
    for step in range(4):
        pair_turn(last, step)
    settle(last)
    for number in (0, 1):
        for copy in outgoing(number, 0):
            copy.wait()
    for copy in saves[:4] + saves[5:]:
        copy.wait()

    def sent(slot, carry):
        for piece in range(len(shapes)):
            copy_to(slabs[piece], piece, route.me, near, slot).wait_send()
        return carry

    lax.fori_loop(0, 31, sent, 0)


def gather_forward(shards, norm, tokens, kept, lengths, owners, shapes, devices):
    rows, width = tokens.shape
    hidden = shapes[EXPAND][0] * devices

    def shape(dims, kind=BF):
        return jax.ShapeDtypeStruct(dims, kind)

    pieces = (ENTRY, EXIT, EXPAND, REDUCE, ALIGN)
    flat = (rows, width)
    outs = [shape((devices,) + shapes[piece]) for piece in pieces] + [
        shape((8, width), F32),
        shape(flat, F32),
        shape(flat),
        shape((rows, 3 * width)),
        shape(flat),
        shape(flat, F32),
        shape(flat),
        shape((rows, hidden)),
        shape((rows, hidden), F32),
        shape(flat),
        shape((rows, 128), F32),
        shape((rows, 1), jnp.int32),
    ]
    scratch = (
        [pltpu.VMEM(dims, BF) for dims in shapes]
        + [pltpu.VMEM((devices,) + shapes[piece], BF) for piece in (TABLE, ENTRY, EXIT)]
        + [
            pltpu.VMEM((devices,) + shapes[EXPAND], BF),
            pltpu.VMEM((devices,) + shapes[REDUCE], BF),
            pltpu.VMEM(flat, BF),
            pltpu.VMEM((8, width), F32),
            pltpu.VMEM(flat, F32),
            pltpu.VMEM(flat, BF),
            pltpu.VMEM((rows, 3 * width), BF),
            pltpu.VMEM(flat, BF),
            pltpu.VMEM(flat, F32),
            pltpu.VMEM(flat, BF),
            pltpu.VMEM((2,) + flat, BF),
            pltpu.VMEM((2,) + flat, F32),
            pltpu.VMEM(flat, BF),
            pltpu.VMEM((rows, 128), F32),
            pltpu.VMEM((rows, 1), jnp.int32),
            pltpu.VMEM((rows, 1), jnp.int32),
            pltpu.SemaphoreType.DMA((6, 31)),
            pltpu.SemaphoreType.DMA((6, devices)),
            pltpu.SemaphoreType.DMA((6,)),
            pltpu.SemaphoreType.DMA((16,)),
            pltpu.SemaphoreType.DMA((16,)),
            pltpu.SemaphoreType.DMA((2, 2)),
        ]
    )
    return pl.pallas_call(
        functools.partial(forward_kernel, shapes),
        out_shape=outs,
        in_specs=[ANY] + [VMEM] * 10,
        out_specs=[ANY] * len(outs),
        scratch_shapes=scratch,
        compiler_params=pltpu.CompilerParams(
            collective_id=0, has_side_effects=True, vmem_limit_bytes=58 * MIB
        ),
        name="gather_forward",
    )(tokens, kept, lengths, owners, *shards, norm)


def norm_back(values, slope, gain):
    center = values - jnp.mean(values, axis=-1, keepdims=True)
    spread = jnp.mean(center * center, axis=-1, keepdims=True)
    scale = lax.rsqrt(spread + LN_EPS)
    unit = center * scale
    scaled = slope * gain
    level = jnp.mean(scaled, axis=-1, keepdims=True)
    tilt = jnp.mean(scaled * unit, axis=-1, keepdims=True)
    return scale * (scaled - level - unit * tilt), slope * unit


def backward_kernel(shapes, *refs):
    count = len(shapes)
    (
        kept,
        segment,
        norms,
        norm_weight,
        norm_first,
        norm_second,
        cot_out_hbm,
        cot_align_hbm,
        entry_hbm,
        exit_hbm,
        expand_hbm,
        reduce_hbm,
        align_hbm,
        residual_hbm,
        normed_one_hbm,
        joint_hbm,
        attended_hbm,
        middle_hbm,
        normed_two_hbm,
        act_hbm,
        slope_hbm,
        low_hbm,
        totals_hbm,
    ) = refs[:23]
    states = [refs[23 + 3 * piece : 26 + 3 * piece] for piece in range(count)]
    refs = refs[23 + 3 * count :]
    outs = refs[:count]
    norm_out, sums_out, aligned_out, token_out = refs[count : 4 + count]
    refs = refs[4 + count :]
    grads, refs = refs[:count], refs[count:]
    from_pair, refs = refs[:count], refs[count:]
    from_far, refs = refs[:count], refs[count:]
    from_near, refs = refs[:count], refs[count:]
    from_peer, refs = refs[:count], refs[count:]
    (
        wide_b,
        spare,
        act,
        expand,
        reduce,
        normed_two,
        grad_feed,
        grad_out,
        grad_two,
        slope,
        query_sum,
        norm_sums,
        held,
        table_first,
        table_second,
        table_third,
        send_sem,
        pair_sem,
        far_sem,
        near_sem,
        peer_sem,
        load_sem,
        save_sem,
        state_sem,
        held_sem,
        sums_sem,
    ) = refs
    rows, width = grad_out.shape
    align_width = cot_align_hbm.shape[1]
    route = Route()
    core = route.core
    near, far, pair = (route.near, core), (route.far, core), (route.dp, 1 - core)

    def load(source, target, number):
        copy = pltpu.make_async_copy(source, target, load_sem.at[number])
        copy.start()
        return copy

    align_low = wide_b.at[:, pl.ds(0, align_width)]
    cot_align = wide_b.at[:, pl.ds(align_width, align_width)]
    cot_align_copy = load(cot_align_hbm, cot_align, 0)
    align_copy = load(align_hbm, align_low, 1)
    low_copy = load(low_hbm, act, 2)
    cot_out_copy = load(cot_out_hbm, spare, 3)
    normed_two_copy = load(normed_two_hbm, normed_two, 4)
    arrive = greet(route.partners + [route.corner])

    def level_rows(step):
        return pl.ds(pl.multiple_of((route.level(step) // 4) * width, width), width)

    def chunk_loads(step):
        here = level_rows(step)
        return (
            pltpu.make_async_copy(reduce_hbm.at[here, :], reduce, load_sem.at[6]),
            pltpu.make_async_copy(expand_hbm.at[here, :], expand, load_sem.at[7]),
            pltpu.make_async_copy(slope_hbm.at[:, here], slope, load_sem.at[8]),
        )

    def act_load(step):
        return pltpu.make_async_copy(act_hbm.at[:, level_rows(step)], act, load_sem.at[9])


    def copy_to(source, target, slot, piece, semaphore, partner):
        return pltpu.make_async_remote_copy(
            src_ref=source,
            dst_ref=target,
            send_sem=send_sem.at[piece, slot],
            recv_sem=semaphore,
            device_id=partner,
            device_id_type=MESH,
        )

    def landed(block, semaphore):
        pltpu.make_async_copy(block, block, semaphore).wait()

    def total(piece, dp, sources):
        landed(from_pair[piece].at[dp], pair_sem.at[piece, dp])
        found = grads[piece][dp * 2 + core].astype(F32) + from_pair[piece][dp].astype(F32)
        for block, semaphore, slot in sources:
            landed(block.at[slot], semaphore.at[piece, slot])
            found = found + block[slot].astype(F32)
        return found

    def stage_pair(piece, step):
        for base in (route.far, route.both, route.near, route.dp):
            dp = route.at(base, step)
            copy_to(
                grads[piece].at[dp * 2 + 1 - core],
                from_pair[piece].at[dp],
                dp,
                piece,
                pair_sem.at[piece, dp],
                pair,
            ).start()

    def forward_sum(piece, dp, sources, target, slot, semaphore, partner):
        grads[piece][dp * 2 + core] = total(piece, dp, sources).astype(BF)
        copy_to(
            grads[piece].at[dp * 2 + core], target, slot, piece, semaphore, partner
        ).start()

    def stage_far(piece, step):
        for side, base in enumerate((route.far, route.both)):
            slot = step * 2 + side
            forward_sum(
                piece,
                route.at(base, step),
                (),
                from_far[piece].at[slot],
                16 + slot,
                far_sem.at[piece, slot],
                far,
            )

    def stage_near(piece, step):
        forward_sum(
            piece,
            route.at(route.near, step),
            ((from_far[piece], far_sem, step * 2 + 1),),
            from_near[piece].at[step],
            24 + step,
            near_sem.at[piece, step],
            near,
        )

    def stage_peer(piece, step):
        forward_sum(
            piece,
            route.level(step),
            ((from_far[piece], far_sem, step * 2), (from_near[piece], near_sem, step)),
            from_peer[piece].at[step - 1],
            27 + step,
            peer_sem.at[piece, step - 1],
            (route.level(step), core),
        )

    def stage_own(piece):
        found = total(
            piece,
            route.dp,
            ((from_far[piece], far_sem, 0), (from_near[piece], near_sem, 0))
            + tuple((from_peer[piece], peer_sem, slot) for slot in range(3)),
        )
        if outs[piece].shape == found.shape:
            outs[piece][...] = found
            return
        blocks = found.shape[1] // 128
        lines = TABLE_ROWS - 1 if piece == TABLE else found.shape[0]
        for block in range(blocks):
            part = found[:, block * 128 : block * 128 + 128]
            outs[piece][pl.ds(block, lines, stride=blocks), :] = part[:lines]
            if piece == TABLE:
                outs[piece][pl.ds(lines * blocks + block, 1), :] = part[lines : lines + 1]
        if piece == TABLE:
            norm_sums[4:5, :] = found[lines + 1 : lines + 2] + found[lines + 2 : lines + 3]

    def each(stage, pieces, first=0):
        def body(turn, carry):
            for piece in pieces:
                stage(piece, turn)
            return carry

        lax.fori_loop(first, 4, body, 0)

    def flow(piece, turn):
        for late, stage in enumerate((stage_far, stage_near, stage_peer)):
            step = 3 - (turn - late)
            lowest = 1 if stage is stage_peer else 0

            @pl.when(jnp.logical_and(step >= lowest, step <= 3))
            def _():
                stage(piece, step)


    norm_sums[...] = jnp.zeros_like(norm_sums)
    cot_align_copy.wait()
    align_copy.wait()
    low_copy.wait()
    cot_out_copy.wait()
    for copy in chunk_loads(3):
        copy.start()

    def head_rows(index, carry):
        span = pl.ds(pl.multiple_of(index * 256, 256), 256)
        keep = segment[span, :] > 0
        slopes = jnp.where(keep, cot_align[span, :], jnp.zeros((256, align_width), BF))
        cot_align[span, :] = slopes
        found = contract(slopes, align_low[...], 1, 1)
        found = found + jnp.where(keep, spare[span, :].astype(F32), 0.0)
        grad_out[span, :] = found
        grad_feed[span, :] = found.astype(BF)
        return carry

    lax.fori_loop(0, rows // 256, head_rows, 0)

    def head_grads(index, carry):
        span = pl.ds(pl.multiple_of(index * 384, 384), 384)
        found = contract(act[:, span], cot_align[...], 0, 0).astype(BF)
        slabs = 384 // shapes[ALIGN][0]
        grads[ALIGN][pl.ds(index * slabs, slabs)] = found.reshape((slabs,) + shapes[ALIGN])
        return carry

    lax.fori_loop(0, width // 384, head_grads, 0)
    arrive()
    each(stage_pair, (ALIGN,))

    def head_out(index, carry):
        span = pl.ds(pl.multiple_of(index * 256, 256), 256)
        result = contract(act[span, :], align_low[...], 1, 0).astype(BF)
        cot_align[span, :] = result
        return carry

    lax.fori_loop(0, rows // 256, head_out, 0)
    aligned_copy = pltpu.make_async_copy(cot_align, aligned_out, save_sem.at[0])
    aligned_copy.start()
    act_load(3).start()
    normed_two_copy.wait()


    def feed_back(turn, carry):
        step = 3 - turn
        for copy in chunk_loads(step):
            copy.wait()

        def rows_block(index, inner):
            span = pl.ds(pl.multiple_of(index * 256, 256), 256)
            found = contract(grad_feed[span, :], reduce[...], 1, 1)
            before = (found * slope[span, :]).astype(BF)
            spare[span, :] = before
            part = contract(before, expand[...], 1, 0)

            @pl.when(turn == 0)
            def _():
                grad_two[span, :] = part

            @pl.when(turn > 0)
            def _():
                grad_two[span, :] += part

            return inner

        lax.fori_loop(0, rows // 256, rows_block, 0)

        @pl.when(turn < 3)
        def _():
            for copy in chunk_loads(step - 1):
                copy.start()

        @pl.when(turn == 3)
        def _():
            pltpu.make_async_copy(middle_hbm, slope, load_sem.at[8]).start()
            pltpu.make_async_copy(exit_hbm, expand, load_sem.at[7]).start()

        @pl.when(turn == 0)
        def _():
            each(stage_far, (ALIGN,))

        @pl.when(turn > 0)
        def _():
            feed_stage(stage_far, step + 1)

        act_load(step).wait()
        per = 384 // shapes[EXPAND][0]
        plane = (route.level(step) // 4) * (width // shapes[EXPAND][0])

        def slabs_block(index, inner):
            span = pl.ds(pl.multiple_of(index * 384, 384), 384)
            here = pl.ds(plane + index * per, per)
            found = contract(act[:, span], grad_feed[...], 0, 0).astype(BF)
            grads[REDUCE][here] = found.reshape((per,) + shapes[REDUCE])
            found = contract(spare[:, span], normed_two[...], 0, 0).astype(BF)
            grads[EXPAND][here] = found.reshape((per,) + shapes[EXPAND])
            return inner

        lax.fori_loop(0, width // 384, slabs_block, 0)

        @pl.when(turn < 3)
        def _():
            act_load(step - 1).start()

        for piece in (REDUCE, EXPAND):
            stage_pair(piece, step)

        return carry

    def feed_stage(stage, step):
        for piece in (REDUCE, EXPAND):
            stage(piece, step)

    lax.fori_loop(0, 4, feed_back, 0)
    aligned_copy.wait()
    joint_copy = load(joint_hbm, wide_b, 5)
    attended_copy = load(attended_hbm, normed_two, 2)
    normed_one_copy = load(normed_one_hbm, act, 9)
    pltpu.make_async_copy(middle_hbm, slope, load_sem.at[8]).wait()
    pltpu.make_async_copy(exit_hbm, expand, load_sem.at[7]).wait()


    def leave_back(index, carry):
        span = pl.ds(pl.multiple_of(index * 256, 256), 256)
        slopes = grad_two[span, :]
        through, gains = norm_back(slope[span, :], slopes, norms[2:3, :])
        norm_sums[2:3, :] += jnp.sum(gains, axis=0, keepdims=True)
        norm_sums[3:4, :] += jnp.sum(slopes, axis=0, keepdims=True)
        found = grad_out[span, :] + through
        grad_out[span, :] = found
        branch = found.astype(BF)
        grad_feed[span, :] = branch
        reduce[span, :] = contract(branch, expand[...], 1, 1).astype(BF)
        return carry

    lax.fori_loop(0, rows // 256, leave_back, 0)
    residual_copy = load(residual_hbm, grad_two, 0)

    def load_entry(part, target):
        return load(entry_hbm.at[:, pl.ds(part * width, width)], target, (1, 3, 6)[part])

    entry_copies = [load_entry(0, expand)]
    key_sum, value_sum, totals = (slope.at[:, pl.ds(number * 128, 128)] for number in range(3))
    totals_copy = load(totals_hbm, totals, 10)
    attended_copy.wait()

    def exit_grads(index, carry):
        span = pl.ds(pl.multiple_of(index * 384, 384), 384)
        found = contract(normed_two[:, span], grad_feed[...], 0, 0).astype(BF)
        slabs = 384 // shapes[EXIT][0]
        grads[EXIT][pl.ds(index * slabs, slabs)] = found.reshape((slabs,) + shapes[EXIT])
        return carry

    lax.fori_loop(0, width // 384, exit_grads, 0)
    each(stage_pair, (EXIT,))
    feed_stage(stage_far, 0)
    joint_copy.wait()


    scale = HD**-0.5
    totals_copy.wait()

    def split(values):
        high = values.astype(BF)
        rest = values - high.astype(F32)
        middle = rest.astype(BF)
        return high, middle, (rest - middle.astype(F32)).astype(BF)

    def with_parts(lane, values, others):
        parts = split(values)
        for number in range(3):
            others = jnp.where(lane == 8 + number, parts[number], others)
        return others

    def attend_pair(index, carry):
        start = pl.multiple_of(index * 128, 128)
        at_query = pl.ds(start, 128)
        at_key = pl.ds(start + width, 128)
        at_value = pl.ds(start + 2 * width, 128)
        key_sum[...] = jnp.zeros_like(key_sum)
        value_sum[...] = jnp.zeros_like(value_sum)
        whole_keys = wide_b[:, at_key]
        whole_values = wide_b[:, at_value]
        turned = whole_keys.astype(F32).T.astype(BF)
        lane = jnp.bitwise_and(lax.broadcasted_iota(jnp.int32, (rows, 128), 1), HD - 1)
        parted = jnp.logical_and(lane >= 8, lane < 11)
        ones = parted.astype(BF)
        keys = []
        for head in (0, 1):
            mine, same = lane_marks(head, segment[...])
            marks = jnp.where(same, 0.0, -1e30).astype(BF)
            keys.append(jnp.where(mine, whole_keys, jnp.where(parted, ones, marks)))

        def chunk(step, inner):
            span = pl.ds(pl.multiple_of(step * 256, 256), 256)
            whole_lane = lax.broadcasted_iota(jnp.int32, (256, 128), 1)
            lane = jnp.bitwise_and(whole_lane, HD - 1)
            scaled = wide_b[span, at_query] * BF(scale)
            both_slopes = reduce[span, at_query]
            zero = jnp.zeros_like(scaled)
            queries, pure_queries, slopes = [], [], []
            for head in (0, 1):
                mine, same = lane_marks(head, segment[span, :])
                log_total = jnp.sum(
                    jnp.where(whole_lane == index * 2 + head, totals[span, :], 0.0),
                    axis=1,
                    keepdims=True,
                )
                marks = with_parts(lane, -log_total, same.astype(BF))
                queries.append(jnp.where(mine, scaled, marks))
                pure_queries.append(jnp.where(mine, scaled, zero))
                slopes.append(jnp.where(mine, both_slopes, zero))
            pure_queries = jnp.concatenate(pure_queries, axis=0)
            slopes = jnp.concatenate(slopes, axis=0)
            scores = [contract(keys[head], queries[head], 1, 1) for head in (0, 1)]
            slope_attention = contract(whole_values, slopes, 1, 1)
            attentions, slope_scores = [], []
            for head in (0, 1):
                attention = jnp.exp(scores[head])
                mine = slope_attention[:, head * 256 : head * 256 + 256]
                inner_sum = jnp.sum(attention * mine, axis=0, keepdims=True)
                slope_scores.append((attention * (mine - inner_sum)).astype(BF))
                attentions.append(attention.astype(BF))
            value_sum[...] += contract(jnp.concatenate(attentions, axis=1), slopes, 1, 0)
            key_sum[...] += contract(jnp.concatenate(slope_scores, axis=1), pure_queries, 1, 0)
            for head in (0, 1):
                half = slice(head * HD, head * HD + HD)
                query_sum[half, span] = contract(turned[half, :], slope_scores[head], 1, 0)
            return inner

        lax.fori_loop(0, rows // 256, chunk, 0)
        wide_b[:, at_query] = (query_sum[...].T * scale).astype(BF)
        wide_b[:, at_key] = key_sum[...].astype(BF)
        wide_b[:, at_value] = value_sum[...].astype(BF)

        @pl.when(index == 0)
        def _():
            feed_stage(stage_near, 3)
            each(stage_far, (EXIT,))

        @pl.when(index == 1)
        def _():
            feed_stage(stage_near, 2)
            each(stage_near, (ALIGN,))

        @pl.when(index == 2)
        def _():
            feed_stage(stage_near, 1)
            feed_stage(stage_peer, 3)
            each(stage_near, (EXIT,))

        @pl.when(index == 3)
        def _():
            feed_stage(stage_near, 0)
            feed_stage(stage_peer, 2)
            each(stage_peer, (ALIGN,), 1)

        @pl.when(index == 4)
        def _():
            feed_stage(stage_peer, 1)
            each(stage_peer, (EXIT,), 1)

        return carry

    lax.fori_loop(0, width // 128, attend_pair, 0)

    table_states = (table_first, table_second, table_third)
    homes, line = {}, {}
    for number in range(3):
        for piece in (ENTRY, EXIT, ALIGN):
            start = line.get(number, 0)
            size = states[piece][number].shape[0]
            homes[piece, number] = slope.at[
                pl.ds(start, size), pl.ds(number * 128, 128)
            ]
            line[number] = start + size
        homes[TABLE, number] = table_states[number]
        for turn, piece in enumerate((EXPAND, REDUCE)):
            size = shapes[piece][0]
            homes[piece, number] = grad_two.at[pl.ds((turn * 3 + number) * size, size), :]

    def state_copy(piece, number):
        return pltpu.make_async_copy(
            states[piece][number], homes[piece, number], state_sem.at[piece, number]
        )

    def start_states(pieces):
        for piece in pieces:
            for number in range(3):
                state_copy(piece, number).start()

    entry_copies.append(load_entry(1, reduce))
    start_states((ENTRY, EXIT, ALIGN, TABLE))


    normed_one_copy.wait()
    for block in range(width // 128):
        lanes = slice(block * 128, block * 128 + 128)
        spare[lanes, :] = act[:, lanes].astype(F32).T.astype(BF)

    entry_copies.append(load_entry(2, act))

    def entry_block(index, carry):
        half = index // 3
        column = pl.ds(pl.multiple_of(lax.rem(index, 3) * width, width), width)
        line = pl.ds(pl.multiple_of(half * 384, 384), 384)
        found = contract(spare[line, :], wide_b[:, column], 1, 0).astype(BF)
        slabs = 384 // shapes[ENTRY][0]
        grads[ENTRY][pl.ds(half * slabs, slabs), :, column] = found.reshape(
            (slabs, shapes[ENTRY][0], width)
        )
        return carry

    lax.fori_loop(0, 6, entry_block, 0)
    each(stage_pair, (ENTRY,))
    for copy in entry_copies:
        copy.wait()
    residual_copy.wait()

    def enter_back(index, carry):
        span = pl.ds(pl.multiple_of(index * 256, 256), 256)
        slopes = contract(wide_b[span, 0:width], expand[...], 1, 1)
        slopes += contract(wide_b[span, width : 2 * width], reduce[...], 1, 1)
        slopes += contract(wide_b[span, 2 * width : 3 * width], act[...], 1, 1)
        through, gains = norm_back(grad_two[span, :], slopes, norms[0:1, :])
        norm_sums[0:1, :] += jnp.sum(gains, axis=0, keepdims=True)
        norm_sums[1:2, :] += jnp.sum(slopes, axis=0, keepdims=True)
        found = grad_out[span, :] + through
        grad_out[span, :] = found
        grad_feed[span, :] = found.astype(BF)
        flow(ENTRY, index)
        return carry

    lax.fori_loop(0, rows // 256, enter_back, 0)
    token_copy = pltpu.make_async_copy(grad_out, token_out, save_sem.at[1])
    token_copy.start()
    start_states((EXPAND, REDUCE))

    slabs = 4
    block_rows = slabs * TABLE_SLAB

    def table_block(index, carry):
        entries = lax.broadcasted_iota(jnp.int32, (block_rows, rows), 0) + index * block_rows
        picks = (entries == slab_places(kept[...])).astype(BF)
        found = contract(picks, grad_feed[...], 1, 0).astype(BF)
        grads[TABLE][pl.ds(index * slabs, slabs)] = found.reshape((slabs, TABLE_SLAB, width))

        @pl.when(lax.rem(index, 2) == 0)
        def _():
            flow(ENTRY, 3 + index // 2)

        return carry

    devices = grads[TABLE].shape[0]
    lax.fori_loop(0, devices // slabs, table_block, 0)
    whole = TABLE_ROWS - 1
    row_id = lax.broadcasted_iota(jnp.int32, (8, width), 0)
    for member in range(4):
        line = norm_sums[member : member + 1, :]
        high = line.astype(BF).astype(F32)
        tail = jnp.where(row_id == 1, high, jnp.where(row_id == 2, line - high, 0.0))

        def tuck(index, carry):
            slab = member * (devices // 4) + index
            kept = grads[TABLE][slab, whole : whole + 8, :].astype(F32)
            grads[TABLE][slab, whole : whole + 8, :] = jnp.where(row_id == 0, kept, tail).astype(BF)
            return carry

        lax.fori_loop(0, devices // 4, tuck, 0)
    each(stage_pair, (TABLE,))
    row_id16 = lax.broadcasted_iota(jnp.int32, (16, 128), 0)

    def squares(piece):
        for number in range(3):
            state_copy(piece, number).wait()
        weight, first, second = (homes[piece, number][...] for number in range(3))
        update = lamb_update(weight, outs[piece][...], first, second, DECAY)[2]
        note(MEMBERS.index(piece), total_square(weight), total_square(update))

    def note(member, weight_square, update_square):
        kept = held[0]
        kept = jnp.where(row_id16 == member, weight_square, kept)
        held[0] = jnp.where(row_id16 == 8 + member, update_square, kept)

    held[0] = jnp.zeros_like(held[0])
    for turn in range(3):
        flow(TABLE, turn)
    for piece in (ALIGN, REDUCE, EXPAND, EXIT):
        stage_own(piece)
        squares(piece)
    for turn in range(3, 6):
        flow(TABLE, turn)
    stage_own(ENTRY)
    squares(ENTRY)
    stage_own(TABLE)
    squares(TABLE)
    norm_row = norm_sums[4:5, :]
    share = lax.rem(route.me, width // NORM_LANES)
    norm_slope = jnp.zeros((1, NORM_LANES), F32)
    for number in range(width // NORM_LANES):
        part = norm_row[:, number * NORM_LANES : (number + 1) * NORM_LANES]
        norm_slope = jnp.where(share == number, part, norm_slope)
    norm_out[...] = norm_slope
    update = lamb_update(norm_weight[...], norm_slope, norm_first[...], norm_second[...], 0.0)[2]
    note(len(MEMBERS), total_square(norm_weight[...]), total_square(update))


    def sums_to(slot, target, partner, number):
        copy = pltpu.make_async_remote_copy(
            src_ref=held.at[slot],
            dst_ref=held.at[target],
            send_sem=sums_sem.at[number],
            recv_sem=held_sem.at[target],
            device_id=partner,
            device_id_type=MESH,
        )
        copy.start()
        return copy

    def sums_from(slot):
        pltpu.make_async_copy(held.at[slot], held.at[slot], held_sem.at[slot]).wait()

    sums_sent = [sums_to(0, 1, pair, 0)]
    sums_from(1)
    column = route.column
    held[2 + column] = held[0] + held[1]
    plane = [(route.near, core), (route.far, core), route.corner]
    for number, partner in enumerate(plane):
        sums_sent.append(sums_to(2 + column, 2 + column, partner, 1 + number))
    for partner, _ in plane:
        sums_from(2 + lax.rem(partner, 4))
    held[6 + route.z] = held[2] + held[3] + held[4] + held[5]
    for number, peer in enumerate(route.peers):
        sums_sent.append(sums_to(6 + route.z, 6 + route.z, (peer, core), 4 + number))
    for peer in route.peers:
        sums_from(6 + peer // 4)
    sums_out[...] = held[6] + held[7] + held[8] + held[9]
    for copy in sums_sent:
        copy.wait_send()

    def sent(slot, carry):
        for piece in range(count):
            copy_to(
                grads[piece].at[0], from_pair[piece].at[0], slot, piece, pair_sem.at[piece, 0], pair
            ).wait_send()
        return carry

    lax.fori_loop(0, 31, sent, 0)
    token_copy.wait()


def scatter_backward(kept, segment, norms, norm_states, arrays, states, shapes, devices):
    rows, width = arrays[0].shape
    align_width = arrays[1].shape[1]
    dps = devices // 2
    flat = (rows, width)

    def buffers(slots):
        return [pltpu.VMEM((slots,) + dims, BF) for dims in shapes]

    count = len(shapes)
    scratch = (
        buffers(devices)
        + buffers(dps)
        + buffers(8)
        + buffers(4)
        + buffers(3)
        + [pltpu.VMEM((rows, 3 * width), BF)]
        + [pltpu.VMEM(flat, BF)] * 6
        + [pltpu.VMEM(flat, F32)] * 3
        + [
            pltpu.VMEM((128, rows), F32),
            pltpu.VMEM((8, width), F32),
            pltpu.VMEM((10, 16, 128), F32),
        ]
        + [pltpu.VMEM(states[3 * TABLE].shape, F32)] * 3
        + [
            pltpu.SemaphoreType.DMA((count, 31)),
            pltpu.SemaphoreType.DMA((count, dps)),
            pltpu.SemaphoreType.DMA((count, 8)),
            pltpu.SemaphoreType.DMA((count, 4)),
            pltpu.SemaphoreType.DMA((count, 3)),
            pltpu.SemaphoreType.DMA((11,)),
            pltpu.SemaphoreType.DMA((2,)),
            pltpu.SemaphoreType.DMA((count, 3)),
            pltpu.SemaphoreType.DMA((10,)),
            pltpu.SemaphoreType.DMA((7,)),
        ]
    )
    outs = [jax.ShapeDtypeStruct(state.shape, F32) for state in states[::3]] + [
        jax.ShapeDtypeStruct((1, NORM_LANES), F32),
        jax.ShapeDtypeStruct((16, 128), F32),
        jax.ShapeDtypeStruct((rows, align_width), BF),
        jax.ShapeDtypeStruct(flat, F32),
    ]
    return pl.pallas_call(
        functools.partial(backward_kernel, shapes),
        out_shape=outs,
        in_specs=[VMEM] * 6 + [ANY] * (len(arrays) + len(states)),
        out_specs=[VMEM] * (count + 2) + [ANY] * 2,
        scratch_shapes=scratch,
        compiler_params=pltpu.CompilerParams(
            collective_id=1, has_side_effects=True, vmem_limit_bytes=60 * MIB
        ),
        name="scatter_backward",
    )(kept, segment, norms, *norm_states, *arrays, *states)


def lamb_update(weight, gradient, first, second, decay):
    new_first = BETA_ONE * first + (1.0 - BETA_ONE) * gradient
    new_second = BETA_TWO * second + (1.0 - BETA_TWO) * gradient * gradient
    update = new_first / (jnp.sqrt(new_second) + ADAM_EPS) + decay * weight
    return new_first, new_second, update


def total_square(values):
    return jnp.sum(jnp.sum(values * values, axis=1, keepdims=True), axis=0, keepdims=True)


def finish_kernel(count, *refs):
    segment, sums, norm_slope = refs[:3]
    norm_states = refs[3:6]
    slopes_hbm = refs[6 : 6 + count]
    refs = refs[6 + count :]
    states, refs = refs[: 3 * count], refs[3 * count :]
    low_hbm, aligned_hbm, token_hbm = refs[:3]
    outs, refs = refs[3 : 3 + 3 * count], refs[3 + 3 * count :]
    norm_outs = refs[:3]
    block_out, aligned_out, token_out, stats = refs[3:7]
    refs = refs[7:]
    held, refs = refs[: 3 * count], refs[3 * count :]
    made, refs = refs[: 3 * count], refs[3 * count :]
    slopes, refs = refs[:count], refs[count:]
    slope_sem, low, aligned, token, in_sem, out_sem, row_sem = refs
    slope_loads = [
        pltpu.make_async_copy(slopes_hbm[piece], slopes[piece], slope_sem.at[piece])
        for piece in range(count)
    ]
    for copy in slope_loads:
        copy.start()
    token_copy = pltpu.make_async_copy(token_hbm, token, row_sem.at[0])
    token_copy.start()
    low_copy = pltpu.make_async_copy(low_hbm, low, row_sem.at[1])
    low_copy.start()
    aligned_copy = pltpu.make_async_copy(aligned_hbm, aligned, row_sem.at[2])
    aligned_copy.start()
    loads = [
        pltpu.make_async_copy(states[number], held[number], in_sem.at[number])
        for number in range(3 * count)
    ]
    for copy in loads:
        copy.start()

    def trust_of(member):
        weight_square = sums[member : member + 1, :]
        update_square = sums[8 + member : 9 + member, :]
        return jnp.sqrt(weight_square) / jnp.sqrt(update_square + TINY)

    lane = lax.broadcasted_iota(jnp.int32, (1, 128), 1)
    lines = [jnp.zeros((1, 128), F32)] * 3
    for member in range(len(MEMBERS) + 1):
        found = (
            trust_of(member),
            jnp.sqrt(sums[member : member + 1, :]),
            jnp.sqrt(sums[8 + member : 9 + member, :]),
        )
        lines = [jnp.where(lane == member, new, line) for new, line in zip(found, lines)]
    for row, line in enumerate(lines):
        stats[row : row + 1, :] = line[:, : stats.shape[1]]
    weight, first, second = (state[...] for state in norm_states)
    made_norm = lamb_update(weight, norm_slope[...], first, second, 0.0)
    norm_outs[0][...] = made_norm[0]
    norm_outs[1][...] = made_norm[1]
    step = RATE * trust_of(len(MEMBERS))[:, :NORM_LANES] * made_norm[2]
    norm_outs[2][...] = weight - step
    token_copy.wait()
    token_copy = pltpu.make_async_copy(token, token_out, row_sem.at[0])
    token_copy.start()
    low_copy.wait()
    keep = segment[...] > 0
    low[...] = jnp.where(keep, low[...], jnp.zeros_like(low))
    low_copy = pltpu.make_async_copy(low, block_out, row_sem.at[1])
    low_copy.start()
    aligned_copy.wait()
    aligned[...] = jnp.where(keep, aligned[...], jnp.zeros_like(aligned))
    aligned_copy = pltpu.make_async_copy(aligned, aligned_out, row_sem.at[2])
    aligned_copy.start()
    saves = []
    for member, piece in enumerate(MEMBERS):
        trust = trust_of(member)
        for number in range(3):
            loads[3 * piece + number].wait()
        slope_loads[piece].wait()
        weight, first, second = (held[3 * piece + number][...] for number in range(3))
        new_first, new_second, update = lamb_update(
            weight, slopes[piece][...], first, second, DECAY
        )
        wide = trust if update.shape[1] == 128 else trust[:, 0:1]
        made[3 * piece][...] = new_first
        made[3 * piece + 1][...] = new_second
        made[3 * piece + 2][...] = weight - RATE * wide * update
        for number in range(3):
            copy = pltpu.make_async_copy(
                made[3 * piece + number], outs[3 * piece + number], out_sem.at[3 * piece + number]
            )
            copy.start()
            saves.append(copy)
    for copy in saves + [low_copy, aligned_copy, token_copy]:
        copy.wait()


def finish(segment, sums, norm_slope, norm_states, slopes, states, rows):
    count = len(slopes)
    low, aligned, token = rows

    def like(array):
        return jax.ShapeDtypeStruct(array.shape, array.dtype)

    outs = (
        [like(state) for state in states]
        + [like(state) for state in norm_states]
        + [like(low), like(aligned), like(token)]
        + [jax.ShapeDtypeStruct((3, len(MEMBERS) + 1), F32)]
    )
    return pl.pallas_call(
        functools.partial(finish_kernel, count),
        out_shape=outs,
        in_specs=[VMEM] * 6 + [ANY] * (4 * count + 3),
        out_specs=[ANY] * (3 * count) + [VMEM] * 3 + [ANY] * 3 + [VMEM],
        scratch_shapes=[pltpu.VMEM(state.shape, F32) for state in states] * 2
        + [pltpu.VMEM(slope.shape, F32) for slope in slopes]
        + [
            pltpu.SemaphoreType.DMA((count,)),
            pltpu.VMEM(low.shape, BF),
            pltpu.VMEM(aligned.shape, BF),
            pltpu.VMEM(token.shape, F32),
            pltpu.SemaphoreType.DMA((3 * count,)),
            pltpu.SemaphoreType.DMA((3 * count,)),
            pltpu.SemaphoreType.DMA((3,)),
        ],
        compiler_params=pltpu.CompilerParams(vmem_limit_bytes=60 * MIB),
        name="finish",
    )(segment, sums, norm_slope, *norm_states, *slopes, *states, low, aligned, token)


def moments_kernel(decays, *refs):
    count = len(decays)
    sums = refs[7 * count]
    row = lax.broadcasted_iota(jnp.int32, (16, 128), 0)
    found = jnp.zeros((16, 128), F32)
    for member, decay in enumerate(decays):
        weight, gradient, first, second = refs[4 * member : 4 * member + 4]
        new_first_ref, new_second_ref, update_ref = refs[
            4 * count + 3 * member : 4 * count + 3 * member + 3
        ]
        slope = gradient[...]
        new_first = BETA_ONE * first[...] + (1.0 - BETA_ONE) * slope
        new_second = BETA_TWO * second[...] + (1.0 - BETA_TWO) * slope * slope
        update = new_first / (jnp.sqrt(new_second) + ADAM_EPS) + decay * weight[...]
        new_first_ref[...] = new_first
        new_second_ref[...] = new_second
        update_ref[...] = update
        found = jnp.where(row == member, jnp.sum(weight[...] * weight[...]), found)
        found = jnp.where(row == 8 + member, jnp.sum(update * update), found)
    sums[...] = found


def moments(members, decays):
    shapes = [jax.ShapeDtypeStruct(member[0].shape, F32) for member in members]
    outs = [shape for shape in shapes for _ in range(3)]
    flat = [array for member in members for array in member]
    return pl.pallas_call(
        functools.partial(moments_kernel, decays),
        out_shape=outs + [jax.ShapeDtypeStruct((16, 128), F32)],
        in_specs=[VMEM] * len(flat),
        out_specs=[VMEM] * (len(outs) + 1),
        compiler_params=pltpu.CompilerParams(vmem_limit_bytes=40 * MIB),
        name="moments",
    )(*flat)


def step_kernel(count, *refs):
    sums = refs[0]
    for member in range(count):
        weight, update = refs[1 + 2 * member : 3 + 2 * member]
        weight_square = sums[member : member + 1, :]
        update_square = sums[8 + member : 9 + member, :]
        trust = jnp.sqrt(weight_square) / jnp.sqrt(update_square + TINY)
        if weight.shape[1] % 128 == 0:
            trust = jnp.concatenate([trust] * (weight.shape[1] // 128), axis=1)
        else:
            trust = trust[:, : weight.shape[1]]
        refs[1 + 2 * count + member][...] = weight[...] - RATE * trust * update[...]


def take_step(sums, pairs):
    count = len(pairs)
    return pl.pallas_call(
        functools.partial(step_kernel, count),
        out_shape=[jax.ShapeDtypeStruct(weight.shape, F32) for weight, _ in pairs],
        in_specs=[VMEM] * (1 + 2 * count),
        out_specs=[VMEM] * count,
        compiler_params=pltpu.CompilerParams(vmem_limit_bytes=40 * MIB),
        name="take_step",
    )(sums, *[array for pair in pairs for array in pair])


def as_rows(flat):
    if flat.ndim == 2:
        return flat
    lanes = max(size for size in range(1, 129) if flat.shape[0] % size == 0)
    return flat.reshape(-1, lanes)


def local(
    tokens,
    kept_patches,
    clip_lengths,
    clip_device,
    cot_output,
    cot_aligned,
    entry_weight,
    entry_first,
    entry_second,
    exit_weight,
    exit_first,
    exit_second,
    align_weight,
    align_first,
    align_second,
    expand_weight,
    expand_first,
    expand_second,
    reduce_weight,
    reduce_first,
    reduce_second,
    position_table,
    position_first,
    position_second,
    norm_params,
    norm_first,
    norm_second,
):
    rows, width = tokens.shape
    align_width = cot_aligned.shape[1]
    axes = ("dp", "tensor")
    pair = lax.axis_size("tensor")
    devices = lax.axis_size("dp") * pair
    hidden = expand_weight.shape[0] * devices
    positions = position_table.shape[0] * devices // width
    routed = devices == 2 * ROUTED_DP and pair == 2
    device = lax.axis_index("dp") * pair + lax.axis_index("tensor")
    shapes = (
        (TABLE_SLAB, width),
        (width // devices, 3 * width),
        (width // devices, width),
        (hidden // devices, width),
        (hidden // devices, width),
        (width // devices, align_width),
    )
    wholes = (
        (positions, width),
        (width, 3 * width),
        (width, width),
        (hidden, width),
        (hidden, width),
        (width, align_width),
    )
    masters = (position_table, entry_weight, exit_weight, expand_weight, reduce_weight, align_weight)
    triples = {
        TABLE: (position_table, position_first, position_second),
        ENTRY: (entry_weight, entry_first, entry_second),
        EXIT: (exit_weight, exit_first, exit_second),
        EXPAND: (expand_weight, expand_first, expand_second),
        REDUCE: (reduce_weight, reduce_first, reduce_second),
        ALIGN: (align_weight, align_first, align_second),
    }
    norms = (norm_params, norm_first, norm_second)
    if routed:
        states = [as_rows(array) for piece in range(6) for array in triples[piece]]
        norm_states = [array.reshape(1, -1) for array in norms]
        kept = kept_patches.reshape(1, -1)
        found = gather_forward(
            states[::3],
            norm_states[0],
            tokens,
            kept,
            clip_lengths.reshape(1, -1),
            clip_device.reshape(1, -1),
            shapes,
            devices,
        )
        lows = [block.reshape(-1, block.shape[2]) for block in found[:5]]
        out_low, segment = found[14], found[16]
        arrays = (cot_output, cot_aligned) + tuple(lows) + tuple(found[6:16])
        results = scatter_backward(
            kept, segment, found[5], norm_states, arrays, states, shapes, devices
        )
        norm_slope, sums, align_rows, token_grad = results[6:]
        done = finish(
            segment,
            sums,
            norm_slope,
            norm_states,
            results[:6],
            states,
            (out_low, align_rows, token_grad),
        )
        outputs = list(done[21:24])
        for piece in MEMBERS:
            for number in range(3):
                outputs.append(done[3 * piece + number].reshape(triples[piece][number].shape))
        outputs = outputs + [array.reshape(-1) for array in done[18:21]] + [done[24]]
        return tuple(outputs)

    segment, valid_rows = row_layout(clip_lengths, clip_device, device, rows)
    segment_column = segment[:, None]
    valid_column = valid_rows[:, None]
    lows = [
        lax.all_gather(master.astype(BF).reshape(-1), axes, axis=0, tiled=True).reshape(whole)
        for master, whole in zip(masters, wholes)
    ]
    norm_low = lax.all_gather(norm_params.astype(BF), axes, axis=0, tiled=True).reshape(4, width)
    patch = kept_patches
    table_low, entry_low, exit_low, expand_low, reduce_low, align_low = lows
    norm_low = norm_low.astype(F32)
    residual = tokens.astype(F32) + jnp.take(table_low, patch, axis=0).astype(F32)
    normed_one = layer_norm(residual, norm_low[0], norm_low[1]).astype(BF)
    joint_low = contract(normed_one, entry_low, 1, 0).astype(BF)
    attended = attend(segment_column, joint_low)
    middle = residual + contract(attended, exit_low, 1, 0)
    normed_two = layer_norm(middle, norm_low[2], norm_low[3]).astype(BF)
    hidden_pre = contract(normed_two, expand_low, 1, 1)
    share = 0.5 + 0.5 * lax.erf(hidden_pre * 0.5**0.5)
    hidden_act = (hidden_pre * share).astype(BF)
    hidden_slope = share + hidden_pre * jnp.exp(-0.5 * hidden_pre * hidden_pre) * (0.5 / math.pi) ** 0.5
    out_low = (middle + contract(hidden_act, reduce_low, 1, 0)).astype(BF)
    align_rows = contract(out_low, align_low, 1, 0).astype(BF)
    cot_align_valid = jnp.where(valid_column, cot_aligned, jnp.zeros_like(cot_aligned))
    grad_align = contract(out_low, cot_align_valid, 0, 0)
    grad_out = jnp.where(valid_column, cot_output.astype(F32), 0.0) + contract(
        cot_align_valid, align_low, 1, 1
    )
    grad_feed = grad_out.astype(BF)
    grad_act = contract(grad_feed, reduce_low, 1, 1)
    grad_pre = (grad_act * hidden_slope).astype(BF)
    grad_reduce = contract(hidden_act, grad_feed, 0, 0)
    grad_expand = contract(grad_pre, normed_two, 0, 0)
    grad_two = contract(grad_pre, expand_low, 1, 0)
    through, gains = norm_back(middle, grad_two, norm_low[2])
    grad_middle = grad_out + through
    grad_branch = grad_middle.astype(BF)
    grad_exit = contract(attended, grad_branch, 0, 0)
    grad_attended = contract(grad_branch, exit_low, 1, 1).astype(BF)
    grad_parts = attend_back(segment_column, joint_low, grad_attended)
    grad_joint = jnp.concatenate([grad_parts[0], grad_parts[1], grad_parts[2]], axis=1)
    grad_entry = contract(normed_one, grad_joint, 0, 0)
    grad_one = contract(grad_joint, entry_low, 1, 1)
    through_one, gains_one = norm_back(residual, grad_one, norm_low[0])
    token_grad = grad_middle + through_one
    places = jnp.arange(positions, dtype=jnp.int32)
    picks = (patch[:, None] == places[None, :]).astype(BF)
    grad_table = contract(picks, token_grad.astype(BF), 0, 0)
    grad_norms = jnp.concatenate(
        [jnp.sum(part, axis=0) for part in (gains_one, grad_one, gains, grad_two)]
    )
    grads = (grad_table, grad_entry, grad_exit, grad_expand, grad_reduce, grad_align)
    summed = [
        lax.psum_scatter(grad.reshape(-1), axes, scatter_dimension=0, tiled=True)
        for grad in grads
    ]
    norm_sum = lax.psum_scatter(grad_norms, axes, scatter_dimension=0, tiled=True)
    block_out = jnp.where(valid_column, out_low, jnp.zeros_like(out_low))
    aligned = jnp.where(valid_column, align_rows, jnp.zeros_like(align_rows))

    def summed_like(master, index):
        return summed[index].reshape(master.shape)

    members = (
        (entry_weight, summed_like(entry_weight, ENTRY), entry_first, entry_second),
        (exit_weight, summed_like(exit_weight, EXIT), exit_first, exit_second),
        (align_weight, summed_like(align_weight, ALIGN), align_first, align_second),
        (expand_weight, summed_like(expand_weight, EXPAND), expand_first, expand_second),
        (reduce_weight, summed_like(reduce_weight, REDUCE), reduce_first, reduce_second),
        (position_table, summed_like(position_table, TABLE), position_first, position_second),
        (norm_params, norm_sum, norm_first, norm_second),
    )
    decays = (DECAY, DECAY, DECAY, DECAY, DECAY, DECAY, 0.0)
    members = [tuple(as_rows(array) for array in member) for member in members]
    found = moments(members, decays)
    sums = found[-1]
    sums = lax.psum(sums, axes)
    stepped = take_step(
        sums, [(members[member][0], found[3 * member + 2]) for member in range(len(members))]
    )
    weight_squares, update_squares = sums[0:7, 0], sums[8:15, 0]
    trust = jnp.sqrt(weight_squares) / jnp.sqrt(update_squares + TINY)
    outputs = [block_out, aligned, token_grad]
    originals = (
        entry_weight,
        exit_weight,
        align_weight,
        expand_weight,
        reduce_weight,
        position_table,
        norm_params,
    )
    for member, original in enumerate(originals):
        for array in (found[3 * member], found[3 * member + 1], stepped[member]):
            outputs.append(array.reshape(original.shape))
    outputs.append(jnp.stack((trust, jnp.sqrt(weight_squares), jnp.sqrt(update_squares))))
    return tuple(outputs)


def solution(mesh):
    both = ("dp", "tensor")
    rows, flat, whole = P(both, None), P(both), P()
    weight_specs = (flat,) * 9 + (rows,) * 6 + (flat,) * 6
    placed = (rows, flat, whole, whole, rows, rows) + weight_specs
    return jax.shard_map(
        local,
        mesh=mesh,
        in_specs=placed,
        out_specs=(rows, rows, rows) + weight_specs + (whole,),
        check_vma=False,
    )
```

```python
import functools
import math

import jax
import jax.numpy as jnp
from jax import lax
from jax.experimental import pallas as pl
from jax.experimental.pallas import tpu as pltpu
from jax.sharding import PartitionSpec as P

H = 12
HD = 64
LN_EPS = 1e-06
RATE = 0.5
BETA_ONE = 0.9
BETA_TWO = 0.98
ADAM_EPS = 1e-06
DECAY = 0.05
TINY = 1e-06
BF = jnp.bfloat16
F32 = jnp.float32
MESH = pl.DeviceIdType.MESH
ANY = pl.BlockSpec(memory_space=pl.ANY)
VMEM = pl.BlockSpec(memory_space=pltpu.VMEM)
MIB = 1 << 20

TABLE, ENTRY, EXIT, EXPAND, REDUCE, ALIGN = range(6)
MEMBERS = (ENTRY, EXIT, ALIGN, EXPAND, REDUCE, TABLE)
TABLE_ROWS = 49
TABLE_SLAB = 56
NORM_LANES = 96
ROUTED_DP = 16


def contract(left, right, left_dim, right_dim):
    return lax.dot_general(
        left, right, (((left_dim,), (right_dim,)), ((), ())), preferred_element_type=F32
    )


def layer_norm(values, gain, shift):
    center = values - jnp.mean(values, axis=-1, keepdims=True)
    spread = jnp.mean(center * center, axis=-1, keepdims=True)
    return center * lax.rsqrt(spread + LN_EPS) * gain + shift


def row_layout(clip_lengths, clip_device, device, row_count):
    mine = clip_device == device
    own_length = jnp.where(mine, clip_lengths, 0)
    starts = jnp.cumsum(own_length) - own_length
    filled = jnp.sum(own_length)
    positions = jnp.arange(row_count, dtype=jnp.int32)
    begun = mine[None, :] & (starts[None, :] <= positions[:, None])
    segment = jnp.sum(begun.astype(jnp.int32), axis=1)
    valid_rows = positions < filled
    return (jnp.where(valid_rows, segment, 0), valid_rows)


class Route:
    def __init__(self):
        dp = lax.axis_index("dp")
        core = lax.axis_index("tensor")
        z, y, x = dp // 4, (dp // 2) % 2, dp % 2
        across_y = dp + 2 - 4 * y
        across_x = dp + 1 - 2 * x
        self.dp, self.core, self.me = dp, core, dp * 2 + core
        self.z, self.column = z, y * 2 + x
        self.near = across_y * (1 - core) + across_x * core
        self.far = across_x * (1 - core) + across_y * core
        self.both = self.near + self.far - dp
        levels = [z + 1 - 2 * (z % 2), 3 - z, (z + 2) % 4]
        self.peers = [level * 4 + y * 2 + x for level in levels]
        self.partners = [(peer, core) for peer in self.peers] + [
            (self.near, core),
            (self.far, core),
            (dp, 1 - core),
        ]
        self.corner = (self.both, core)

    def level(self, step):
        high = lax.rem(self.z // 2 + step // 2, 2)
        low = lax.rem(self.z % 2 + step // 2 + step % 2, 2)
        return (high * 2 + low) * 4 + self.column

    def at(self, base, step):
        return (self.level(step) // 4) * 4 + base % 4


def greet(partners):
    barrier = pltpu.get_barrier_semaphore()
    for partner in partners:
        pl.semaphore_signal(barrier, inc=1, device_id=partner, device_id_type=MESH)
    return lambda: pl.semaphore_wait(barrier, len(partners))


def fold_rows(source, rows, columns):
    blocks = columns // 128
    for block in range(blocks):
        yield block, source[pl.ds(block, rows, stride=blocks), :]


def lane_marks(head, segment_column):
    lane = lax.broadcasted_iota(jnp.int32, (segment_column.shape[0], 128), 1)
    mine = lax.shift_right_logical(lane, 6) == head
    same = jnp.bitwise_and(lane, HD - 1) == segment_column
    return mine, same


def attend_kernel(segment, query, key, value, out):
    rows = query.shape[0]
    chunk = 256
    for head in (0, 1):
        mine, same = lane_marks(head, segment[...])
        keys = jnp.where(mine, key[...], jnp.where(same, 0.0, -1e30).astype(BF))
        queries = jnp.where(mine, query[...] * BF(HD**-0.5), same.astype(BF))
        values = value[...]
        for start in range(0, rows, chunk):
            scores = contract(queries[start : start + chunk], keys, 1, 1)
            peak = jnp.max(scores, axis=1, keepdims=True)
            raised = jnp.exp(scores - peak)
            scale = 1.0 / jnp.sum(raised, axis=1, keepdims=True)
            attention = (raised * scale).astype(BF)
            result = contract(attention, values, 1, 0).astype(BF)
            span = slice(start, start + chunk)
            if head == 0:
                out[span, :] = result
            else:
                out[span, :] = jnp.where(mine[span], result, out[span, :])


def attend(segment, joint):
    rows, width = joint.shape[0], joint.shape[1] // 3
    pairs = width // 128
    return pl.pallas_call(
        attend_kernel,
        grid=(pairs,),
        out_shape=jax.ShapeDtypeStruct((rows, width), BF),
        in_specs=[
            pl.BlockSpec((rows, 1), lambda pair: (0, 0)),
            pl.BlockSpec((rows, 128), lambda pair: (0, pair)),
            pl.BlockSpec((rows, 128), lambda pair: (0, pairs + pair)),
            pl.BlockSpec((rows, 128), lambda pair: (0, 2 * pairs + pair)),
        ],
        out_specs=pl.BlockSpec((rows, 128), lambda pair: (0, pair)),
        compiler_params=pltpu.CompilerParams(vmem_limit_bytes=40 * MIB),
        name="attend",
    )(segment, joint, joint, joint)


def attend_back_kernel(segment, query, key, value, grad, out, key_sum, value_sum):
    rows = query.shape[0]
    chunk = 256
    scale = HD**-0.5
    for head in (0, 1):
        mine, same = lane_marks(head, segment[...])
        keys = jnp.where(mine, key[...], jnp.where(same, 0.0, -1e30).astype(BF))
        scaled = query[...] * BF(scale)
        queries = jnp.where(mine, scaled, same.astype(BF))
        zero = jnp.zeros_like(scaled)
        pure_queries = jnp.where(mine, scaled, zero)
        pure_keys = jnp.where(mine, key[...], zero)
        grads = jnp.where(mine, grad[...], zero)
        values = value[...]
        for start in range(0, rows, chunk):
            span = slice(start, start + chunk)
            scores = contract(keys, queries[span], 1, 1)
            peak = jnp.max(scores, axis=0, keepdims=True)
            raised = jnp.exp(scores - peak)
            attention = raised * (1.0 / jnp.sum(raised, axis=0, keepdims=True))
            grad_values = contract(attention.astype(BF), grads[span], 1, 0)
            grad_attention = contract(values, grads[span], 1, 1)
            inner = jnp.sum(attention * grad_attention, axis=0, keepdims=True)
            grad_score = (attention * (grad_attention - inner)).astype(BF)
            grad_keys = contract(grad_score, pure_queries[span], 1, 0)
            grad_queries = contract(grad_score, pure_keys, 0, 0) * scale
            if head == 0:
                out[0, span, :] = grad_queries.astype(BF)
            else:
                out[0, span, :] = jnp.where(mine[span], grad_queries.astype(BF), out[0, span, :])
            if head == 0 and start == 0:
                key_sum[...] = grad_keys
                value_sum[...] = grad_values
            else:
                key_sum[...] += grad_keys
                value_sum[...] += grad_values
    out[1] = key_sum[...].astype(BF)
    out[2] = value_sum[...].astype(BF)


def attend_back(segment, joint, grad_attended):
    rows, width = grad_attended.shape
    pairs = width // 128
    return pl.pallas_call(
        attend_back_kernel,
        grid=(pairs,),
        out_shape=jax.ShapeDtypeStruct((3, rows, width), BF),
        in_specs=[
            pl.BlockSpec((rows, 1), lambda pair: (0, 0)),
            pl.BlockSpec((rows, 128), lambda pair: (0, pair)),
            pl.BlockSpec((rows, 128), lambda pair: (0, pairs + pair)),
            pl.BlockSpec((rows, 128), lambda pair: (0, 2 * pairs + pair)),
            pl.BlockSpec((rows, 128), lambda pair: (0, pair)),
        ],
        out_specs=pl.BlockSpec((3, rows, 128), lambda pair: (0, 0, pair)),
        scratch_shapes=[pltpu.VMEM((rows, 128), F32), pltpu.VMEM((rows, 128), F32)],
        compiler_params=pltpu.CompilerParams(vmem_limit_bytes=40 * MIB),
        name="attend_back",
    )(segment, joint, joint, joint, grad_attended)


def segments(lengths, owners, device, rows):
    count = lengths.shape[1]
    mine = owners == device
    own = jnp.broadcast_to(jnp.where(mine, lengths, 0).astype(F32), (8, count))
    before = lax.broadcasted_iota(jnp.int32, (count, count), 0)
    after = lax.broadcasted_iota(jnp.int32, (count, count), 1)
    starts = lax.dot_general(
        own,
        (before < after).astype(F32),
        (((1,), (0,)), ((), ())),
        precision=lax.Precision.HIGHEST,
        preferred_element_type=F32,
    )[0:1, :]
    filled = jnp.sum(own[0:1, :], axis=1, keepdims=True)
    place = lax.broadcasted_iota(jnp.int32, (rows, count), 0).astype(F32)
    begun = jnp.where(jnp.logical_and(mine, starts <= place), 1.0, 0.0)
    number = jnp.sum(begun, axis=1, keepdims=True)
    return jnp.where(place[:, 0:1] < filled, number, 0.0).astype(jnp.int32)


def slab_places(patch):
    return patch + lax.shift_right_logical(patch * 1338, 16) * (TABLE_SLAB - TABLE_ROWS)


def forward_kernel(shapes, *refs):
    (
        tokens_hbm,
        kept,
        lengths,
        owners,
        table_f,
        entry_f,
        exit_f,
        expand_f,
        reduce_f,
        align_f,
        norm,
        entry_out,
        exit_out,
        expand_out,
        reduce_out,
        align_out,
        norms_out,
        residual_out,
        normed_one_out,
        joint_out,
        attended_out,
        middle_out,
        normed_two_out,
        act_out,
        slope_out,
        low_out,
        totals_out,
        segment_out,
        table_slab,
        entry_slab,
        exit_slab,
        expand_slab,
        reduce_slab,
        align_slab,
        table,
        entry,
        exit_low,
        wide,
        narrow,
        tokens,
        norms,
        residual,
        normed_one,
        joint,
        attended,
        feed,
        normed_two,
        act,
        slope,
        low,
        totals,
        patch,
        segment,
        send_sem,
        recv_sem,
        own_sem,
        load_sem,
        save_sem,
        act_sem,
    ) = refs
    width = residual.shape[1]
    rows = residual.shape[0]
    slabs = (table_slab, entry_slab, exit_slab, expand_slab, reduce_slab, align_slab)
    targets = (table, entry, exit_low, wide, narrow, align_out)
    route = Route()
    core = route.core
    arrive = greet(route.partners)
    tokens_copy = pltpu.make_async_copy(tokens_hbm, tokens, load_sem.at[0])
    tokens_copy.start()
    near, far, pair = (route.near, core), (route.far, core), (route.dp, 1 - core)
    peers = [(peer, core) for peer in route.peers]

    def copy_to(source, piece, origin, partner, slot):
        return pltpu.make_async_remote_copy(
            src_ref=source,
            dst_ref=targets[piece].at[origin],
            send_sem=send_sem.at[piece, slot],
            recv_sem=recv_sem.at[piece, origin],
            device_id=partner,
            device_id_type=MESH,
        )

    def wait(piece, origin):
        block = targets[piece].at[origin]
        pltpu.make_async_copy(block, block, recv_sem.at[piece, origin]).wait()

    def pass_on(group, origin, partners, slot):
        for piece in group:
            wait(piece, origin)
            for index, partner in enumerate(partners):
                copy_to(targets[piece].at[origin], piece, origin, partner, slot + index).start()

    def launch(group, wide_part, plane_part):
        for index, partner in enumerate([near, far] + peers + [pair]):
            if plane_part if index < 2 else wide_part:
                for piece in group:
                    copy_to(slabs[piece], piece, route.me, partner, index).start()
        if wide_part:
            for piece in group:
                pltpu.make_async_copy(
                    slabs[piece], targets[piece].at[route.me], own_sem.at[piece]
                ).start()

    def peer_turn(group, step):
        pass_on(group, route.level(step) * 2 + core, (near, far, pair), 6 + (step - 1) * 3)

    def near_turn(group, step):
        pass_on(group, route.at(route.near, step) * 2 + core, (far, pair), 15 + step * 2)

    def far_turn(group, step):
        pass_on(group, route.at(route.far, step) * 2 + core, (pair,), 23 + step * 2)
        pass_on(group, route.at(route.both, step) * 2 + core, (pair,), 24 + step * 2)

    def pair_turn(group, step):
        for base in (route.dp, route.near, route.far, route.both):
            for piece in group:
                wait(piece, route.at(base, step) * 2 + 1 - core)

    def settle(group):
        for piece in group:
            pltpu.make_async_copy(
                slabs[piece], targets[piece].at[route.me], own_sem.at[piece]
            ).wait()

    totals[...] = jnp.zeros_like(totals)
    segment[...] = segments(lengths[...], owners[...], route.me, rows)
    lifted = jnp.broadcast_to(slab_places(kept[...]).astype(F32), (8, rows))
    patch[...] = lifted.T[:, 0:1].astype(jnp.int32)
    blocks = width // 128
    whole = TABLE_ROWS - 1
    row_id = lax.broadcasted_iota(jnp.int32, (8, width), 0)
    lane_id = lax.broadcasted_iota(jnp.int32, (NORM_LANES, width), 1)
    from_id = lax.broadcasted_iota(jnp.int32, (NORM_LANES, width), 0)
    parts = width // NORM_LANES
    offset = lax.rem(route.me, parts) * NORM_LANES
    place = (lane_id == from_id + offset).astype(BF)
    spread = contract(norm[...].astype(BF), place, 1, 0)
    tail = jnp.where(row_id == 1, spread, 0.0)
    for block in range(blocks):
        lanes = slice(block * 128, block * 128 + 128)
        table_slab[0:whole, lanes] = table_f[pl.ds(block, whole, stride=blocks), :].astype(BF)
        last = table_f[pl.ds(whole * blocks + block, 1), :]
        mixed = jnp.where(row_id[:, lanes] == 0, last, tail[:, lanes])
        table_slab[whole : whole + 8, lanes] = mixed.astype(BF)
    for block, part in fold_rows(entry_f, *shapes[ENTRY]):
        entry_slab[:, block * 128 : block * 128 + 128] = part.astype(BF)
    for block, part in fold_rows(exit_f, *shapes[EXIT]):
        exit_slab[:, block * 128 : block * 128 + 128] = part.astype(BF)
    arrive()
    early = (TABLE, ENTRY, EXIT)
    last = (ALIGN,)
    launch(early, True, True)
    expand_slab[...] = expand_f[...].astype(BF)
    reduce_slab[...] = reduce_f[...].astype(BF)
    for block, part in fold_rows(align_f, *shapes[ALIGN]):
        align_slab[:, block * 128 : block * 128 + 128] = part.astype(BF)
    late = (EXPAND, REDUCE, ALIGN)

    def turn_of(group, turn):
        if 1 <= turn <= 3:
            peer_turn(group, turn)
        if 1 <= turn <= 4:
            near_turn(group, turn - 1)
        if 2 <= turn <= 5:
            far_turn(group, turn - 2)

    launch(late, True, False)
    for turn in range(1, 6):
        turn_of(early, turn)
    launch(late, False, True)
    for step in range(4):
        pair_turn((TABLE,), step)
    settle((TABLE,))
    tokens_copy.wait()

    for member in range(4):
        total = jnp.zeros((8, width), F32)
        for part in range(parts):
            total = total + table[member * parts + part, whole : whole + 8, :].astype(F32)
        norms[member : member + 1, :] = total[1:2, :]

    def embed(index, carry):
        span = pl.ds(pl.multiple_of(index * 256, 256), 256)
        entries = table.shape[0] * table.shape[1]
        picks = lax.broadcasted_iota(jnp.int32, (256, entries), 1) == patch[span, :]
        found = contract(picks.astype(BF), table[...].reshape(entries, width), 1, 0)
        values = tokens[span, :].astype(F32) + found
        residual[span, :] = values
        normed_one[span, :] = layer_norm(values, norms[0:1, :], norms[1:2, :]).astype(BF)
        return carry

    lax.fori_loop(0, rows // 256, embed, 0)
    for step in range(4):
        pair_turn((ENTRY, EXIT), step)
    settle((ENTRY, EXIT))

    saves = []

    def save(source, target):
        copy = pltpu.make_async_copy(source, target, save_sem.at[len(saves)])
        copy.start()
        saves.append(copy)

    save(entry, entry_out)
    save(exit_low, exit_out)
    save(norms, norms_out)
    save(segment, segment_out)
    save(residual, residual_out)
    save(normed_one, normed_one_out)

    def project(index, carry):
        span = pl.ds(pl.multiple_of(index * 256, 256), 256)
        weight = entry[:, :, span].reshape(width, 256)
        joint[:, span] = contract(normed_one[...], weight, 1, 0).astype(BF)
        return carry

    lax.fori_loop(0, 3 * width // 256, project, 0)
    save(joint, joint_out)

    def service(group, turn):
        @pl.when(turn <= 4)
        def _():
            near_turn(group, turn - 1)

        @pl.when(jnp.logical_and(turn >= 2, turn <= 5))
        def _():
            far_turn(group, turn - 2)

        @pl.when(turn <= 3)
        def _():
            peer_turn(group, turn)

    def attend_pair(index, carry):
        start = pl.multiple_of(index * 128, 128)
        here = pl.ds(start, 128)
        whole_keys = joint[:, pl.ds(start + width, 128)]
        values = joint[:, pl.ds(start + 2 * width, 128)]
        keys = []
        for head in (0, 1):
            mine, same = lane_marks(head, segment[...])
            keys.append(jnp.where(mine, whole_keys, jnp.where(same, 0.0, -1e30).astype(BF)))

        def chunk(step, inner):
            span = pl.ds(pl.multiple_of(step * 256, 256), 256)
            lane = lax.broadcasted_iota(jnp.int32, (256, 128), 1)
            scaled = joint[span, here] * BF(HD**-0.5)
            found = []
            logs = totals[span, :]
            for head in (0, 1):
                mine, same = lane_marks(head, segment[span, :])
                queries = jnp.where(mine, scaled, same.astype(BF))
                scores = contract(queries, keys[head], 1, 1)
                peak = jnp.max(scores, axis=1, keepdims=True)
                raised = jnp.exp(scores - peak)
                total = jnp.sum(raised, axis=1, keepdims=True)
                attention = (raised * (1.0 / total)).astype(BF)
                found.append(contract(attention, values, 1, 0))
                logs = jnp.where(lane == index * 2 + head, peak + jnp.log(total), logs)
            totals[span, :] = logs
            attended[span, here] = jnp.where(lane < HD, found[0], found[1]).astype(BF)
            return inner

        lax.fori_loop(0, rows // 256, chunk, 0)

        @pl.when(lax.rem(index, 2) == 0)
        def _():
            service(late, index // 2 + 1)

        return carry

    lax.fori_loop(0, width // 128, attend_pair, 0)
    save(attended, attended_out)
    save(totals, totals_out)

    def leave(index, carry):
        span = pl.ds(pl.multiple_of(index * 256, 256), 256)
        weight = exit_low[...].reshape(width, width)
        values = residual[span, :] + contract(attended[span, :], weight, 1, 0)
        feed[span, :] = values
        normed_two[span, :] = layer_norm(values, norms[2:3, :], norms[3:4, :]).astype(BF)
        return carry

    saves[4].wait()
    lax.fori_loop(0, rows // 256, leave, 0)
    def keep(index, carry):
        span = pl.ds(pl.multiple_of(index * 256, 256), 256)
        residual[span, :] = feed[span, :]
        return carry

    lax.fori_loop(0, rows // 256, keep, 0)
    save(residual, middle_out)
    save(normed_two, normed_two_out)

    plane = width // expand_slab.shape[0]

    def feed_level(step, carry):
        level = route.level(step) // 4
        pair_turn((EXPAND, REDUCE), step)

        @pl.when(step == 0)
        def _():
            settle((EXPAND, REDUCE))

        slot = lax.rem(step, 2)

        @pl.when(step >= 2)
        def _():
            for copy in outgoing(slot, 0):
                copy.wait()

        slabs_here = pl.ds(level * plane, plane)

        def rows_block(index, inner):
            span = pl.ds(pl.multiple_of(index * 256, 256), 256)
            up = wide[slabs_here].reshape(width, width)
            values = contract(normed_two[span, :], up, 1, 1)
            share = 0.5 + 0.5 * lax.erf(values * (0.5**0.5))
            lifted = (values * share).astype(BF)
            act[slot, span, :] = lifted
            bell = jnp.exp(values * values * -0.5) * (0.5 / math.pi) ** 0.5
            slope[slot, span, :] = share + values * bell
            down = narrow[slabs_here].reshape(width, width)
            feed[span, :] += contract(lifted, down, 1, 0)
            return inner

        lax.fori_loop(0, rows // 256, rows_block, 0)
        for copy in outgoing(slot, level):
            copy.start()

        @pl.when(step <= 1)
        def _():
            service(late, step + 4)

        return carry

    def outgoing(number, level):
        hidden = pl.ds(pl.multiple_of(level * width, width), width)
        return (
            pltpu.make_async_copy(act.at[number], act_out.at[:, hidden], act_sem.at[0, number]),
            pltpu.make_async_copy(slope.at[number], slope_out.at[:, hidden], act_sem.at[1, number]),
        )

    lax.fori_loop(0, 4, feed_level, 0)
    save(wide, expand_out)
    save(narrow, reduce_out)

    def close(index, carry):
        span = pl.ds(pl.multiple_of(index * 256, 256), 256)
        low[span, :] = feed[span, :].astype(BF)
        return carry

    lax.fori_loop(0, rows // 256, close, 0)
    save(low, low_out)
    for step in range(4):
        pair_turn(last, step)
    settle(last)
    for number in (0, 1):
        for copy in outgoing(number, 0):
            copy.wait()
    for copy in saves[:4] + saves[5:]:
        copy.wait()

    def sent(slot, carry):
        for piece in range(len(shapes)):
            copy_to(slabs[piece], piece, route.me, near, slot).wait_send()
        return carry

    lax.fori_loop(0, 31, sent, 0)


def gather_forward(shards, norm, tokens, kept, lengths, owners, shapes, devices):
    rows, width = tokens.shape
    hidden = shapes[EXPAND][0] * devices

    def shape(dims, kind=BF):
        return jax.ShapeDtypeStruct(dims, kind)

    pieces = (ENTRY, EXIT, EXPAND, REDUCE, ALIGN)
    flat = (rows, width)
    outs = [shape((devices,) + shapes[piece]) for piece in pieces] + [
        shape((8, width), F32),
        shape(flat, F32),
        shape(flat),
        shape((rows, 3 * width)),
        shape(flat),
        shape(flat, F32),
        shape(flat),
        shape((rows, hidden)),
        shape((rows, hidden), F32),
        shape(flat),
        shape((rows, 128), F32),
        shape((rows, 1), jnp.int32),
    ]
    scratch = (
        [pltpu.VMEM(dims, BF) for dims in shapes]
        + [pltpu.VMEM((devices,) + shapes[piece], BF) for piece in (TABLE, ENTRY, EXIT)]
        + [
            pltpu.VMEM((devices,) + shapes[EXPAND], BF),
            pltpu.VMEM((devices,) + shapes[REDUCE], BF),
            pltpu.VMEM(flat, BF),
            pltpu.VMEM((8, width), F32),
            pltpu.VMEM(flat, F32),
            pltpu.VMEM(flat, BF),
            pltpu.VMEM((rows, 3 * width), BF),
            pltpu.VMEM(flat, BF),
            pltpu.VMEM(flat, F32),
            pltpu.VMEM(flat, BF),
            pltpu.VMEM((2,) + flat, BF),
            pltpu.VMEM((2,) + flat, F32),
            pltpu.VMEM(flat, BF),
            pltpu.VMEM((rows, 128), F32),
            pltpu.VMEM((rows, 1), jnp.int32),
            pltpu.VMEM((rows, 1), jnp.int32),
            pltpu.SemaphoreType.DMA((6, 31)),
            pltpu.SemaphoreType.DMA((6, devices)),
            pltpu.SemaphoreType.DMA((6,)),
            pltpu.SemaphoreType.DMA((16,)),
            pltpu.SemaphoreType.DMA((16,)),
            pltpu.SemaphoreType.DMA((2, 2)),
        ]
    )
    return pl.pallas_call(
        functools.partial(forward_kernel, shapes),
        out_shape=outs,
        in_specs=[ANY] + [VMEM] * 10,
        out_specs=[ANY] * len(outs),
        scratch_shapes=scratch,
        compiler_params=pltpu.CompilerParams(
            collective_id=0, has_side_effects=True, vmem_limit_bytes=58 * MIB
        ),
        name="gather_forward",
    )(tokens, kept, lengths, owners, *shards, norm)


def norm_back(values, slope, gain):
    center = values - jnp.mean(values, axis=-1, keepdims=True)
    spread = jnp.mean(center * center, axis=-1, keepdims=True)
    scale = lax.rsqrt(spread + LN_EPS)
    unit = center * scale
    scaled = slope * gain
    level = jnp.mean(scaled, axis=-1, keepdims=True)
    tilt = jnp.mean(scaled * unit, axis=-1, keepdims=True)
    return scale * (scaled - level - unit * tilt), slope * unit


def backward_kernel(shapes, *refs):
    count = len(shapes)
    (
        kept,
        segment,
        norms,
        norm_weight,
        norm_first,
        norm_second,
        cot_out_hbm,
        cot_align_hbm,
        entry_hbm,
        exit_hbm,
        expand_hbm,
        reduce_hbm,
        align_hbm,
        residual_hbm,
        normed_one_hbm,
        joint_hbm,
        attended_hbm,
        middle_hbm,
        normed_two_hbm,
        act_hbm,
        slope_hbm,
        low_hbm,
        totals_hbm,
    ) = refs[:23]
    states = [refs[23 + 3 * piece : 26 + 3 * piece] for piece in range(count)]
    refs = refs[23 + 3 * count :]
    outs = refs[:count]
    norm_out, sums_out, aligned_out, token_out = refs[count : 4 + count]
    refs = refs[4 + count :]
    grads, refs = refs[:count], refs[count:]
    from_pair, refs = refs[:count], refs[count:]
    from_far, refs = refs[:count], refs[count:]
    from_near, refs = refs[:count], refs[count:]
    from_peer, refs = refs[:count], refs[count:]
    (
        wide_b,
        spare,
        act,
        expand,
        reduce,
        normed_two,
        grad_feed,
        grad_out,
        grad_two,
        slope,
        query_sum,
        norm_sums,
        held,
        table_first,
        table_second,
        table_third,
        send_sem,
        pair_sem,
        far_sem,
        near_sem,
        peer_sem,
        load_sem,
        save_sem,
        state_sem,
        held_sem,
        sums_sem,
    ) = refs
    rows, width = grad_out.shape
    align_width = cot_align_hbm.shape[1]
    route = Route()
    core = route.core
    near, far, pair = (route.near, core), (route.far, core), (route.dp, 1 - core)

    def load(source, target, number):
        copy = pltpu.make_async_copy(source, target, load_sem.at[number])
        copy.start()
        return copy

    align_low = wide_b.at[:, pl.ds(0, align_width)]
    cot_align = wide_b.at[:, pl.ds(align_width, align_width)]
    cot_align_copy = load(cot_align_hbm, cot_align, 0)
    align_copy = load(align_hbm, align_low, 1)
    low_copy = load(low_hbm, act, 2)
    cot_out_copy = load(cot_out_hbm, spare, 3)
    normed_two_copy = load(normed_two_hbm, normed_two, 4)
    arrive = greet(route.partners + [route.corner])

    def level_rows(step):
        return pl.ds(pl.multiple_of((route.level(step) // 4) * width, width), width)

    def chunk_loads(step):
        here = level_rows(step)
        return (
            pltpu.make_async_copy(reduce_hbm.at[here, :], reduce, load_sem.at[6]),
            pltpu.make_async_copy(expand_hbm.at[here, :], expand, load_sem.at[7]),
            pltpu.make_async_copy(slope_hbm.at[:, here], slope, load_sem.at[8]),
        )

    def act_load(step):
        return pltpu.make_async_copy(act_hbm.at[:, level_rows(step)], act, load_sem.at[9])


    def copy_to(source, target, slot, piece, semaphore, partner):
        return pltpu.make_async_remote_copy(
            src_ref=source,
            dst_ref=target,
            send_sem=send_sem.at[piece, slot],
            recv_sem=semaphore,
            device_id=partner,
            device_id_type=MESH,
        )

    def landed(block, semaphore):
        pltpu.make_async_copy(block, block, semaphore).wait()

    def total(piece, dp, sources):
        landed(from_pair[piece].at[dp], pair_sem.at[piece, dp])
        found = grads[piece][dp * 2 + core].astype(F32) + from_pair[piece][dp].astype(F32)
        for block, semaphore, slot in sources:
            landed(block.at[slot], semaphore.at[piece, slot])
            found = found + block[slot].astype(F32)
        return found

    def stage_pair(piece, step):
        for base in (route.far, route.both, route.near, route.dp):
            dp = route.at(base, step)
            copy_to(
                grads[piece].at[dp * 2 + 1 - core],
                from_pair[piece].at[dp],
                dp,
                piece,
                pair_sem.at[piece, dp],
                pair,
            ).start()

    def forward_sum(piece, dp, sources, target, slot, semaphore, partner):
        grads[piece][dp * 2 + core] = total(piece, dp, sources).astype(BF)
        copy_to(
            grads[piece].at[dp * 2 + core], target, slot, piece, semaphore, partner
        ).start()

    def stage_far(piece, step):
        for side, base in enumerate((route.far, route.both)):
            slot = step * 2 + side
            forward_sum(
                piece,
                route.at(base, step),
                (),
                from_far[piece].at[slot],
                16 + slot,
                far_sem.at[piece, slot],
                far,
            )

    def stage_near(piece, step):
        forward_sum(
            piece,
            route.at(route.near, step),
            ((from_far[piece], far_sem, step * 2 + 1),),
            from_near[piece].at[step],
            24 + step,
            near_sem.at[piece, step],
            near,
        )

    def stage_peer(piece, step):
        forward_sum(
            piece,
            route.level(step),
            ((from_far[piece], far_sem, step * 2), (from_near[piece], near_sem, step)),
            from_peer[piece].at[step - 1],
            27 + step,
            peer_sem.at[piece, step - 1],
            (route.level(step), core),
        )

    def stage_own(piece):
        found = total(
            piece,
            route.dp,
            ((from_far[piece], far_sem, 0), (from_near[piece], near_sem, 0))
            + tuple((from_peer[piece], peer_sem, slot) for slot in range(3)),
        )
        if outs[piece].shape == found.shape:
            outs[piece][...] = found
            return
        blocks = found.shape[1] // 128
        lines = TABLE_ROWS - 1 if piece == TABLE else found.shape[0]
        for block in range(blocks):
            part = found[:, block * 128 : block * 128 + 128]
            outs[piece][pl.ds(block, lines, stride=blocks), :] = part[:lines]
            if piece == TABLE:
                outs[piece][pl.ds(lines * blocks + block, 1), :] = part[lines : lines + 1]
        if piece == TABLE:
            norm_sums[4:5, :] = found[lines + 1 : lines + 2] + found[lines + 2 : lines + 3]

    def each(stage, pieces, first=0):
        def body(turn, carry):
            for piece in pieces:
                stage(piece, turn)
            return carry

        lax.fori_loop(first, 4, body, 0)

    def flow(piece, turn):
        for late, stage in enumerate((stage_far, stage_near, stage_peer)):
            step = 3 - (turn - late)
            lowest = 1 if stage is stage_peer else 0

            @pl.when(jnp.logical_and(step >= lowest, step <= 3))
            def _():
                stage(piece, step)


    norm_sums[...] = jnp.zeros_like(norm_sums)
    cot_align_copy.wait()
    align_copy.wait()
    low_copy.wait()
    cot_out_copy.wait()
    for copy in chunk_loads(3):
        copy.start()

    def head_rows(index, carry):
        span = pl.ds(pl.multiple_of(index * 256, 256), 256)
        keep = segment[span, :] > 0
        slopes = jnp.where(keep, cot_align[span, :], jnp.zeros((256, align_width), BF))
        cot_align[span, :] = slopes
        found = contract(slopes, align_low[...], 1, 1)
        found = found + jnp.where(keep, spare[span, :].astype(F32), 0.0)
        grad_out[span, :] = found
        grad_feed[span, :] = found.astype(BF)
        return carry

    lax.fori_loop(0, rows // 256, head_rows, 0)

    def head_grads(index, carry):
        span = pl.ds(pl.multiple_of(index * 384, 384), 384)
        found = contract(act[:, span], cot_align[...], 0, 0).astype(BF)
        slabs = 384 // shapes[ALIGN][0]
        grads[ALIGN][pl.ds(index * slabs, slabs)] = found.reshape((slabs,) + shapes[ALIGN])
        return carry

    lax.fori_loop(0, width // 384, head_grads, 0)
    arrive()
    each(stage_pair, (ALIGN,))

    def head_out(index, carry):
        span = pl.ds(pl.multiple_of(index * 256, 256), 256)
        result = contract(act[span, :], align_low[...], 1, 0).astype(BF)
        cot_align[span, :] = result
        return carry

    lax.fori_loop(0, rows // 256, head_out, 0)
    aligned_copy = pltpu.make_async_copy(cot_align, aligned_out, save_sem.at[0])
    aligned_copy.start()
    act_load(3).start()
    normed_two_copy.wait()


    def feed_back(turn, carry):
        step = 3 - turn
        for copy in chunk_loads(step):
            copy.wait()

        def rows_block(index, inner):
            span = pl.ds(pl.multiple_of(index * 256, 256), 256)
            found = contract(grad_feed[span, :], reduce[...], 1, 1)
            before = (found * slope[span, :]).astype(BF)
            spare[span, :] = before
            part = contract(before, expand[...], 1, 0)

            @pl.when(turn == 0)
            def _():
                grad_two[span, :] = part

            @pl.when(turn > 0)
            def _():
                grad_two[span, :] += part

            return inner

        lax.fori_loop(0, rows // 256, rows_block, 0)

        @pl.when(turn < 3)
        def _():
            for copy in chunk_loads(step - 1):
                copy.start()

        @pl.when(turn == 3)
        def _():
            pltpu.make_async_copy(middle_hbm, slope, load_sem.at[8]).start()
            pltpu.make_async_copy(exit_hbm, expand, load_sem.at[7]).start()

        @pl.when(turn == 0)
        def _():
            each(stage_far, (ALIGN,))

        @pl.when(turn > 0)
        def _():
            feed_stage(stage_far, step + 1)

        act_load(step).wait()
        per = 384 // shapes[EXPAND][0]
        plane = (route.level(step) // 4) * (width // shapes[EXPAND][0])

        def slabs_block(index, inner):
            span = pl.ds(pl.multiple_of(index * 384, 384), 384)
            here = pl.ds(plane + index * per, per)
            found = contract(act[:, span], grad_feed[...], 0, 0).astype(BF)
            grads[REDUCE][here] = found.reshape((per,) + shapes[REDUCE])
            found = contract(spare[:, span], normed_two[...], 0, 0).astype(BF)
            grads[EXPAND][here] = found.reshape((per,) + shapes[EXPAND])
            return inner

        lax.fori_loop(0, width // 384, slabs_block, 0)

        @pl.when(turn < 3)
        def _():
            act_load(step - 1).start()

        for piece in (REDUCE, EXPAND):
            stage_pair(piece, step)

        return carry

    def feed_stage(stage, step):
        for piece in (REDUCE, EXPAND):
            stage(piece, step)

    lax.fori_loop(0, 4, feed_back, 0)
    aligned_copy.wait()
    joint_copy = load(joint_hbm, wide_b, 5)
    attended_copy = load(attended_hbm, normed_two, 2)
    normed_one_copy = load(normed_one_hbm, act, 9)
    pltpu.make_async_copy(middle_hbm, slope, load_sem.at[8]).wait()
    pltpu.make_async_copy(exit_hbm, expand, load_sem.at[7]).wait()


    def leave_back(index, carry):
        span = pl.ds(pl.multiple_of(index * 256, 256), 256)
        slopes = grad_two[span, :]
        through, gains = norm_back(slope[span, :], slopes, norms[2:3, :])
        norm_sums[2:3, :] += jnp.sum(gains, axis=0, keepdims=True)
        norm_sums[3:4, :] += jnp.sum(slopes, axis=0, keepdims=True)
        found = grad_out[span, :] + through
        grad_out[span, :] = found
        branch = found.astype(BF)
        grad_feed[span, :] = branch
        reduce[span, :] = contract(branch, expand[...], 1, 1).astype(BF)
        return carry

    lax.fori_loop(0, rows // 256, leave_back, 0)
    residual_copy = load(residual_hbm, grad_two, 0)

    def load_entry(part, target):
        return load(entry_hbm.at[:, pl.ds(part * width, width)], target, (1, 3, 6)[part])

    entry_copies = [load_entry(0, expand)]
    key_sum, value_sum, totals = (slope.at[:, pl.ds(number * 128, 128)] for number in range(3))
    totals_copy = load(totals_hbm, totals, 10)
    attended_copy.wait()

    feed_stage(stage_far, 0)

    def exit_grads(index, carry):
        span = pl.ds(pl.multiple_of(index * 384, 384), 384)
        found = contract(normed_two[:, span], grad_feed[...], 0, 0).astype(BF)
        slabs = 384 // shapes[EXIT][0]
        grads[EXIT][pl.ds(index * slabs, slabs)] = found.reshape((slabs,) + shapes[EXIT])
        return carry

    lax.fori_loop(0, width // 384, exit_grads, 0)
    each(stage_pair, (EXIT,))
    joint_copy.wait()


    scale = HD**-0.5
    totals_copy.wait()

    def split(values):
        high = values.astype(BF)
        rest = values - high.astype(F32)
        middle = rest.astype(BF)
        return high, middle, (rest - middle.astype(F32)).astype(BF)

    def with_parts(lane, values, others):
        parts = split(values)
        for number in range(3):
            others = jnp.where(lane == 8 + number, parts[number], others)
        return others

    def attend_pair(index, carry):
        start = pl.multiple_of(index * 128, 128)
        at_query = pl.ds(start, 128)
        at_key = pl.ds(start + width, 128)
        at_value = pl.ds(start + 2 * width, 128)
        key_sum[...] = jnp.zeros_like(key_sum)
        value_sum[...] = jnp.zeros_like(value_sum)
        whole_keys = wide_b[:, at_key]
        whole_values = wide_b[:, at_value]
        turned = whole_keys.astype(F32).T.astype(BF)
        lane = jnp.bitwise_and(lax.broadcasted_iota(jnp.int32, (rows, 128), 1), HD - 1)
        parted = jnp.logical_and(lane >= 8, lane < 11)
        ones = parted.astype(BF)
        keys = []
        for head in (0, 1):
            mine, same = lane_marks(head, segment[...])
            marks = jnp.where(same, 0.0, -1e30).astype(BF)
            keys.append(jnp.where(mine, whole_keys, jnp.where(parted, ones, marks)))

        def chunk(step, inner):
            span = pl.ds(pl.multiple_of(step * 256, 256), 256)
            whole_lane = lax.broadcasted_iota(jnp.int32, (256, 128), 1)
            lane = jnp.bitwise_and(whole_lane, HD - 1)
            scaled = wide_b[span, at_query] * BF(scale)
            both_slopes = reduce[span, at_query]
            zero = jnp.zeros_like(scaled)
            queries, pure_queries, slopes = [], [], []
            for head in (0, 1):
                mine, same = lane_marks(head, segment[span, :])
                log_total = jnp.sum(
                    jnp.where(whole_lane == index * 2 + head, totals[span, :], 0.0),
                    axis=1,
                    keepdims=True,
                )
                marks = with_parts(lane, -log_total, same.astype(BF))
                queries.append(jnp.where(mine, scaled, marks))
                pure_queries.append(jnp.where(mine, scaled, zero))
                slopes.append(jnp.where(mine, both_slopes, zero))
            pure_queries = jnp.concatenate(pure_queries, axis=0)
            slopes = jnp.concatenate(slopes, axis=0)
            scores = [contract(keys[head], queries[head], 1, 1) for head in (0, 1)]
            slope_attention = contract(whole_values, slopes, 1, 1)
            attentions, slope_scores = [], []
            for head in (0, 1):
                attention = jnp.exp(scores[head])
                mine = slope_attention[:, head * 256 : head * 256 + 256]
                inner_sum = jnp.sum(attention * mine, axis=0, keepdims=True)
                slope_scores.append((attention * (mine - inner_sum)).astype(BF))
                attentions.append(attention.astype(BF))
            value_sum[...] += contract(jnp.concatenate(attentions, axis=1), slopes, 1, 0)
            key_sum[...] += contract(jnp.concatenate(slope_scores, axis=1), pure_queries, 1, 0)
            for head in (0, 1):
                half = slice(head * HD, head * HD + HD)
                query_sum[half, span] = contract(turned[half, :], slope_scores[head], 1, 0)
            return inner

        lax.fori_loop(0, rows // 256, chunk, 0)
        wide_b[:, at_query] = (query_sum[...].T * scale).astype(BF)
        wide_b[:, at_key] = key_sum[...].astype(BF)
        wide_b[:, at_value] = value_sum[...].astype(BF)

        @pl.when(index == 0)
        def _():
            each(stage_far, (EXIT,))

        @pl.when(index == 1)
        def _():
            feed_stage(stage_near, 3)
            each(stage_near, (ALIGN,))

        @pl.when(index == 2)
        def _():
            feed_stage(stage_near, 2)
            each(stage_near, (EXIT,))

        @pl.when(index == 3)
        def _():
            feed_stage(stage_near, 1)
            feed_stage(stage_peer, 3)
            each(stage_peer, (ALIGN,), 1)

        @pl.when(index == 4)
        def _():
            feed_stage(stage_near, 0)
            feed_stage(stage_peer, 2)
            each(stage_peer, (EXIT,), 1)

        @pl.when(index == 5)
        def _():
            feed_stage(stage_peer, 1)

        return carry

    lax.fori_loop(0, width // 128, attend_pair, 0)

    table_states = (table_first, table_second, table_third)
    homes, line = {}, {}
    for number in range(3):
        for piece in (ENTRY, EXIT, ALIGN):
            start = line.get(number, 0)
            size = states[piece][number].shape[0]
            homes[piece, number] = slope.at[
                pl.ds(start, size), pl.ds(number * 128, 128)
            ]
            line[number] = start + size
        homes[TABLE, number] = table_states[number]
        for turn, piece in enumerate((EXPAND, REDUCE)):
            size = shapes[piece][0]
            homes[piece, number] = grad_two.at[pl.ds((turn * 3 + number) * size, size), :]

    def state_copy(piece, number):
        return pltpu.make_async_copy(
            states[piece][number], homes[piece, number], state_sem.at[piece, number]
        )

    def start_states(pieces):
        for piece in pieces:
            for number in range(3):
                state_copy(piece, number).start()

    entry_copies.append(load_entry(1, reduce))
    start_states((ENTRY, EXIT, ALIGN, TABLE))


    normed_one_copy.wait()
    for block in range(width // 128):
        lanes = slice(block * 128, block * 128 + 128)
        spare[lanes, :] = act[:, lanes].astype(F32).T.astype(BF)

    entry_copies.append(load_entry(2, act))

    def entry_block(index, carry):
        half = index // 3
        column = pl.ds(pl.multiple_of(lax.rem(index, 3) * width, width), width)
        line = pl.ds(pl.multiple_of(half * 384, 384), 384)
        found = contract(spare[line, :], wide_b[:, column], 1, 0).astype(BF)
        slabs = 384 // shapes[ENTRY][0]
        grads[ENTRY][pl.ds(half * slabs, slabs), :, column] = found.reshape(
            (slabs, shapes[ENTRY][0], width)
        )
        return carry

    lax.fori_loop(0, 6, entry_block, 0)
    each(stage_pair, (ENTRY,))
    for copy in entry_copies:
        copy.wait()
    residual_copy.wait()

    def enter_back(index, carry):
        span = pl.ds(pl.multiple_of(index * 256, 256), 256)
        slopes = contract(wide_b[span, 0:width], expand[...], 1, 1)
        slopes += contract(wide_b[span, width : 2 * width], reduce[...], 1, 1)
        slopes += contract(wide_b[span, 2 * width : 3 * width], act[...], 1, 1)
        through, gains = norm_back(grad_two[span, :], slopes, norms[0:1, :])
        norm_sums[0:1, :] += jnp.sum(gains, axis=0, keepdims=True)
        norm_sums[1:2, :] += jnp.sum(slopes, axis=0, keepdims=True)
        found = grad_out[span, :] + through
        grad_out[span, :] = found
        grad_feed[span, :] = found.astype(BF)
        flow(ENTRY, index)
        return carry

    lax.fori_loop(0, rows // 256, enter_back, 0)
    token_copy = pltpu.make_async_copy(grad_out, token_out, save_sem.at[1])
    token_copy.start()
    start_states((EXPAND, REDUCE))

    slabs = 4
    block_rows = slabs * TABLE_SLAB

    def table_block(index, carry):
        entries = lax.broadcasted_iota(jnp.int32, (block_rows, rows), 0) + index * block_rows
        picks = (entries == slab_places(kept[...])).astype(BF)
        found = contract(picks, grad_feed[...], 1, 0).astype(BF)
        grads[TABLE][pl.ds(index * slabs, slabs)] = found.reshape((slabs, TABLE_SLAB, width))

        @pl.when(lax.rem(index, 2) == 0)
        def _():
            flow(ENTRY, 3 + index // 2)

        return carry

    devices = grads[TABLE].shape[0]
    lax.fori_loop(0, devices // slabs, table_block, 0)
    whole = TABLE_ROWS - 1
    row_id = lax.broadcasted_iota(jnp.int32, (8, width), 0)
    for member in range(4):
        line = norm_sums[member : member + 1, :]
        high = line.astype(BF).astype(F32)
        tail = jnp.where(row_id == 1, high, jnp.where(row_id == 2, line - high, 0.0))

        def tuck(index, carry):
            slab = member * (devices // 4) + index
            kept = grads[TABLE][slab, whole : whole + 8, :].astype(F32)
            grads[TABLE][slab, whole : whole + 8, :] = jnp.where(row_id == 0, kept, tail).astype(BF)
            return carry

        lax.fori_loop(0, devices // 4, tuck, 0)
    each(stage_pair, (TABLE,))
    row_id16 = lax.broadcasted_iota(jnp.int32, (16, 128), 0)

    def squares(piece):
        for number in range(3):
            state_copy(piece, number).wait()
        weight, first, second = (homes[piece, number][...] for number in range(3))
        update = lamb_update(weight, outs[piece][...], first, second, DECAY)[2]
        note(MEMBERS.index(piece), total_square(weight), total_square(update))

    def note(member, weight_square, update_square):
        kept = held[0]
        kept = jnp.where(row_id16 == member, weight_square, kept)
        held[0] = jnp.where(row_id16 == 8 + member, update_square, kept)

    held[0] = jnp.zeros_like(held[0])
    for turn in range(3):
        flow(TABLE, turn)
    for piece in (ALIGN, REDUCE, EXPAND, EXIT):
        stage_own(piece)
        squares(piece)
    for turn in range(3, 6):
        flow(TABLE, turn)
    stage_own(ENTRY)
    squares(ENTRY)
    stage_own(TABLE)
    squares(TABLE)
    norm_row = norm_sums[4:5, :]
    share = lax.rem(route.me, width // NORM_LANES)
    norm_slope = jnp.zeros((1, NORM_LANES), F32)
    for number in range(width // NORM_LANES):
        part = norm_row[:, number * NORM_LANES : (number + 1) * NORM_LANES]
        norm_slope = jnp.where(share == number, part, norm_slope)
    norm_out[...] = norm_slope
    update = lamb_update(norm_weight[...], norm_slope, norm_first[...], norm_second[...], 0.0)[2]
    note(len(MEMBERS), total_square(norm_weight[...]), total_square(update))


    def sums_to(slot, target, partner, number):
        copy = pltpu.make_async_remote_copy(
            src_ref=held.at[slot],
            dst_ref=held.at[target],
            send_sem=sums_sem.at[number],
            recv_sem=held_sem.at[target],
            device_id=partner,
            device_id_type=MESH,
        )
        copy.start()
        return copy

    def sums_from(slot):
        pltpu.make_async_copy(held.at[slot], held.at[slot], held_sem.at[slot]).wait()

    sums_sent = [sums_to(0, 1, pair, 0)]
    sums_from(1)
    column = route.column
    held[2 + column] = held[0] + held[1]
    plane = [(route.near, core), (route.far, core), route.corner]
    for number, partner in enumerate(plane):
        sums_sent.append(sums_to(2 + column, 2 + column, partner, 1 + number))
    for partner, _ in plane:
        sums_from(2 + lax.rem(partner, 4))
    held[6 + route.z] = held[2] + held[3] + held[4] + held[5]
    for number, peer in enumerate(route.peers):
        sums_sent.append(sums_to(6 + route.z, 6 + route.z, (peer, core), 4 + number))
    for peer in route.peers:
        sums_from(6 + peer // 4)
    sums_out[...] = held[6] + held[7] + held[8] + held[9]
    for copy in sums_sent:
        copy.wait_send()

    def sent(slot, carry):
        for piece in range(count):
            copy_to(
                grads[piece].at[0], from_pair[piece].at[0], slot, piece, pair_sem.at[piece, 0], pair
            ).wait_send()
        return carry

    lax.fori_loop(0, 31, sent, 0)
    token_copy.wait()


def scatter_backward(kept, segment, norms, norm_states, arrays, states, shapes, devices):
    rows, width = arrays[0].shape
    align_width = arrays[1].shape[1]
    dps = devices // 2
    flat = (rows, width)

    def buffers(slots):
        return [pltpu.VMEM((slots,) + dims, BF) for dims in shapes]

    count = len(shapes)
    scratch = (
        buffers(devices)
        + buffers(dps)
        + buffers(8)
        + buffers(4)
        + buffers(3)
        + [pltpu.VMEM((rows, 3 * width), BF)]
        + [pltpu.VMEM(flat, BF)] * 6
        + [pltpu.VMEM(flat, F32)] * 3
        + [
            pltpu.VMEM((128, rows), F32),
            pltpu.VMEM((8, width), F32),
            pltpu.VMEM((10, 16, 128), F32),
        ]
        + [pltpu.VMEM(states[3 * TABLE].shape, F32)] * 3
        + [
            pltpu.SemaphoreType.DMA((count, 31)),
            pltpu.SemaphoreType.DMA((count, dps)),
            pltpu.SemaphoreType.DMA((count, 8)),
            pltpu.SemaphoreType.DMA((count, 4)),
            pltpu.SemaphoreType.DMA((count, 3)),
            pltpu.SemaphoreType.DMA((11,)),
            pltpu.SemaphoreType.DMA((2,)),
            pltpu.SemaphoreType.DMA((count, 3)),
            pltpu.SemaphoreType.DMA((10,)),
            pltpu.SemaphoreType.DMA((7,)),
        ]
    )
    outs = [jax.ShapeDtypeStruct(state.shape, F32) for state in states[::3]] + [
        jax.ShapeDtypeStruct((1, NORM_LANES), F32),
        jax.ShapeDtypeStruct((16, 128), F32),
        jax.ShapeDtypeStruct((rows, align_width), BF),
        jax.ShapeDtypeStruct(flat, F32),
    ]
    return pl.pallas_call(
        functools.partial(backward_kernel, shapes),
        out_shape=outs,
        in_specs=[VMEM] * 6 + [ANY] * (len(arrays) + len(states)),
        out_specs=[VMEM] * (count + 2) + [ANY] * 2,
        scratch_shapes=scratch,
        compiler_params=pltpu.CompilerParams(
            collective_id=1, has_side_effects=True, vmem_limit_bytes=60 * MIB
        ),
        name="scatter_backward",
    )(kept, segment, norms, *norm_states, *arrays, *states)


def lamb_update(weight, gradient, first, second, decay):
    new_first = BETA_ONE * first + (1.0 - BETA_ONE) * gradient
    new_second = BETA_TWO * second + (1.0 - BETA_TWO) * gradient * gradient
    update = new_first / (jnp.sqrt(new_second) + ADAM_EPS) + decay * weight
    return new_first, new_second, update


def total_square(values):
    return jnp.sum(jnp.sum(values * values, axis=1, keepdims=True), axis=0, keepdims=True)


def finish_kernel(count, *refs):
    segment, sums, norm_slope = refs[:3]
    norm_states = refs[3:6]
    slopes_hbm = refs[6 : 6 + count]
    refs = refs[6 + count :]
    states, refs = refs[: 3 * count], refs[3 * count :]
    low_hbm, aligned_hbm, token_hbm = refs[:3]
    outs, refs = refs[3 : 3 + 3 * count], refs[3 + 3 * count :]
    norm_outs = refs[:3]
    block_out, aligned_out, token_out, stats = refs[3:7]
    refs = refs[7:]
    held, refs = refs[: 3 * count], refs[3 * count :]
    made, refs = refs[: 3 * count], refs[3 * count :]
    slopes, refs = refs[:count], refs[count:]
    slope_sem, low, aligned, token, in_sem, out_sem, row_sem = refs
    slope_loads = [
        pltpu.make_async_copy(slopes_hbm[piece], slopes[piece], slope_sem.at[piece])
        for piece in range(count)
    ]
    for copy in slope_loads:
        copy.start()
    token_copy = pltpu.make_async_copy(token_hbm, token, row_sem.at[0])
    token_copy.start()
    low_copy = pltpu.make_async_copy(low_hbm, low, row_sem.at[1])
    low_copy.start()
    aligned_copy = pltpu.make_async_copy(aligned_hbm, aligned, row_sem.at[2])
    aligned_copy.start()
    loads = [
        pltpu.make_async_copy(states[number], held[number], in_sem.at[number])
        for number in range(3 * count)
    ]
    for copy in loads:
        copy.start()

    def trust_of(member):
        weight_square = sums[member : member + 1, :]
        update_square = sums[8 + member : 9 + member, :]
        return jnp.sqrt(weight_square) / jnp.sqrt(update_square + TINY)

    lane = lax.broadcasted_iota(jnp.int32, (1, 128), 1)
    lines = [jnp.zeros((1, 128), F32)] * 3
    for member in range(len(MEMBERS) + 1):
        found = (
            trust_of(member),
            jnp.sqrt(sums[member : member + 1, :]),
            jnp.sqrt(sums[8 + member : 9 + member, :]),
        )
        lines = [jnp.where(lane == member, new, line) for new, line in zip(found, lines)]
    for row, line in enumerate(lines):
        stats[row : row + 1, :] = line[:, : stats.shape[1]]
    weight, first, second = (state[...] for state in norm_states)
    made_norm = lamb_update(weight, norm_slope[...], first, second, 0.0)
    norm_outs[0][...] = made_norm[0]
    norm_outs[1][...] = made_norm[1]
    step = RATE * trust_of(len(MEMBERS))[:, :NORM_LANES] * made_norm[2]
    norm_outs[2][...] = weight - step
    token_copy.wait()
    token_copy = pltpu.make_async_copy(token, token_out, row_sem.at[0])
    token_copy.start()
    low_copy.wait()
    keep = segment[...] > 0
    low[...] = jnp.where(keep, low[...], jnp.zeros_like(low))
    low_copy = pltpu.make_async_copy(low, block_out, row_sem.at[1])
    low_copy.start()
    aligned_copy.wait()
    aligned[...] = jnp.where(keep, aligned[...], jnp.zeros_like(aligned))
    aligned_copy = pltpu.make_async_copy(aligned, aligned_out, row_sem.at[2])
    aligned_copy.start()
    saves = []
    for member, piece in enumerate(MEMBERS):
        trust = trust_of(member)
        for number in range(3):
            loads[3 * piece + number].wait()
        slope_loads[piece].wait()
        weight, first, second = (held[3 * piece + number][...] for number in range(3))
        new_first, new_second, update = lamb_update(
            weight, slopes[piece][...], first, second, DECAY
        )
        wide = trust if update.shape[1] == 128 else trust[:, 0:1]
        made[3 * piece][...] = new_first
        made[3 * piece + 1][...] = new_second
        made[3 * piece + 2][...] = weight - RATE * wide * update
        for number in range(3):
            copy = pltpu.make_async_copy(
                made[3 * piece + number], outs[3 * piece + number], out_sem.at[3 * piece + number]
            )
            copy.start()
            saves.append(copy)
    for copy in saves + [low_copy, aligned_copy, token_copy]:
        copy.wait()


def finish(segment, sums, norm_slope, norm_states, slopes, states, rows):
    count = len(slopes)
    low, aligned, token = rows

    def like(array):
        return jax.ShapeDtypeStruct(array.shape, array.dtype)

    outs = (
        [like(state) for state in states]
        + [like(state) for state in norm_states]
        + [like(low), like(aligned), like(token)]
        + [jax.ShapeDtypeStruct((3, len(MEMBERS) + 1), F32)]
    )
    return pl.pallas_call(
        functools.partial(finish_kernel, count),
        out_shape=outs,
        in_specs=[VMEM] * 6 + [ANY] * (4 * count + 3),
        out_specs=[ANY] * (3 * count) + [VMEM] * 3 + [ANY] * 3 + [VMEM],
        scratch_shapes=[pltpu.VMEM(state.shape, F32) for state in states] * 2
        + [pltpu.VMEM(slope.shape, F32) for slope in slopes]
        + [
            pltpu.SemaphoreType.DMA((count,)),
            pltpu.VMEM(low.shape, BF),
            pltpu.VMEM(aligned.shape, BF),
            pltpu.VMEM(token.shape, F32),
            pltpu.SemaphoreType.DMA((3 * count,)),
            pltpu.SemaphoreType.DMA((3 * count,)),
            pltpu.SemaphoreType.DMA((3,)),
        ],
        compiler_params=pltpu.CompilerParams(vmem_limit_bytes=60 * MIB),
        name="finish",
    )(segment, sums, norm_slope, *norm_states, *slopes, *states, low, aligned, token)


def moments_kernel(decays, *refs):
    count = len(decays)
    sums = refs[7 * count]
    row = lax.broadcasted_iota(jnp.int32, (16, 128), 0)
    found = jnp.zeros((16, 128), F32)
    for member, decay in enumerate(decays):
        weight, gradient, first, second = refs[4 * member : 4 * member + 4]
        new_first_ref, new_second_ref, update_ref = refs[
            4 * count + 3 * member : 4 * count + 3 * member + 3
        ]
        slope = gradient[...]
        new_first = BETA_ONE * first[...] + (1.0 - BETA_ONE) * slope
        new_second = BETA_TWO * second[...] + (1.0 - BETA_TWO) * slope * slope
        update = new_first / (jnp.sqrt(new_second) + ADAM_EPS) + decay * weight[...]
        new_first_ref[...] = new_first
        new_second_ref[...] = new_second
        update_ref[...] = update
        found = jnp.where(row == member, jnp.sum(weight[...] * weight[...]), found)
        found = jnp.where(row == 8 + member, jnp.sum(update * update), found)
    sums[...] = found


def moments(members, decays):
    shapes = [jax.ShapeDtypeStruct(member[0].shape, F32) for member in members]
    outs = [shape for shape in shapes for _ in range(3)]
    flat = [array for member in members for array in member]
    return pl.pallas_call(
        functools.partial(moments_kernel, decays),
        out_shape=outs + [jax.ShapeDtypeStruct((16, 128), F32)],
        in_specs=[VMEM] * len(flat),
        out_specs=[VMEM] * (len(outs) + 1),
        compiler_params=pltpu.CompilerParams(vmem_limit_bytes=40 * MIB),
        name="moments",
    )(*flat)


def step_kernel(count, *refs):
    sums = refs[0]
    for member in range(count):
        weight, update = refs[1 + 2 * member : 3 + 2 * member]
        weight_square = sums[member : member + 1, :]
        update_square = sums[8 + member : 9 + member, :]
        trust = jnp.sqrt(weight_square) / jnp.sqrt(update_square + TINY)
        if weight.shape[1] % 128 == 0:
            trust = jnp.concatenate([trust] * (weight.shape[1] // 128), axis=1)
        else:
            trust = trust[:, : weight.shape[1]]
        refs[1 + 2 * count + member][...] = weight[...] - RATE * trust * update[...]


def take_step(sums, pairs):
    count = len(pairs)
    return pl.pallas_call(
        functools.partial(step_kernel, count),
        out_shape=[jax.ShapeDtypeStruct(weight.shape, F32) for weight, _ in pairs],
        in_specs=[VMEM] * (1 + 2 * count),
        out_specs=[VMEM] * count,
        compiler_params=pltpu.CompilerParams(vmem_limit_bytes=40 * MIB),
        name="take_step",
    )(sums, *[array for pair in pairs for array in pair])


def as_rows(flat):
    if flat.ndim == 2:
        return flat
    lanes = max(size for size in range(1, 129) if flat.shape[0] % size == 0)
    return flat.reshape(-1, lanes)


def local(
    tokens,
    kept_patches,
    clip_lengths,
    clip_device,
    cot_output,
    cot_aligned,
    entry_weight,
    entry_first,
    entry_second,
    exit_weight,
    exit_first,
    exit_second,
    align_weight,
    align_first,
    align_second,
    expand_weight,
    expand_first,
    expand_second,
    reduce_weight,
    reduce_first,
    reduce_second,
    position_table,
    position_first,
    position_second,
    norm_params,
    norm_first,
    norm_second,
):
    rows, width = tokens.shape
    align_width = cot_aligned.shape[1]
    axes = ("dp", "tensor")
    pair = lax.axis_size("tensor")
    devices = lax.axis_size("dp") * pair
    hidden = expand_weight.shape[0] * devices
    positions = position_table.shape[0] * devices // width
    routed = devices == 2 * ROUTED_DP and pair == 2
    device = lax.axis_index("dp") * pair + lax.axis_index("tensor")
    shapes = (
        (TABLE_SLAB, width),
        (width // devices, 3 * width),
        (width // devices, width),
        (hidden // devices, width),
        (hidden // devices, width),
        (width // devices, align_width),
    )
    wholes = (
        (positions, width),
        (width, 3 * width),
        (width, width),
        (hidden, width),
        (hidden, width),
        (width, align_width),
    )
    masters = (position_table, entry_weight, exit_weight, expand_weight, reduce_weight, align_weight)
    triples = {
        TABLE: (position_table, position_first, position_second),
        ENTRY: (entry_weight, entry_first, entry_second),
        EXIT: (exit_weight, exit_first, exit_second),
        EXPAND: (expand_weight, expand_first, expand_second),
        REDUCE: (reduce_weight, reduce_first, reduce_second),
        ALIGN: (align_weight, align_first, align_second),
    }
    norms = (norm_params, norm_first, norm_second)
    if routed:
        states = [as_rows(array) for piece in range(6) for array in triples[piece]]
        norm_states = [array.reshape(1, -1) for array in norms]
        kept = kept_patches.reshape(1, -1)
        found = gather_forward(
            states[::3],
            norm_states[0],
            tokens,
            kept,
            clip_lengths.reshape(1, -1),
            clip_device.reshape(1, -1),
            shapes,
            devices,
        )
        lows = [block.reshape(-1, block.shape[2]) for block in found[:5]]
        out_low, segment = found[14], found[16]
        arrays = (cot_output, cot_aligned) + tuple(lows) + tuple(found[6:16])
        results = scatter_backward(
            kept, segment, found[5], norm_states, arrays, states, shapes, devices
        )
        norm_slope, sums, align_rows, token_grad = results[6:]
        done = finish(
            segment,
            sums,
            norm_slope,
            norm_states,
            results[:6],
            states,
            (out_low, align_rows, token_grad),
        )
        outputs = list(done[21:24])
        for piece in MEMBERS:
            for number in range(3):
                outputs.append(done[3 * piece + number].reshape(triples[piece][number].shape))
        outputs = outputs + [array.reshape(-1) for array in done[18:21]] + [done[24]]
        return tuple(outputs)

    segment, valid_rows = row_layout(clip_lengths, clip_device, device, rows)
    segment_column = segment[:, None]
    valid_column = valid_rows[:, None]
    lows = [
        lax.all_gather(master.astype(BF).reshape(-1), axes, axis=0, tiled=True).reshape(whole)
        for master, whole in zip(masters, wholes)
    ]
    norm_low = lax.all_gather(norm_params.astype(BF), axes, axis=0, tiled=True).reshape(4, width)
    patch = kept_patches
    table_low, entry_low, exit_low, expand_low, reduce_low, align_low = lows
    norm_low = norm_low.astype(F32)
    residual = tokens.astype(F32) + jnp.take(table_low, patch, axis=0).astype(F32)
    normed_one = layer_norm(residual, norm_low[0], norm_low[1]).astype(BF)
    joint_low = contract(normed_one, entry_low, 1, 0).astype(BF)
    attended = attend(segment_column, joint_low)
    middle = residual + contract(attended, exit_low, 1, 0)
    normed_two = layer_norm(middle, norm_low[2], norm_low[3]).astype(BF)
    hidden_pre = contract(normed_two, expand_low, 1, 1)
    share = 0.5 + 0.5 * lax.erf(hidden_pre * 0.5**0.5)
    hidden_act = (hidden_pre * share).astype(BF)
    hidden_slope = share + hidden_pre * jnp.exp(-0.5 * hidden_pre * hidden_pre) * (0.5 / math.pi) ** 0.5
    out_low = (middle + contract(hidden_act, reduce_low, 1, 0)).astype(BF)
    align_rows = contract(out_low, align_low, 1, 0).astype(BF)
    cot_align_valid = jnp.where(valid_column, cot_aligned, jnp.zeros_like(cot_aligned))
    grad_align = contract(out_low, cot_align_valid, 0, 0)
    grad_out = jnp.where(valid_column, cot_output.astype(F32), 0.0) + contract(
        cot_align_valid, align_low, 1, 1
    )
    grad_feed = grad_out.astype(BF)
    grad_act = contract(grad_feed, reduce_low, 1, 1)
    grad_pre = (grad_act * hidden_slope).astype(BF)
    grad_reduce = contract(hidden_act, grad_feed, 0, 0)
    grad_expand = contract(grad_pre, normed_two, 0, 0)
    grad_two = contract(grad_pre, expand_low, 1, 0)
    through, gains = norm_back(middle, grad_two, norm_low[2])
    grad_middle = grad_out + through
    grad_branch = grad_middle.astype(BF)
    grad_exit = contract(attended, grad_branch, 0, 0)
    grad_attended = contract(grad_branch, exit_low, 1, 1).astype(BF)
    grad_parts = attend_back(segment_column, joint_low, grad_attended)
    grad_joint = jnp.concatenate([grad_parts[0], grad_parts[1], grad_parts[2]], axis=1)
    grad_entry = contract(normed_one, grad_joint, 0, 0)
    grad_one = contract(grad_joint, entry_low, 1, 1)
    through_one, gains_one = norm_back(residual, grad_one, norm_low[0])
    token_grad = grad_middle + through_one
    places = jnp.arange(positions, dtype=jnp.int32)
    picks = (patch[:, None] == places[None, :]).astype(BF)
    grad_table = contract(picks, token_grad.astype(BF), 0, 0)
    grad_norms = jnp.concatenate(
        [jnp.sum(part, axis=0) for part in (gains_one, grad_one, gains, grad_two)]
    )
    grads = (grad_table, grad_entry, grad_exit, grad_expand, grad_reduce, grad_align)
    summed = [
        lax.psum_scatter(grad.reshape(-1), axes, scatter_dimension=0, tiled=True)
        for grad in grads
    ]
    norm_sum = lax.psum_scatter(grad_norms, axes, scatter_dimension=0, tiled=True)
    block_out = jnp.where(valid_column, out_low, jnp.zeros_like(out_low))
    aligned = jnp.where(valid_column, align_rows, jnp.zeros_like(align_rows))

    def summed_like(master, index):
        return summed[index].reshape(master.shape)

    members = (
        (entry_weight, summed_like(entry_weight, ENTRY), entry_first, entry_second),
        (exit_weight, summed_like(exit_weight, EXIT), exit_first, exit_second),
        (align_weight, summed_like(align_weight, ALIGN), align_first, align_second),
        (expand_weight, summed_like(expand_weight, EXPAND), expand_first, expand_second),
        (reduce_weight, summed_like(reduce_weight, REDUCE), reduce_first, reduce_second),
        (position_table, summed_like(position_table, TABLE), position_first, position_second),
        (norm_params, norm_sum, norm_first, norm_second),
    )
    decays = (DECAY, DECAY, DECAY, DECAY, DECAY, DECAY, 0.0)
    members = [tuple(as_rows(array) for array in member) for member in members]
    found = moments(members, decays)
    sums = found[-1]
    sums = lax.psum(sums, axes)
    stepped = take_step(
        sums, [(members[member][0], found[3 * member + 2]) for member in range(len(members))]
    )
    weight_squares, update_squares = sums[0:7, 0], sums[8:15, 0]
    trust = jnp.sqrt(weight_squares) / jnp.sqrt(update_squares + TINY)
    outputs = [block_out, aligned, token_grad]
    originals = (
        entry_weight,
        exit_weight,
        align_weight,
        expand_weight,
        reduce_weight,
        position_table,
        norm_params,
    )
    for member, original in enumerate(originals):
        for array in (found[3 * member], found[3 * member + 1], stepped[member]):
            outputs.append(array.reshape(original.shape))
    outputs.append(jnp.stack((trust, jnp.sqrt(weight_squares), jnp.sqrt(update_squares))))
    return tuple(outputs)


def solution(mesh):
    both = ("dp", "tensor")
    rows, flat, whole = P(both, None), P(both), P()
    weight_specs = (flat,) * 9 + (rows,) * 6 + (flat,) * 6
    placed = (rows, flat, whole, whole, rows, rows) + weight_specs
    return jax.shard_map(
        local,
        mesh=mesh,
        in_specs=placed,
        out_specs=(rows, rows, rows) + weight_specs + (whole,),
        check_vma=False,
    )
```
